32 devices in a mesh: dp: 4 (over x, core), row: 4 (over z), col: 2 (over y).
Axes of the slice: x: 2, y: 2, z: 4, core: 2. Of those that a mesh axis runs over, the one named last changes fastest.
Arguments:
- hidden: bfloat16 [16384, 1024], P(('dp', 'col'), 'row')
- memory: bfloat16 [8192, 1024], P(('dp', 'col'), 'row')
- compressed: bfloat16 [8192, 1024], P(('dp', 'col'), 'row')
- seg_ids: int32 [16384], P(('dp', 'row')), may hold values from -1 to 32767, as said below
- positions: int32 [16384], P(('dp', 'row')), may hold values from 0 to 1022, as said below
- keep_mask: int32 [16384], P(('dp', 'row')), may hold values from 0 to 1
- mem_seg: int32 [16384], P(('dp', 'row')), may hold values from 0 to 32767, as said below
- cotangent: bfloat16 [16384, 1024], P(('dp', 'col'), 'row'), may hold values from -6 to 6
- w_qkv: float32 [1024, 3, 8, 128], P('row', None, 'col', 'dp'), may hold values from -0.1875 to 0.1875
- w_out: float32 [8, 128, 1024], P('col', 'dp', 'row'), may hold values from -1 to 1
- w_up: float32 [1024, 4096], P('row', ('dp', 'col')), may hold values from -0.1875 to 0.1875
- w_down: float32 [4096, 1024], P(('dp', 'col'), 'row'), may hold values from -0.09375 to 0.09375
- norm_attn: float32 [1024], P('row'), may hold values from 0.5 to 1.5
- norm_ffn: float32 [1024], P('row'), may hold values from 0.5 to 1.5
- conv_w: float32 [3, 1024], P(None, 'row'), may hold values from -3.5 to 3.5
Outputs:
- out: bfloat16 [16384, 1024], P(('dp', 'col'), 'row')
- d_hidden: bfloat16 [16384, 1024], P(('dp', 'col'), 'row')
- grad_w_qkv: float32 [1024, 3, 8, 128], P('row', None, 'col', 'dp')
- grad_w_out: float32 [8, 128, 1024], P('col', 'dp', 'row')
- grad_w_up: float32 [1024, 4096], P('row', ('dp', 'col'))
- grad_w_down: float32 [4096, 1024], P(('dp', 'col'), 'row')
- grad_norm_attn: float32 [1024], P('row')
- grad_norm_ffn: float32 [1024], P('row')
- grad_conv_w: float32 [3, 1024], P(None, 'row')
The draws below stay inside these ranges and needn't reach their ends.
Inputs may be any that keep to these rules, and one draw needn't show every extreme that they name: `seg_ids`: -1 marks padding, which stands at the end of a sequence; other equal ids mark one document, and a sequence's first document may continue in memory rows with the same id. `positions`: offset from the document's first token in the sequence; 0 for padding. `mem_seg`: for each sequence its 512 compressed rows, then its 512 memory rows, oldest first.
All inputs are finite; a program needn't handle non-finite values.
Results may differ from the reference program's by a relative error of at most 0.018.
Values may be sent and summed in bfloat16 or wider, within the bound.
No kernel may reach another device: no remote copies, remote signals or barrier semaphores. Data moves between devices by JAX's collectives and lax.ppermute only.
A program may use at most 256 MiB of HBM per device.

```python
import jax
import jax.numpy as jnp
from jax import lax

D = 1024
H = 8
DH = 128
FF = 4096
MEM = 512
CMEM = 512
RATE = 3
NEWC = 128
SEQ_LEN = 1024
SEQS = 16
TOKENS = 16384


def doc_layout(key):
    stream_len = CMEM + MEM + SEQ_LEN
    fresh = jax.random.randint(jax.random.fold_in(key, 11), (SEQS, stream_len), 0, max(SEQ_LEN // 3, 2))
    stream_index = jnp.arange(stream_len, dtype=jnp.int32)
    seq_index = jnp.arange(SEQS, dtype=jnp.int32)
    whole_doc = (seq_index[:, None] == 0) & (stream_index[None, :] >= CMEM + MEM)
    fresh = jnp.where(whole_doc, 1, fresh)
    starts = jnp.where((fresh == 0) | (stream_index[None, :] == 0), 1, 0).astype(jnp.int32)
    doc_ids = jnp.cumsum(starts, axis=1).astype(jnp.int32) - 1 + seq_index[:, None] * stream_len
    pad_count = jax.random.randint(jax.random.fold_in(key, 12), (SEQS, 1), 1, SEQ_LEN // 8 + 1)
    pad_count = jnp.where(seq_index[:, None] == 0, 1, pad_count).astype(jnp.int32)
    tok_index = jnp.arange(SEQ_LEN, dtype=jnp.int32)
    keep_tok = jnp.where(tok_index[None, :] < SEQ_LEN - pad_count, 1, 0).astype(jnp.int32)
    tok_starts = jnp.where((starts[:, CMEM + MEM:] == 1) | (tok_index[None, :] == 0), tok_index[None, :], 0)
    last_start = lax.cummax(tok_starts, axis=1)
    pos_tok = ((tok_index[None, :] - last_start) * keep_tok).astype(jnp.int32)
    seg_tok = jnp.where(keep_tok == 1, doc_ids[:, CMEM + MEM:], -1).astype(jnp.int32)
    return (seg_tok, pos_tok, keep_tok, doc_ids[:, :CMEM + MEM])


def draw_seg_ids(key, part):
    return doc_layout(key)[0].reshape(-1)


def draw_positions(key, part):
    return doc_layout(key)[1].reshape(-1)


def draw_keep_mask(key, part):
    return doc_layout(key)[2].reshape(-1)


def draw_mem_seg(key, part):
    return doc_layout(key)[3].reshape(-1)


def feature_rows(key, row_count, salt):
    noise = jnp.clip(jax.random.normal(jax.random.fold_in(key, salt), (row_count, D), jnp.float32), -6.0, 6.0)
    return noise.astype(jnp.bfloat16)


def draw_hidden(key, part):
    return feature_rows(key, TOKENS, 21)


def draw_memory(key, part):
    return feature_rows(key, SEQS * MEM, 31)


def draw_compressed(key, part):
    return feature_rows(key, SEQS * CMEM, 41)


def block_levels(key, shape, shards, least, largest):
    loudness = 1.0
    for dim, shards_of in shards:
        draws = jax.random.uniform(jax.random.fold_in(jax.random.fold_in(key, 6), dim), (shards_of,), jnp.float32, least / len(shards), largest / len(shards))
        loudness = loudness * jnp.repeat(jnp.exp(draws), shape[dim] // shards_of).reshape((-1,) + (1,) * (len(shape) - 1 - dim))
    return loudness


def normal_values(rng, dims, width, limit, split=(), kind=jnp.bfloat16):
    gain = block_levels(rng, dims, split, -0.22, 0.18) if split else 1.0
    values = jax.random.normal(rng, dims, jnp.float32) * width * gain
    return jnp.minimum(jnp.maximum(values, -limit), limit).astype(kind)


def setup_inputs(seed: int = 0) -> dict:
    key_of = jax.random.split(jax.random.key(seed), 16)
    return {
        "hidden": draw_hidden(jax.random.fold_in(key_of[15], 71), 0),
        "memory": draw_memory(jax.random.fold_in(key_of[15], 71), 0),
        "compressed": draw_compressed(jax.random.fold_in(key_of[15], 71), 0),
        "seg_ids": draw_seg_ids(jax.random.fold_in(key_of[15], 71), 0),
        "positions": draw_positions(jax.random.fold_in(key_of[15], 71), 0),
        "keep_mask": draw_keep_mask(jax.random.fold_in(key_of[15], 71), 0),
        "mem_seg": draw_mem_seg(jax.random.fold_in(key_of[15], 71), 0),
        "cotangent": normal_values(key_of[7], (TOKENS, D), 1.0, 6.0, ((0, 8), (1, 4))),
        "w_qkv": normal_values(key_of[8], (D, 3, H, DH), D ** -0.5, 0.1875, ((0, 4), (2, 2), (3, 4)), jnp.float32),
        "w_out": normal_values(key_of[9], (H, DH, D), (H * DH // 32) ** -0.5, 1.0, ((0, 2), (1, 4), (2, 4)), jnp.float32),
        "w_up": normal_values(key_of[10], (D, FF), D ** -0.5, 0.1875, ((0, 4), (1, 8)), jnp.float32),
        "w_down": normal_values(key_of[11], (FF, D), FF ** -0.5, 0.09375, ((0, 8), (1, 4)), jnp.float32),
        "norm_attn": jnp.clip(1.0 + 0.1 * jax.random.normal(key_of[12], (D,), jnp.float32), 0.5, 1.5),
        "norm_ffn": jnp.clip(1.0 + 0.1 * jax.random.normal(key_of[13], (D,), jnp.float32), 0.5, 1.5),
        "conv_w": normal_values(key_of[14], (RATE, D), RATE ** -0.5, 3.5, ((1, 4),), jnp.float32),
    }


EPSILON = 1e-05
MASKED = -1e+30
HIGHEST = lax.Precision.HIGHEST

@jax.custom_vjp
def low(v):
    return lax.optimization_barrier(v.astype(jnp.bfloat16)).astype(jnp.float32)

@jax.custom_vjp
def low_back(v):
    return v

def low_keep(v):
    return (low(v), None)

def low_pass(kept, grad):
    return (grad,)

def back_keep(v):
    return (v, None)

def back_low(kept, grad):
    return (low(grad),)
low.defvjp(low_keep, low_pass)
low_back.defvjp(back_keep, back_low)

def rounded_both(values):
    return low_back(low(values))

def matmul(left_side, right_side):
    return jnp.dot(left_side, right_side, precision=HIGHEST, preferred_element_type=jnp.float32)

def layer_norm(values, gain_row):
    center = values - lax.optimization_barrier(jnp.mean(values, axis=-1, keepdims=True))
    spread = lax.optimization_barrier(jnp.mean(center * center, axis=-1, keepdims=True))
    return center * lax.rsqrt(spread + EPSILON) * gain_row

def score_of(queries, key_rows):
    return low_back(jnp.einsum('qhd,khd->hqk', queries, key_rows, precision=HIGHEST) * DH ** (-0.5))

def softmax_attend(scores, value_rows):
    probs_low = low(jax.nn.softmax(scores, axis=-1))
    return jnp.einsum('hqk,khd->qhd', probs_low, value_rows, precision=HIGHEST)

def one_sequence(entries):
    queries, keys_tok, values_tok, keys_mem, values_mem, keys_new, values_new, seg_tok, pos_tok, keep_tok, seg_mem = entries
    tok_index = jnp.arange(SEQ_LEN, dtype=jnp.int32)
    mem_ok = seg_mem[None, :] == seg_tok[:, None]
    tok_ok = (seg_tok[None, :] == seg_tok[:, None]) & (pos_tok[None, :] <= pos_tok[:, None]) & (keep_tok[None, :] == 1) | (tok_index[None, :] == tok_index[:, None])
    allowed = jnp.concatenate([mem_ok, tok_ok], axis=1)
    all_keys = jnp.concatenate([keys_mem, keys_tok], axis=0)
    all_values = jnp.concatenate([values_mem, values_tok], axis=0)
    scores = jnp.where(allowed[None], score_of(queries, all_keys), MASKED)
    result = softmax_attend(scores, all_values)
    old_keys = keys_mem[CMEM:CMEM + RATE * NEWC]
    old_values = values_mem[CMEM:CMEM + RATE * NEWC]
    old_out = low_back(softmax_attend(score_of(queries, old_keys), old_values))
    new_out = low_back(softmax_attend(score_of(queries, keys_new), values_new))
    recon_gap = old_out - new_out
    return (result, 0.5 * jnp.sum(recon_gap * recon_gap))

def forward(params, hidden, memory, compressed, seg_tok, pos_tok, keep_tok, seg_mem):
    w_qkv, w_out, w_up, w_down, norm_attn, norm_ffn, conv_w = params
    seq_count = hidden.shape[0] // SEQ_LEN
    qkv_low = low(w_qkv)
    w_tok = qkv_low.reshape(D, 3 * H * DH)
    w_mem = qkv_low[:, 1:].reshape(D, 2 * H * DH)
    x_low = low(layer_norm(hidden, norm_attn))
    c_low = low(layer_norm(compressed, norm_attn))
    m_norm = layer_norm(memory, norm_attn)
    m_low = low(m_norm)
    oldest = m_norm.reshape(seq_count, MEM, D)[:, :RATE * NEWC].reshape(seq_count, NEWC, RATE, D)
    packed = low(lax.optimization_barrier(jnp.sum(oldest * conv_w[None, None], axis=2))).reshape(seq_count * NEWC, D)
    tok_proj = rounded_both(matmul(x_low, w_tok)).reshape(seq_count, SEQ_LEN, 3, H, DH)
    cm_proj = rounded_both(matmul(c_low, w_mem)).reshape(seq_count, CMEM, 2, H, DH)
    m_proj = rounded_both(matmul(m_low, w_mem)).reshape(seq_count, MEM, 2, H, DH)
    new_proj = rounded_both(matmul(packed, w_mem)).reshape(seq_count, NEWC, 2, H, DH)
    mem_proj = jnp.concatenate([cm_proj, m_proj], axis=1)
    entries = (tok_proj[:, :, 0], tok_proj[:, :, 1], tok_proj[:, :, 2], mem_proj[:, :, 0], mem_proj[:, :, 1], new_proj[:, :, 0], new_proj[:, :, 1], seg_tok.reshape(seq_count, SEQ_LEN), pos_tok.reshape(seq_count, SEQ_LEN), keep_tok.reshape(seq_count, SEQ_LEN), seg_mem.reshape(seq_count, CMEM + MEM))
    heads_out, recon_loss = lax.map(jax.checkpoint(one_sequence), entries)
    heads_low = rounded_both(heads_out).reshape(seq_count * SEQ_LEN, H * DH)
    mid_state = hidden + low_back(matmul(heads_low, low(w_out).reshape(H * DH, D)))
    x2_low = low(layer_norm(mid_state, norm_ffn))
    pre_act = low_back(matmul(x2_low, low(w_up)))
    act_low = low(jax.nn.gelu(pre_act, approximate=True))
    return (mid_state + low_back(matmul(act_low, low(w_down))), jnp.sum(recon_loss))

def reference(hidden, memory, compressed, seg_ids, positions, keep_mask, mem_seg, cotangent, w_qkv, w_out, w_up, w_down, norm_attn, norm_ffn, conv_w):
    group_seqs = 4
    steps_count = SEQS // group_seqs
    tok_span = group_seqs * SEQ_LEN
    params = (w_qkv, w_out, w_up, w_down, norm_attn, norm_ffn, conv_w)
    inputs = (hidden.astype(jnp.float32).reshape(steps_count, tok_span, D), memory.astype(jnp.float32).reshape(steps_count, group_seqs * MEM, D), compressed.astype(jnp.float32).reshape(steps_count, group_seqs * CMEM, D), seg_ids.reshape(steps_count, tok_span), positions.reshape(steps_count, tok_span), keep_mask.reshape(steps_count, tok_span), mem_seg.reshape(steps_count, group_seqs * (CMEM + MEM)), cotangent.astype(jnp.float32).reshape(steps_count, tok_span, D))

    def advance(totals, piece_in):
        x_part, m_part, c_part, seg_part, pos_part, keep_part, mseg_part, cot_part = piece_in

        def local_fn(weights, x_in):
            return forward(weights, x_in, m_part, c_part, seg_part, pos_part, keep_part, mseg_part)
        (result, recon_loss), pull_back = jax.vjp(local_fn, params, x_part)
        weight_grads, d_input = pull_back((cot_part, jnp.ones_like(recon_loss)))
        totals = jax.tree.map(lambda running, extra: running + extra, totals, weight_grads)
        return (totals, (result.astype(jnp.bfloat16), d_input.astype(jnp.bfloat16)))
    start_totals = jax.tree.map(jnp.zeros_like, params)
    totals, (results, d_inputs) = lax.scan(advance, start_totals, inputs)
    return (results.reshape(TOKENS, D), d_inputs.reshape(TOKENS, D), totals[0], totals[1], totals[2], totals[3], totals[4], totals[5], totals[6])
```

```python
import functools

import jax
import jax.numpy as jnp
from jax import lax
from jax.experimental import pallas as pl
from jax.experimental.pallas import tpu as pltpu
from jax.sharding import PartitionSpec as P

D = 1024
DH = 128
MEM = 512
CMEM = 512
RATE = 3
NEWC = 128
SEQ_LEN = 1024
HALF = SEQ_LEN // 2
HEADS = 4
OLD = RATE * NEWC
MROWS = CMEM + MEM
KM = MROWS + NEWC
QUARTER = D // 4
CHUNK = 256

EPSILON = 1e-05
MASKED = -1e30
LOG2E = 1.4426950408889634
SCALE = DH**-0.5
SCALE2 = SCALE * LOG2E
F32 = jnp.float32
BF = jnp.bfloat16


def nn(a, b):
    return lax.dot_general(a, b, (((1,), (0,)), ((), ())), preferred_element_type=F32)


def nt(a, b):
    return lax.dot_general(a, b, (((1,), (1,)), ((), ())), preferred_element_type=F32)


def tn(a, b):
    return lax.dot_general(a, b, (((0,), (0,)), ((), ())), preferred_element_type=F32)


def swap(x, axis, distance):
    n = lax.axis_size(axis)
    return lax.ppermute(x, axis, [(i, i ^ distance) for i in range(n)])


def add_low(a, b):
    return (a.astype(F32) + b.astype(F32)).astype(BF)


def params(limit_mb, dims=1):
    return pltpu.CompilerParams(
        dimension_semantics=("arbitrary",) * dims, vmem_limit_bytes=limit_mb << 20
    )


def shape(dims, kind):
    return jax.ShapeDtypeStruct(dims, kind)


def whole(dims):
    zeros = (0,) * len(dims)
    return pl.BlockSpec(dims, lambda *_: zeros)


def norm_block(pieces, gain_ref, row_id):
    columns, values, total = [], [], 0.0
    for k in range(4):
        start = pl.multiple_of((row_id ^ k) * QUARTER, QUARTER)
        columns.append(pl.ds(start, QUARTER))
        v = pieces[k].astype(F32)
        values.append(v)
        total = total + jnp.sum(v, axis=1, keepdims=True)
    mean = total / D
    square = 0.0
    for k in range(4):
        values[k] = values[k] - mean
        square = square + jnp.sum(values[k] * values[k], axis=1, keepdims=True)
    factor = lax.rsqrt(square / D + EPSILON)
    return columns, [values[k] * factor * gain_ref[:, columns[k]] for k in range(4)]


def tok_norm_kernel(where, p0, p1, p2, p3, gain_ref, low_ref, raw_ref):
    pieces = [p[...] for p in (p0, p1, p2, p3)]
    columns, normed = norm_block(pieces, gain_ref, where[0])
    for k in range(4):
        low_ref[:, columns[k]] = normed[k].astype(BF)
        raw_ref[:, columns[k]] = pieces[k]


def tok_norm(where, pieces, gain):
    block = 256
    count = SEQ_LEN // block
    piece = pl.BlockSpec((block, QUARTER), lambda i, w: ((i + w[1] * (count // 2)) % count, 0))
    out = pl.BlockSpec((block, D), lambda i, w: (i, 0))
    return pl.pallas_call(
        tok_norm_kernel,
        out_shape=(shape((SEQ_LEN, D), BF), shape((SEQ_LEN, D), BF)),
        grid_spec=pltpu.PrefetchScalarGridSpec(
            num_scalar_prefetch=1,
            grid=(count,),
            in_specs=[piece] * 4 + [whole((1, D))],
            out_specs=[out, out],
        ),
        compiler_params=params(24),
        name="tok_norm",
    )(where, *pieces, gain)


def mem_norm_kernel(where, p0, p1, p2, p3, gain_ref, conv_ref, low_ref, raw_ref, keep_ref):
    for block in range(MROWS // 256):
        rows = slice(block * 256, block * 256 + 256)
        pieces = [p[rows, :] for p in (p0, p1, p2, p3)]
        columns, normed = norm_block(pieces, gain_ref, where[0])
        for k in range(4):
            low_ref[rows, columns[k]] = normed[k].astype(BF)
            raw_ref[rows, columns[k]] = pieces[k]
            if block * 256 >= CMEM:
                start = block * 256 - CMEM
                for j in range(2):
                    lanes = (where[0] ^ k) * 2 + j
                    keep_ref[lanes, start : start + 256, :] = normed[k][:, j * DH : j * DH + DH]
    for j in range(D // DH):
        lanes = slice(j * DH, j * DH + DH)
        packed = 0.0
        for t in range(RATE):
            picked = keep_ref[j, pl.ds(t, NEWC, stride=RATE), :]
            packed = packed + conv_ref[t : t + 1, lanes] * picked
        low_ref[MROWS:, lanes] = packed.astype(BF)


def mem_norm(where, pieces, gain, conv):
    return pl.pallas_call(
        mem_norm_kernel,
        out_shape=(shape((KM, D), BF), shape((MROWS, D), BF)),
        grid_spec=pltpu.PrefetchScalarGridSpec(
            num_scalar_prefetch=1,
            grid=(1,),
            in_specs=[whole((MROWS, QUARTER))] * 4 + [whole((1, D)), whole((RATE, D))],
            out_specs=[whole((KM, D)), whole((MROWS, D))],
            scratch_shapes=[pltpu.VMEM((D // DH, MEM, DH), F32)],
        ),
        compiler_params=params(32),
        name="mem_norm",
    )(where, *pieces, gain, conv)


def fill_bias(bias_ref, row_ref, col_ref):
    seg_q, pos_q = row_ref[0:1, :], row_ref[1:2, :]

    def memory_chunk(c, carry):
        rows = pl.ds(pl.multiple_of(c * CHUNK, CHUNK), CHUNK)
        bias_ref[rows, :] = jnp.where(col_ref[rows, 2:3] == seg_q, 0.0, MASKED)
        return carry

    def token_chunk(c, carry):
        start = pl.multiple_of(c * CHUNK, CHUNK)
        rows = pl.ds(start, CHUNK)
        same = (col_ref[rows, 0:1] == seg_q) & (col_ref[rows, 1:2] <= pos_q)
        key_id = lax.broadcasted_iota(jnp.int32, (CHUNK, SEQ_LEN), 0) + start
        query_id = lax.broadcasted_iota(jnp.int32, (CHUNK, SEQ_LEN), 1)
        target = pl.ds(pl.multiple_of(MROWS + c * CHUNK, CHUNK), CHUNK)
        bias_ref[target, :] = jnp.where(same | (key_id == query_id), 0.0, MASKED)
        return carry

    lax.fori_loop(0, MROWS // CHUNK, memory_chunk, 0)
    lax.fori_loop(0, SEQ_LEN // CHUNK, token_chunk, 0)


def forward_kernel(tok_ref, mem_ref, row_ref, col_ref, o_ref, log_ref, bias_ref, s_ref, acc_ref):
    @pl.when(pl.program_id(0) == 0)
    def _():
        fill_bias(bias_ref, row_ref, col_ref)

    queries = tok_ref[:, :DH]

    def scores(key_ref, columns, offset):
        def step(c, top):
            rows = pl.ds(pl.multiple_of(c * CHUNK, CHUNK), CHUNK)
            target = pl.ds(pl.multiple_of(offset + c * CHUNK, CHUNK), CHUNK)
            s = nt(key_ref[rows, columns], queries) * SCALE2 + bias_ref[target, :]
            s_ref[target, :] = s
            return jnp.maximum(top, jnp.max(s.reshape(CHUNK // 8, 8, SEQ_LEN), axis=0))

        return step

    top = jnp.full((8, SEQ_LEN), -3.0e38, F32)
    top = lax.fori_loop(0, MROWS // CHUNK, scores(mem_ref, slice(0, DH), 0), top)
    top = lax.fori_loop(0, SEQ_LEN // CHUNK, scores(tok_ref, slice(DH, 2 * DH), MROWS), top)
    top = jnp.max(top, axis=0, keepdims=True)
    acc_ref[...] = jnp.zeros_like(acc_ref)

    def values(value_ref, columns, offset):
        def step(c, total):
            rows = pl.ds(pl.multiple_of(c * CHUNK, CHUNK), CHUNK)
            target = pl.ds(pl.multiple_of(offset + c * CHUNK, CHUNK), CHUNK)
            p = jnp.exp2(s_ref[target, :] - top)
            acc_ref[...] += nn(value_ref[rows, columns].T, p.astype(BF))
            return total + jnp.sum(p.reshape(CHUNK // 8, 8, SEQ_LEN), axis=0)

        return step

    total = jnp.zeros((8, SEQ_LEN), F32)
    total = lax.fori_loop(0, MROWS // CHUNK, values(mem_ref, slice(DH, 2 * DH), 0), total)
    total = lax.fori_loop(
        0, SEQ_LEN // CHUNK, values(tok_ref, slice(2 * DH, 3 * DH), MROWS), total
    )
    total = jnp.sum(total, axis=0, keepdims=True)
    o_ref[...] = (acc_ref[...] / total).T.astype(BF)
    log_ref[...] = (top + jnp.log2(total)).reshape(1, 1, SEQ_LEN)


def attention_forward(tok_p, mem_p, row_attr, col_attr):
    return pl.pallas_call(
        forward_kernel,
        out_shape=(shape((SEQ_LEN, HEADS * DH), BF), shape((HEADS, 1, SEQ_LEN), F32)),
        grid=(HEADS,),
        in_specs=[
            pl.BlockSpec((SEQ_LEN, 3 * DH), lambda h: (0, h)),
            pl.BlockSpec((KM, 2 * DH), lambda h: (0, h)),
            whole(row_attr.shape),
            whole(col_attr.shape),
        ],
        out_specs=[
            pl.BlockSpec((SEQ_LEN, DH), lambda h: (0, h)),
            pl.BlockSpec((1, 1, SEQ_LEN), lambda h: (h, 0, 0)),
        ],
        scratch_shapes=[
            pltpu.VMEM((MROWS + SEQ_LEN, SEQ_LEN), F32),
            pltpu.VMEM((MROWS + SEQ_LEN, SEQ_LEN), F32),
            pltpu.VMEM((DH, SEQ_LEN), F32),
        ],
        compiler_params=params(40),
        name="attention_forward",
    )(tok_p, mem_p, row_attr, col_attr)


def recon_kernel(tok_ref, mem_ref, gq_ref, gm_ref):
    q = tok_ref[:, :DH]
    old, new = slice(CMEM, CMEM + OLD), slice(MROWS, KM)
    keys, values = slice(0, DH), slice(DH, 2 * DH)

    def softmax_rows(key_rows):
        s = nt(key_rows, q) * SCALE2
        p = jnp.exp2(s - jnp.max(s, axis=0, keepdims=True))
        return p / jnp.sum(p, axis=0, keepdims=True)

    ko, vo, kn, vn = mem_ref[old, keys], mem_ref[old, values], mem_ref[new, keys], mem_ref[new, values]
    po, pn = softmax_rows(ko), softmax_rows(kn)
    po_low, pn_low = po.astype(BF), pn.astype(BF)
    out_o, out_n = nn(vo.T, po_low), nn(vn.T, pn_low)
    gap = (out_o - out_n).astype(BF)
    gap32 = gap.astype(F32)
    do = (po * (nn(vo, gap) - jnp.sum(gap32 * out_o, axis=0, keepdims=True))).astype(BF)
    dn = (pn * (jnp.sum(gap32 * out_n, axis=0, keepdims=True) - nn(vn, gap))).astype(BF)
    gq_ref[...] = ((nn(ko.T, do) + nn(kn.T, dn)) * SCALE).reshape(1, DH, SEQ_LEN)
    gap_t = gap32.T.astype(BF)
    gm_ref[:OLD, keys] = nn(do, q) * SCALE
    gm_ref[:OLD, values] = nn(po_low, gap_t)
    gm_ref[OLD:MEM, :] = jnp.zeros((MEM - OLD, 2 * DH), F32)
    gm_ref[MEM:, keys] = nn(dn, q) * SCALE
    gm_ref[MEM:, values] = -nn(pn_low, gap_t)


def reconstruction(tok_p, mem_p):
    return pl.pallas_call(
        recon_kernel,
        out_shape=(
            shape((HEADS, DH, SEQ_LEN), F32),
            shape((MEM + NEWC, HEADS * 2 * DH), F32),
        ),
        grid=(HEADS,),
        in_specs=[
            pl.BlockSpec((SEQ_LEN, 3 * DH), lambda h: (0, h)),
            pl.BlockSpec((KM, 2 * DH), lambda h: (0, h)),
        ],
        out_specs=[
            pl.BlockSpec((1, DH, SEQ_LEN), lambda h: (h, 0, 0)),
            pl.BlockSpec((MEM + NEWC, 2 * DH), lambda h: (0, h)),
        ],
        compiler_params=params(40),
        name="reconstruction",
    )(tok_p, mem_p)


def backward_kernel(
    tok_ref, mem_ref, own_ref, got_ref, o_ref, log_ref, rq_ref, rm_ref, row_ref, col_ref,
    gt_ref, gm_ref, bias_ref, acc_ref,
):
    @pl.when(pl.program_id(0) == 0)
    def _():
        fill_bias(bias_ref, row_ref, col_ref)

    q = tok_ref[:, :DH]
    go = jnp.concatenate([own_ref[...], got_ref[...]], axis=0)
    product = go.astype(F32) * o_ref[...].astype(F32)
    delta = jnp.sum(product.T, axis=0, keepdims=True)
    log_total = log_ref[...].reshape(1, SEQ_LEN)
    acc_ref[...] = rq_ref[...].reshape(DH, SEQ_LEN)

    def piece(k, v, offset):
        s = nt(k, q) * SCALE2 + bias_ref[offset, :]
        p = jnp.exp2(s - log_total)
        d = (p * (nt(v, go) - delta)).astype(BF)
        acc_ref[...] += nn(k.T, d) * SCALE
        return nn(d, q) * SCALE, nn(p.astype(BF), go)

    def memory_chunk(c, carry):
        rows = pl.ds(pl.multiple_of(c * CHUNK, CHUNK), CHUNK)
        gk, gv = piece(mem_ref[rows, :DH], mem_ref[rows, DH:], rows)
        gm_ref[rows, :DH] = gk.astype(BF)
        gm_ref[rows, DH:] = gv.astype(BF)
        return carry

    def shared_chunk(c, carry):
        rows = pl.ds(pl.multiple_of(c * CHUNK, CHUNK), CHUNK)
        extra = pl.ds(pl.multiple_of(c * CHUNK - CMEM, CHUNK), CHUNK)
        gk, gv = piece(mem_ref[rows, :DH], mem_ref[rows, DH:], rows)
        gm_ref[rows, :DH] = (gk + rm_ref[extra, :DH]).astype(BF)
        gm_ref[rows, DH:] = (gv + rm_ref[extra, DH:]).astype(BF)
        return carry

    def token_chunk(c, carry):
        rows = pl.ds(pl.multiple_of(c * CHUNK, CHUNK), CHUNK)
        target = pl.ds(pl.multiple_of(MROWS + c * CHUNK, CHUNK), CHUNK)
        gk, gv = piece(tok_ref[rows, DH : 2 * DH], tok_ref[rows, 2 * DH :], target)
        gt_ref[rows, DH : 2 * DH] = gk.astype(BF)
        gt_ref[rows, 2 * DH :] = gv.astype(BF)
        return carry

    lax.fori_loop(0, CMEM // CHUNK, memory_chunk, 0)
    lax.fori_loop(CMEM // CHUNK, MROWS // CHUNK, shared_chunk, 0)
    lax.fori_loop(0, SEQ_LEN // CHUNK, token_chunk, 0)
    gm_ref[MROWS:, :] = rm_ref[MEM:, :].astype(BF)
    gt_ref[:, :DH] = acc_ref[...].T.astype(BF)


def attention_backward(tok_p, mem_p, go_own, go_got, o, logs, rec_q, rec_m, row_attr, col_attr):
    half = pl.BlockSpec((HALF, DH), lambda h: (0, h))
    return pl.pallas_call(
        backward_kernel,
        out_shape=(
            shape((SEQ_LEN, HEADS * 3 * DH), BF),
            shape((KM, HEADS * 2 * DH), BF),
        ),
        grid=(HEADS,),
        in_specs=[
            pl.BlockSpec((SEQ_LEN, 3 * DH), lambda h: (0, h)),
            pl.BlockSpec((KM, 2 * DH), lambda h: (0, h)),
            half,
            half,
            pl.BlockSpec((SEQ_LEN, DH), lambda h: (0, h)),
            pl.BlockSpec((1, 1, SEQ_LEN), lambda h: (h, 0, 0)),
            pl.BlockSpec((1, DH, SEQ_LEN), lambda h: (h, 0, 0)),
            pl.BlockSpec((MEM + NEWC, 2 * DH), lambda h: (0, h)),
            whole(row_attr.shape),
            whole(col_attr.shape),
        ],
        out_specs=[
            pl.BlockSpec((SEQ_LEN, 3 * DH), lambda h: (0, h)),
            pl.BlockSpec((KM, 2 * DH), lambda h: (0, h)),
        ],
        scratch_shapes=[
            pltpu.VMEM((MROWS + SEQ_LEN, SEQ_LEN), F32),
            pltpu.VMEM((DH, SEQ_LEN), F32),
        ],
        compiler_params=params(40),
        name="attention_backward",
    )(tok_p, mem_p, go_own, go_got, o, logs, rec_q, rec_m, row_attr, col_attr)


def center_rows(rows):
    centered = rows - jnp.mean(rows, axis=1, keepdims=True)
    factor = lax.rsqrt(jnp.mean(centered * centered, axis=1, keepdims=True) + EPSILON)
    return centered * factor, factor


def mid_kernel(raw_ref, own_ref, got_ref, w_ref, gain_ref, mid_ref, x2_ref, x2t_ref):
    width = own_ref.shape[1]
    mid = raw_ref[...].astype(F32) + (
        nn(own_ref[...], w_ref[:width, :]) + nn(got_ref[...], w_ref[width:, :])
    )
    unit, _ = center_rows(mid)
    normed = unit * gain_ref[...]
    mid_ref[...] = mid
    x2_ref[...] = normed.astype(BF)
    x2t_ref[...] = normed.T.astype(BF)


def residual_mid(raw, o, o_got, w_out, gain):
    block = 256
    rows = lambda width: pl.BlockSpec((block, width), lambda i: (i, 0))
    return pl.pallas_call(
        mid_kernel,
        out_shape=(shape((HALF, D), F32), shape((HALF, D), BF), shape((D, HALF), BF)),
        grid=(HALF // block,),
        in_specs=[rows(D), rows(HEADS * DH), rows(HEADS * DH), whole((D, D)), whole((1, D))],
        out_specs=[rows(D), rows(D), pl.BlockSpec((D, block), lambda i: (0, i))],
        compiler_params=params(32),
        name="residual_mid",
    )(raw, o, o_got, w_out, gain)


def ffn_kernel(first, order, x2_ref, x2t_ref, cot_ref, cott_ref, w_ref, *rest):
    if first:
        up_ref, down_ref, out_ref, gx_ref = rest
    else:
        out0_ref, gx0_ref, up_ref, down_ref, out_ref, gx_ref = rest

    @pl.when(pl.program_id(0) == 0)
    def _():
        if first:
            out_ref[...] = jnp.zeros_like(out_ref)
            gx_ref[...] = jnp.zeros_like(gx_ref)
        else:
            out_ref[...] = out0_ref[...]
            gx_ref[...] = gx0_ref[...]

    width = w_ref.shape[-1]
    w_up = w_ref[0, :, 0].reshape(D, width)
    w_down = w_ref[0, :, 1].reshape(D, width)
    v = nn(x2_ref[...], w_up)
    g_act = nn(cot_ref[...], w_down)
    c0, c1 = 0.7978845608028654, 0.044715
    v2 = v * v
    t = jnp.tanh(c0 * v * (1.0 + c1 * v2))
    half = 0.5 * (1.0 + t)
    act = (v * half).astype(BF)
    slope = half + (0.5 * c0) * v * (1.0 - t * t) * (1.0 + (3.0 * c1) * v2)
    g_pre = (g_act * slope).astype(BF)
    out_ref[...] += nt(act, w_down)
    gx_ref[...] += nt(g_pre, w_up)
    up_ref[0] = nn(x2t_ref[...], g_pre).astype(BF).reshape(4, QUARTER, width)
    down_ref[0] = nn(cott_ref[...], act).astype(BF).reshape(4, QUARTER, width)


def feed_forward(order, x2, x2t, cot, cott, weights, sums=None):
    count = order.shape[0]
    width = weights.shape[-1]
    grads = shape((count, 4, QUARTER, width), BF)
    grad_spec = pl.BlockSpec((1, 4, QUARTER, width), lambda i, f: (i, 0, 0, 0))
    rows, cols = whole((HALF, D)), whole((D, HALF))
    extra = () if sums is None else sums
    return pl.pallas_call(
        functools.partial(ffn_kernel, sums is None),
        out_shape=(grads, grads, shape((HALF, D), F32), shape((HALF, D), F32)),
        grid_spec=pltpu.PrefetchScalarGridSpec(
            num_scalar_prefetch=1,
            grid=(count,),
            in_specs=[rows, cols, rows, cols]
            + [pl.BlockSpec((1, 4, 2, QUARTER, width), lambda i, f: (f[i], 0, 0, 0, 0))]
            + [rows] * len(extra),
            out_specs=[grad_spec, grad_spec, rows, rows],
        ),
        compiler_params=params(56),
        name="feed_forward",
    )(order, x2, x2t, cot, cott, weights, *extra)


def mid_back_kernel(gx_ref, mid_ref, cot_ref, gain_ref, w_ref, gm_ref, ga_ref, keep_ref, send_ref, gn_ref):
    @pl.when(pl.program_id(0) == 0)
    def _():
        gn_ref[...] = jnp.zeros_like(gn_ref)

    unit, factor = center_rows(mid_ref[...])
    gx = gx_ref[...]
    gn_ref[...] += jnp.sum(gx * unit, axis=0, keepdims=True)
    s = gx * gain_ref[...]
    g_mid = cot_ref[...].astype(F32) + factor * (
        s - jnp.mean(s, axis=1, keepdims=True) - unit * jnp.mean(s * unit, axis=1, keepdims=True)
    )
    gm_ref[...] = g_mid
    low = g_mid.astype(BF)
    ga_ref[...] = low
    width = keep_ref.shape[1]
    send_ref[...] = nt(low, w_ref[width:, :]).astype(BF)
    keep_ref[...] = nt(low, w_ref[:width, :]).astype(BF)


def mid_back(gx, mid, cot, gain, w_out):
    block = 256
    rows = lambda width: pl.BlockSpec((block, width), lambda i: (i, 0))
    half = shape((HALF, HEADS * DH), BF)
    return pl.pallas_call(
        mid_back_kernel,
        out_shape=(shape((HALF, D), F32), shape((HALF, D), BF), half, half, shape((1, D), F32)),
        grid=(HALF // block,),
        in_specs=[rows(D), rows(D), rows(D), whole((1, D)), whole((D, D))],
        out_specs=[rows(D), rows(D), rows(HEADS * DH), rows(HEADS * DH), whole((1, D))],
        compiler_params=params(32),
        name="mid_back",
    )(gx, mid, cot, gain, w_out)


def input_grad_kernel(keep_ref, got_ref, raw_ref, gm_ref, gain_ref, out_ref, gn_ref):
    @pl.when(pl.program_id(0) == 0)
    def _():
        gn_ref[...] = jnp.zeros_like(gn_ref)

    unit, factor = center_rows(raw_ref[...].astype(F32))
    gx = keep_ref[...] + got_ref[...].astype(F32)
    gn_ref[...] += jnp.sum(gx * unit, axis=0, keepdims=True)
    s = gx * gain_ref[...]
    g = gm_ref[...] + factor * (
        s - jnp.mean(s, axis=1, keepdims=True) - unit * jnp.mean(s * unit, axis=1, keepdims=True)
    )
    for k in range(4):
        out_ref[k] = g[:, k * QUARTER : (k + 1) * QUARTER].astype(BF)


def input_grad(keep, got, raw, g_mid, gain):
    block = 256
    rows = pl.BlockSpec((block, D), lambda i: (i, 0))
    return pl.pallas_call(
        input_grad_kernel,
        out_shape=(shape((4, HALF, QUARTER), BF), shape((1, D), F32)),
        grid=(HALF // block,),
        in_specs=[rows, rows, rows, rows, whole((1, D))],
        out_specs=[pl.BlockSpec((4, block, QUARTER), lambda i: (0, i, 0)), whole((1, D))],
        compiler_params=params(32),
        name="input_grad",
    )(keep, got, raw, g_mid, gain)


def mem_grad_kernel(g_ref, w_ref, raw_ref, gain_ref, conv_ref, gn_ref, gc_ref, unit_ref):
    total = jnp.zeros((1, D), F32)
    for block in range(MROWS // 256):
        rows = slice(block * 256, block * 256 + 256)
        unit, _ = center_rows(raw_ref[rows, :].astype(F32))
        total = total + jnp.sum(nn(g_ref[rows, :], w_ref[...]) * unit, axis=0, keepdims=True)
        if block * 256 >= CMEM:
            start = block * 256 - CMEM
            for j in range(D // DH):
                unit_ref[j, start : start + 256, :] = unit[:, j * DH : j * DH + DH]
    gn_ref[...] = total
    packed = nn(g_ref[MROWS:, :], w_ref[...])
    for j in range(D // DH):
        lanes = slice(j * DH, j * DH + DH)
        for t in range(RATE):
            picked = unit_ref[j, pl.ds(t, NEWC, stride=RATE), :]
            term = jnp.sum(packed[:, lanes] * picked, axis=0, keepdims=True)
            gc_ref[t : t + 1, lanes] = term * gain_ref[:, lanes]
            gn_ref[:, lanes] += conv_ref[t : t + 1, lanes] * term


def mem_grad(g_mem, w_mem, raw, gain, conv):
    return pl.pallas_call(
        mem_grad_kernel,
        out_shape=(shape((1, D), F32), shape((RATE, D), F32)),
        grid=(1,),
        in_specs=[
            whole((KM, D)), whole((D, D)), whole((MROWS, D)), whole((1, D)), whole((RATE, D)),
        ],
        out_specs=[whole((1, D)), whole((RATE, D))],
        scratch_shapes=[pltpu.VMEM((D // DH, MEM, DH), F32)],
        compiler_params=params(40),
        name="mem_grad",
    )(g_mem, w_mem, raw, gain, conv)


def halve_x(g):
    return add_low(g[0], swap(g[1], "dp", 2))


def halve_col(g):
    while g.shape[0] > 1:
        n = g.shape[0] // 2
        g = add_low(g[:n], swap(g[n:], "col", n))
    return g[0]


def pick(g, index, axis=0):
    return lax.dynamic_index_in_dim(g, index, axis, keepdims=False)


def halve_row(g, z_high, z_low):
    g = g.reshape((2, 2) + g.shape[1:])
    g = add_low(pick(g, z_high), swap(pick(g, 1 - z_high), "row", 2))
    got = swap(pick(g, 1 - z_low), "row", 1)
    return pick(g, z_low).astype(F32) + got.astype(F32)


def split_axis_of(g, axis, index):
    return pick(g, index, axis), pick(g, 1 - index, axis)


def sum_all(v):
    for axis, distances in (("dp", (1, 2)), ("row", (1, 2)), ("col", None)):
        if distances is None:
            distances, n = [], 1
            while n < lax.axis_size(axis):
                distances.append(n)
                n *= 2
        for distance in distances:
            v = v + swap(v, axis, distance)
    return v


def per_device(
    hidden, memory, compressed, seg_ids, positions, keep_mask, mem_seg, cotangent,
    w_qkv, w_out, w_up, w_down, norm_attn, norm_ffn, conv_w,
):
    n_col = lax.axis_size("col")
    heads_part = w_qkv.shape[2]
    dp, row, col = lax.axis_index("dp"), lax.axis_index("row"), lax.axis_index("col")
    z_high, z_low = row // 2, row % 2
    everything = ("dp", "col", "row")
    where = jnp.stack([row, z_low]).astype(jnp.int32)

    def gather_rows(rows):
        mine, other = pick(rows, z_high), pick(rows, 1 - z_high)
        far = swap(other, "row", 2)
        near = swap(mine, "row", 1)
        return [mine, near, far, swap(far, "row", 1)]

    tok_pieces = gather_rows(hidden.reshape(2, SEQ_LEN, QUARTER))
    mem_rows = jnp.concatenate(
        [compressed.reshape(2, CMEM, QUARTER), memory.reshape(2, MEM, QUARTER)], axis=1
    )
    mem_pieces = gather_rows(mem_rows)

    small = jnp.concatenate(
        [norm_attn, norm_ffn, conv_w.reshape(-1)]
        + [a.astype(F32) for a in (seg_ids, positions, keep_mask, mem_seg)]
    )
    shared = jnp.stack([small] + [swap(small, "row", k) for k in (1, 2, 3)])
    gains = jnp.stack([pick(shared, row ^ k) for k in range(4)])[:, : 5 * QUARTER]
    gains = gains.reshape(4, 5, QUARTER).transpose(1, 0, 2).reshape(5, D)
    gain1, gain2, conv = gains[0:1], gains[1:2], gains[2:5]
    spans = seg_ids.shape[0] // SEQ_LEN
    sequence = 2 * col + z_high
    ids = pick(shared, row ^ (sequence // spans))[5 * QUARTER :]
    ids = pick(ids.reshape(4, spans, SEQ_LEN), sequence % spans, 1)
    rolled = jnp.concatenate([ids[:3, HALF:], ids[:3, :HALF]], axis=1)
    seg, pos, keep = jnp.where(z_low == 0, ids[:3], rolled)
    row_attr = jnp.stack([seg, pos])
    col_attr = jnp.stack([jnp.where(keep == 1, seg, -2.0), pos, ids[3]], axis=1)

    qkv_t = w_qkv.astype(BF).transpose(1, 2, 3, 0)
    qkv_all = lax.all_gather(qkv_t, everything, axis=0, tiled=False)
    qkv_all = qkv_all.reshape(4, n_col, 4, 3, heads_part, DH // 4, QUARTER)
    out_all = lax.all_gather(w_out.astype(BF), everything, axis=0, tiled=False)
    out_all = out_all.reshape(4, n_col, 4, heads_part, DH // 4, QUARTER)
    if heads_part % 2 == 0:
        part = heads_part // 2
        w_tok = lax.dynamic_slice_in_dim(qkv_all, z_low * part, part, 4)
        outs = [lax.dynamic_slice_in_dim(out_all, z * part, part, 3) for z in (z_low, 1 - z_low)]
    else:
        part = n_col // 2
        w_tok = lax.dynamic_slice_in_dim(qkv_all, z_low * part, part, 1)
        outs = [lax.dynamic_slice_in_dim(out_all, z * part, part, 1) for z in (z_low, 1 - z_low)]
    w_tok = w_tok.transpose(1, 4, 3, 0, 5, 2, 6).reshape(HEADS * 3 * DH, D)
    w_mem = w_tok.reshape(HEADS, 3, DH, D)[:, 1:].reshape(HEADS * 2 * DH, D)
    w_back = jnp.concatenate(
        [w.transpose(1, 3, 0, 4, 2, 5).reshape(HEADS * DH, D) for w in outs], axis=0
    )
    ffn_part = jnp.stack([w_up.astype(BF), w_down.astype(BF).T])
    ffn_all = lax.all_gather(ffn_part, everything, axis=0, tiled=False)
    ffn_all = ffn_all.reshape(4 * n_col, 4, 2, QUARTER, w_up.shape[1])

    x_tok, raw_tok = tok_norm(where, tok_pieces, gain1)
    x_mem, raw_mem = mem_norm(where, mem_pieces, gain1, conv)
    tok_p = nt(x_tok, w_tok).astype(BF)
    mem_p = nt(x_mem, w_mem).astype(BF)
    o, logs = attention_forward(tok_p, mem_p, row_attr, col_attr)
    o_got = swap(o[HALF:], "row", 1)
    rec_q, rec_m = reconstruction(tok_p, mem_p)

    cotangent, _ = lax.optimization_barrier((cotangent, mem_pieces[3]))
    cot = lax.all_to_all(cotangent, "row", split_axis=0, concat_axis=0, tiled=True)
    cot = cot.reshape(4, HALF, QUARTER).transpose(1, 0, 2).reshape(HALF, D)
    cott = cot.T

    mid, x2, x2t = residual_mid(raw_tok, o, o_got, w_back, gain2)

    steps = jnp.arange(2 * n_col, dtype=jnp.int32)
    x_rel, col_rel = steps // n_col, steps % n_col
    order = lambda core: (dp ^ (2 * x_rel + core)) * n_col + (col ^ col_rel)
    up_send, down_send, out_sum, gx_sum = feed_forward(order(1), x2, x2t, cot, cott, ffn_all)
    up_got, down_got = swap(up_send, "dp", 1), swap(down_send, "dp", 1)
    up_keep, down_keep, out_sum, gx_sum = feed_forward(
        order(0), x2, x2t, cot, cott, ffn_all, (out_sum, gx_sum)
    )
    g_mid, g_attn, go_keep, go_send, gain2_sum = mid_back(gx_sum, mid, cot, gain2, w_back)
    go_got = swap(go_send, "row", 1)
    blocks = (2, n_col) + up_keep.shape[1:]
    grad_up = halve_x(add_low(up_keep, up_got).reshape(blocks))
    grad_up = halve_row(halve_col(grad_up), z_high, z_low)
    grad_down = add_low(down_keep, down_got).reshape(blocks).swapaxes(0, 1)
    grad_down = halve_x(halve_col(grad_down[:, None])[0])
    grad_down = halve_row(grad_down, z_high, z_low).T

    g_tok, g_mem = attention_backward(
        tok_p, mem_p, go_keep, go_got, o, logs, rec_q, rec_m, row_attr, col_attr
    )
    gx = nn(g_tok, w_tok)
    gx_got = swap(gx[HALF:].astype(BF), "row", 1)

    out = (mid + out_sum).astype(BF).reshape(HALF, 4, QUARTER).transpose(1, 0, 2)
    out = lax.all_to_all(
        out.reshape(4 * HALF, QUARTER), "row", split_axis=0, concat_axis=0, tiled=True
    )

    g_tok_w = tn(g_tok, x_tok).reshape(HEADS, 3, DH, D)
    g_mem_w = tn(g_mem, x_mem).reshape(HEADS, 2, DH, D)
    g_qkv = jnp.concatenate([g_tok_w[:, :1], g_tok_w[:, 1:] + g_mem_w], axis=1).astype(BF)
    g_out = jnp.concatenate([tn(o[:HALF], g_attn), tn(o_got, g_attn)], axis=0).astype(BF)
    grad_qkv, grad_out = reduce_heads(g_qkv, g_out, n_col, heads_part, dp, z_high, z_low)

    d_rows, gain1_tok = input_grad(gx, gx_got, raw_tok, g_mid, gain1)
    d_input = lax.all_to_all(
        d_rows.reshape(4 * HALF, QUARTER), "row", split_axis=0, concat_axis=0, tiled=True
    )
    gain1_mem, conv_sum = mem_grad(g_mem, w_mem, raw_mem, gain1, conv)
    sums = sum_all(jnp.concatenate([gain1_tok + gain1_mem, gain2_sum, conv_sum], axis=0))
    sums = pick(sums.reshape(5, 4, QUARTER), row, 1)
    return (out, d_input, grad_qkv, grad_out, grad_up, grad_down, sums[0], sums[1], sums[2:])


def reduce_heads(g_qkv, g_out, n_col, heads_part, dp, z_high, z_low):
    core, x_id = dp % 2, dp // 2
    quarter = DH // 4
    g_qkv = g_qkv.reshape(HEADS, 3, 2, 2, quarter, 4, QUARTER)
    g_out = g_out.reshape(2, HEADS, 2, 2, quarter, 4, QUARTER)
    g_out = jnp.stack([pick(g_out, z_low), pick(g_out, 1 - z_low)])

    def over_dp(g, axis):
        mine, other = split_axis_of(g, axis + 1, core)
        g = add_low(mine, swap(other, "dp", 1))
        mine, other = split_axis_of(g, axis, x_id)
        return add_low(mine, swap(other, "dp", 2))

    g_qkv = over_dp(g_qkv, 2)
    g_out = over_dp(g_out, 2)
    if n_col == 2:
        c = lax.axis_index("col")
        part = heads_part // 2
        mine, other = split_axis_of(g_qkv.reshape(2, part, 3, quarter, 4, QUARTER), 0, c)
        g_qkv = add_low(mine, swap(other, "col", 1))
        mine, other = split_axis_of(g_out.reshape(2, 2, part, quarter, 4, QUARTER), 1, c)
        g_out = add_low(mine, swap(other, "col", 1))
        g_qkv = g_qkv.transpose(3, 0, 1, 2, 4).reshape(4, part * 3 * quarter, QUARTER)
        g_qkv = lax.all_to_all(g_qkv, "row", split_axis=0, concat_axis=0, tiled=True)
        g_qkv = g_qkv.astype(F32).reshape(2, 2, part, 3, quarter, QUARTER).sum(axis=0)
        g_qkv = g_qkv.reshape(heads_part, 3, quarter, QUARTER)
        g_out = g_out.transpose(3, 0, 1, 2, 4).reshape(4, heads_part, quarter, QUARTER)
        g_out = halve_row(g_out, z_high, z_low)
    else:
        zeros = jnp.zeros_like(g_qkv)
        g_qkv = jnp.where(
            z_low == 0, jnp.concatenate([g_qkv, zeros]), jnp.concatenate([zeros, g_qkv])
        )
        scatter = lambda g, axis, name: lax.psum_scatter(
            g, name, scatter_dimension=axis, tiled=True
        )
        g_qkv = scatter(scatter(g_qkv, 0, "col"), 3, "row")[:, :, :, 0].astype(F32)
        g_out = g_out.reshape((2 * HEADS,) + g_out.shape[2:])
        g_out = scatter(scatter(g_out, 0, "col"), 2, "row")[:, :, 0].astype(F32)
    return g_qkv.transpose(3, 1, 0, 2), g_out


def solution(mesh):
    tokens, features = ("dp", "col"), "row"
    placed = (
        P(tokens, features),
        P(tokens, features),
        P(tokens, features),
        P(("dp", "row")),
        P(("dp", "row")),
        P(("dp", "row")),
        P(("dp", "row")),
        P(tokens, features),
        P("row", None, "col", "dp"),
        P("col", "dp", "row"),
        P("row", tokens),
        P(tokens, "row"),
        P("row"),
        P("row"),
        P(None, "row"),
    )
    return jax.shard_map(
        per_device,
        mesh=mesh,
        in_specs=placed,
        out_specs=(
            P(tokens, features),
            P(tokens, features),
            P("row", None, "col", "dp"),
            P("col", "dp", "row"),
            P("row", tokens),
            P(tokens, "row"),
            P("row"),
            P("row"),
            P(None, "row"),
        ),
        check_vma=False,
    )
```

```python
import functools

import jax
import jax.numpy as jnp
from jax import lax
from jax.experimental import pallas as pl
from jax.experimental.pallas import tpu as pltpu
from jax.sharding import PartitionSpec as P

D = 1024
DH = 128
MEM = 512
CMEM = 512
RATE = 3
NEWC = 128
SEQ_LEN = 1024
HALF = SEQ_LEN // 2
HEADS = 4
OLD = RATE * NEWC
MROWS = CMEM + MEM
KM = MROWS + NEWC
QUARTER = D // 4
CHUNK = 256
LIMIT = 60

EPSILON = 1e-05
MASKED = -1e30
LOG2E = 1.4426950408889634
SCALE = DH**-0.5
SCALE2 = SCALE * LOG2E
F32 = jnp.float32
BF = jnp.bfloat16


def nn(a, b):
    return lax.dot_general(a, b, (((1,), (0,)), ((), ())), preferred_element_type=F32)


def nt(a, b):
    return lax.dot_general(a, b, (((1,), (1,)), ((), ())), preferred_element_type=F32)


def tn(a, b):
    return lax.dot_general(a, b, (((0,), (0,)), ((), ())), preferred_element_type=F32)


def swap(x, axis, distance):
    n = lax.axis_size(axis)
    return lax.ppermute(x, axis, [(i, i ^ distance) for i in range(n)])


def add_low(a, b):
    return (a.astype(F32) + b.astype(F32)).astype(BF)


def params(limit_mb, dims=1):
    return pltpu.CompilerParams(
        dimension_semantics=("arbitrary",) * dims, vmem_limit_bytes=limit_mb << 20
    )


ANY = pl.BlockSpec(memory_space=pl.ANY)


def cost(flops):
    return pl.CostEstimate(flops=flops, transcendentals=0, bytes_accessed=flops // 1000)


def shape(dims, kind):
    return jax.ShapeDtypeStruct(dims, kind)


def whole(dims):
    zeros = (0,) * len(dims)
    return pl.BlockSpec(dims, lambda *_: zeros)


def norm_block(pieces, gain_ref):
    values = [p.astype(F32) for p in pieces]
    mean = sum(jnp.sum(v, axis=1, keepdims=True) for v in values) / D
    values = [v - mean for v in values]
    spread = sum(jnp.sum(v * v, axis=1, keepdims=True) for v in values) / D
    factor = lax.rsqrt(spread + EPSILON)
    return [values[k] * factor * gain_ref[:, block_of(k)] for k in range(4)]


def block_of(k):
    return slice(k * QUARTER, (k + 1) * QUARTER)


def tok_norm_kernel(where, p0, p1, p2, p3, gain_ref, low_ref, raw_ref):
    pieces = [p[...] for p in (p0, p1, p2, p3)]
    normed = norm_block(pieces, gain_ref)
    for k in range(4):
        low_ref[:, block_of(k)] = normed[k].astype(BF)
        raw_ref[:, block_of(k)] = pieces[k]


def tok_norm(where, pieces, gain):
    block = 256
    count = SEQ_LEN // block
    piece = pl.BlockSpec((block, QUARTER), lambda i, w: ((i + w[0] * (count // 2)) % count, 0))
    out = pl.BlockSpec((block, D), lambda i, w: (i, 0))
    return pl.pallas_call(
        tok_norm_kernel,
        out_shape=(shape((SEQ_LEN, D), BF), shape((SEQ_LEN, D), BF)),
        grid_spec=pltpu.PrefetchScalarGridSpec(
            num_scalar_prefetch=1,
            grid=(count,),
            in_specs=[piece] * 4 + [whole((1, D))],
            out_specs=[out, out],
        ),
        compiler_params=params(LIMIT),
        name="tok_norm",
    )(where, *pieces, gain)


def mem_norm_kernel(p0, p1, p2, p3, gain_ref, conv_ref, low_ref, raw_ref, keep_ref):
    for block in range(MROWS // 256):
        rows = slice(block * 256, block * 256 + 256)
        pieces = [p[rows, :] for p in (p0, p1, p2, p3)]
        normed = norm_block(pieces, gain_ref)
        for k in range(4):
            low_ref[rows, block_of(k)] = normed[k].astype(BF)
            raw_ref[rows, block_of(k)] = pieces[k]
            if block * 256 >= CMEM:
                start = block * 256 - CMEM
                for j in range(2):
                    keep_ref[k * 2 + j, start : start + 256, :] = normed[k][:, j * DH : j * DH + DH]
    for j in range(D // DH):
        lanes = slice(j * DH, j * DH + DH)
        packed = 0.0
        for t in range(RATE):
            picked = keep_ref[j, pl.ds(t, NEWC, stride=RATE), :]
            packed = packed + conv_ref[t : t + 1, lanes] * picked
        low_ref[MROWS:, lanes] = packed.astype(BF)


def mem_norm(pieces, gain, conv):
    return pl.pallas_call(
        mem_norm_kernel,
        out_shape=(shape((KM, D), BF), shape((MROWS, D), BF)),
        grid=(1,),
        in_specs=[whole((MROWS, QUARTER))] * 4 + [whole((1, D)), whole((RATE, D))],
        out_specs=[whole((KM, D)), whole((MROWS, D))],
        scratch_shapes=[pltpu.VMEM((D // DH, MEM, DH), F32)],
        compiler_params=params(LIMIT),
        name="mem_norm",
    )(*pieces, gain, conv)


def join_kernel(*refs):
    parts, (tok_ref, mem_ref, back_ref) = refs[:4], refs[4:]
    cols, _, part, _, span, _ = parts[0].shape
    for head in range(HEADS):
        c, i = head // part, head % part
        for kind in range(5):
            for dp, ref in enumerate(parts):
                low = dp * span
                for k in range(4):
                    value = ref[c, k, i, kind]
                    if kind < 3:
                        row = (head * 3 + kind) * DH + low
                        tok_ref[row : row + span, block_of(k)] = value
                    if 0 < kind < 3:
                        row = (head * 2 + kind - 1) * DH + low
                        mem_ref[row : row + span, block_of(k)] = value
                    if kind > 2:
                        row = ((kind - 3) * HEADS + head) * DH + low
                        back_ref[row : row + span, block_of(k)] = value


def join_weights(parts):
    dims = ((HEADS * 3 * DH, D), (HEADS * 2 * DH, D), (HEADS * 2 * DH, D))
    return pl.pallas_call(
        join_kernel,
        out_shape=tuple(shape(d, BF) for d in dims),
        grid=(1,),
        in_specs=[whole(p.shape) for p in parts],
        out_specs=[whole(d) for d in dims],
        compiler_params=params(LIMIT),
        name="join_weights",
    )(*parts)


def fill_bias(bias_ref, row_ref, col_ref):
    seg_q, pos_q = row_ref[0:1, :], row_ref[1:2, :]

    def memory_chunk(c, carry):
        rows = pl.ds(pl.multiple_of(c * CHUNK, CHUNK), CHUNK)
        bias_ref[rows, :] = jnp.where(col_ref[rows, 2:3] == seg_q, 0.0, MASKED)
        return carry

    def token_chunk(c, carry):
        start = pl.multiple_of(c * CHUNK, CHUNK)
        rows = pl.ds(start, CHUNK)
        same = (col_ref[rows, 0:1] == seg_q) & (col_ref[rows, 1:2] <= pos_q)
        key_id = lax.broadcasted_iota(jnp.int32, (CHUNK, SEQ_LEN), 0) + start
        query_id = lax.broadcasted_iota(jnp.int32, (CHUNK, SEQ_LEN), 1)
        target = pl.ds(pl.multiple_of(MROWS + c * CHUNK, CHUNK), CHUNK)
        bias_ref[target, :] = jnp.where(same | (key_id == query_id), 0.0, MASKED)
        return carry

    lax.fori_loop(0, MROWS // CHUNK, memory_chunk, 0)
    lax.fori_loop(0, SEQ_LEN // CHUNK, token_chunk, 0)


def forward_kernel(tok_ref, mem_ref, row_ref, col_ref, o_ref, log_ref, bias_ref, s_ref, acc_ref):
    @pl.when(pl.program_id(0) == 0)
    def _():
        fill_bias(bias_ref, row_ref, col_ref)

    queries = tok_ref[:, :DH]

    def scores(key_ref, columns, offset):
        def step(c, top):
            rows = pl.ds(pl.multiple_of(c * CHUNK, CHUNK), CHUNK)
            target = pl.ds(pl.multiple_of(offset + c * CHUNK, CHUNK), CHUNK)
            s = nt(key_ref[rows, columns], queries) * SCALE2 + bias_ref[target, :]
            s_ref[target, :] = s
            return jnp.maximum(top, jnp.max(s.reshape(CHUNK // 8, 8, SEQ_LEN), axis=0))

        return step

    top = jnp.full((8, SEQ_LEN), -3.0e38, F32)
    top = lax.fori_loop(0, MROWS // CHUNK, scores(mem_ref, slice(0, DH), 0), top)
    top = lax.fori_loop(0, SEQ_LEN // CHUNK, scores(tok_ref, slice(DH, 2 * DH), MROWS), top)
    top = jnp.max(top, axis=0, keepdims=True)
    acc_ref[...] = jnp.zeros_like(acc_ref)

    def values(value_ref, columns, offset):
        def step(c, total):
            rows = pl.ds(pl.multiple_of(c * CHUNK, CHUNK), CHUNK)
            target = pl.ds(pl.multiple_of(offset + c * CHUNK, CHUNK), CHUNK)
            p = jnp.exp2(s_ref[target, :] - top)
            acc_ref[...] += nn(value_ref[rows, columns].T, p.astype(BF))
            return total + jnp.sum(p.reshape(CHUNK // 8, 8, SEQ_LEN), axis=0)

        return step

    total = jnp.zeros((8, SEQ_LEN), F32)
    total = lax.fori_loop(0, MROWS // CHUNK, values(mem_ref, slice(DH, 2 * DH), 0), total)
    total = lax.fori_loop(
        0, SEQ_LEN // CHUNK, values(tok_ref, slice(2 * DH, 3 * DH), MROWS), total
    )
    total = jnp.sum(total, axis=0, keepdims=True)
    o_ref[...] = (acc_ref[...] / total).T.astype(BF)
    log_ref[...] = (top + jnp.log2(total)).reshape(1, 1, SEQ_LEN)


def attention_forward(tok_p, mem_p, row_attr, col_attr):
    return pl.pallas_call(
        forward_kernel,
        out_shape=(shape((SEQ_LEN, HEADS * DH), BF), shape((HEADS, 1, SEQ_LEN), F32)),
        grid=(HEADS,),
        in_specs=[
            pl.BlockSpec((SEQ_LEN, 3 * DH), lambda h: (0, h)),
            pl.BlockSpec((KM, 2 * DH), lambda h: (0, h)),
            whole(row_attr.shape),
            whole(col_attr.shape),
        ],
        out_specs=[
            pl.BlockSpec((SEQ_LEN, DH), lambda h: (0, h)),
            pl.BlockSpec((1, 1, SEQ_LEN), lambda h: (h, 0, 0)),
        ],
        scratch_shapes=[
            pltpu.VMEM((MROWS + SEQ_LEN, SEQ_LEN), F32),
            pltpu.VMEM((MROWS + SEQ_LEN, SEQ_LEN), F32),
            pltpu.VMEM((DH, SEQ_LEN), F32),
        ],
        compiler_params=params(LIMIT),
        cost_estimate=cost(25_000_000_000),
        name="attention_forward",
    )(tok_p, mem_p, row_attr, col_attr)


def recon_kernel(tok_ref, mem_ref, _, gq_ref, gm_ref):
    q = tok_ref[:, :DH]
    old, new = slice(CMEM, CMEM + OLD), slice(MROWS, KM)
    keys, values = slice(0, DH), slice(DH, 2 * DH)

    def softmax_rows(key_rows):
        s = nt(key_rows, q) * SCALE2
        p = jnp.exp2(s - jnp.max(s, axis=0, keepdims=True))
        return p / jnp.sum(p, axis=0, keepdims=True)

    ko, vo, kn, vn = mem_ref[old, keys], mem_ref[old, values], mem_ref[new, keys], mem_ref[new, values]
    po, pn = softmax_rows(ko), softmax_rows(kn)
    po_low, pn_low = po.astype(BF), pn.astype(BF)
    out_o, out_n = nn(vo.T, po_low), nn(vn.T, pn_low)
    gap = (out_o - out_n).astype(BF)
    gap32 = gap.astype(F32)
    do = (po * (nn(vo, gap) - jnp.sum(gap32 * out_o, axis=0, keepdims=True))).astype(BF)
    dn = (pn * (jnp.sum(gap32 * out_n, axis=0, keepdims=True) - nn(vn, gap))).astype(BF)
    gq_ref[...] = ((nn(ko.T, do) + nn(kn.T, dn)) * SCALE).reshape(1, DH, SEQ_LEN)
    gap_t = gap32.T.astype(BF)
    gm_ref[:OLD, keys] = nn(do, q) * SCALE
    gm_ref[:OLD, values] = nn(po_low, gap_t)
    gm_ref[OLD:MEM, :] = jnp.zeros((MEM - OLD, 2 * DH), F32)
    gm_ref[MEM:, keys] = nn(dn, q) * SCALE
    gm_ref[MEM:, values] = -nn(pn_low, gap_t)


def reconstruction(tok_p, mem_p, earlier):
    return pl.pallas_call(
        recon_kernel,
        out_shape=(
            shape((HEADS, DH, SEQ_LEN), F32),
            shape((MEM + NEWC, HEADS * 2 * DH), F32),
        ),
        grid=(HEADS,),
        in_specs=[
            pl.BlockSpec((SEQ_LEN, 3 * DH), lambda h: (0, h)),
            pl.BlockSpec((KM, 2 * DH), lambda h: (0, h)),
            ANY,
        ],
        out_specs=[
            pl.BlockSpec((1, DH, SEQ_LEN), lambda h: (h, 0, 0)),
            pl.BlockSpec((MEM + NEWC, 2 * DH), lambda h: (0, h)),
        ],
        compiler_params=params(LIMIT),
        cost_estimate=cost(10_000_000_000),
        name="reconstruction",
    )(tok_p, mem_p, earlier)


def backward_kernel(
    tok_ref, mem_ref, own_ref, got_ref, o_ref, log_ref, rq_ref, rm_ref, row_ref, col_ref,
    *refs,
):
    gt_ref, gm_ref, bias_ref, acc_ref = refs[-4:]

    @pl.when(pl.program_id(0) == 0)
    def _():
        fill_bias(bias_ref, row_ref, col_ref)

    q = tok_ref[:, :DH]
    go = jnp.concatenate([own_ref[...], got_ref[...]], axis=0)
    product = go.astype(F32) * o_ref[...].astype(F32)
    delta = jnp.sum(product.T, axis=0, keepdims=True)
    log_total = log_ref[...].reshape(1, SEQ_LEN)
    acc_ref[...] = rq_ref[...].reshape(DH, SEQ_LEN)

    def piece(k, v, offset):
        s = nt(k, q) * SCALE2 + bias_ref[offset, :]
        p = jnp.exp2(s - log_total)
        d = (p * (nt(v, go) - delta)).astype(BF)
        acc_ref[...] += nn(k.T, d) * SCALE
        return nn(d, q) * SCALE, nn(p.astype(BF), go)

    def memory_chunk(c, carry):
        rows = pl.ds(pl.multiple_of(c * CHUNK, CHUNK), CHUNK)
        gk, gv = piece(mem_ref[rows, :DH], mem_ref[rows, DH:], rows)
        gm_ref[rows, :DH] = gk.astype(BF)
        gm_ref[rows, DH:] = gv.astype(BF)
        return carry

    def shared_chunk(c, carry):
        rows = pl.ds(pl.multiple_of(c * CHUNK, CHUNK), CHUNK)
        extra = pl.ds(pl.multiple_of(c * CHUNK - CMEM, CHUNK), CHUNK)
        gk, gv = piece(mem_ref[rows, :DH], mem_ref[rows, DH:], rows)
        gm_ref[rows, :DH] = (gk + rm_ref[extra, :DH]).astype(BF)
        gm_ref[rows, DH:] = (gv + rm_ref[extra, DH:]).astype(BF)
        return carry

    def token_chunk(c, carry):
        rows = pl.ds(pl.multiple_of(c * CHUNK, CHUNK), CHUNK)
        target = pl.ds(pl.multiple_of(MROWS + c * CHUNK, CHUNK), CHUNK)
        gk, gv = piece(tok_ref[rows, DH : 2 * DH], tok_ref[rows, 2 * DH :], target)
        gt_ref[rows, DH : 2 * DH] = gk.astype(BF)
        gt_ref[rows, 2 * DH :] = gv.astype(BF)
        return carry

    lax.fori_loop(0, CMEM // CHUNK, memory_chunk, 0)
    lax.fori_loop(CMEM // CHUNK, MROWS // CHUNK, shared_chunk, 0)
    lax.fori_loop(0, SEQ_LEN // CHUNK, token_chunk, 0)
    gm_ref[MROWS:, :] = rm_ref[MEM:, :].astype(BF)
    gt_ref[:, :DH] = acc_ref[...].T.astype(BF)


def attention_backward(
    tok_p, mem_p, go_own, go_got, o, logs, rec_q, rec_m, row_attr, col_attr, *earlier
):
    half = pl.BlockSpec((HALF, DH), lambda h: (0, h))
    return pl.pallas_call(
        backward_kernel,
        out_shape=(
            shape((SEQ_LEN, HEADS * 3 * DH), BF),
            shape((KM, HEADS * 2 * DH), BF),
        ),
        grid=(HEADS,),
        in_specs=[
            pl.BlockSpec((SEQ_LEN, 3 * DH), lambda h: (0, h)),
            pl.BlockSpec((KM, 2 * DH), lambda h: (0, h)),
            half,
            half,
            pl.BlockSpec((SEQ_LEN, DH), lambda h: (0, h)),
            pl.BlockSpec((1, 1, SEQ_LEN), lambda h: (h, 0, 0)),
            pl.BlockSpec((1, DH, SEQ_LEN), lambda h: (h, 0, 0)),
            pl.BlockSpec((MEM + NEWC, 2 * DH), lambda h: (0, h)),
            whole(row_attr.shape),
            whole(col_attr.shape),
        ]
        + [ANY] * len(earlier),
        out_specs=[
            pl.BlockSpec((SEQ_LEN, 3 * DH), lambda h: (0, h)),
            pl.BlockSpec((KM, 2 * DH), lambda h: (0, h)),
        ],
        scratch_shapes=[
            pltpu.VMEM((MROWS + SEQ_LEN, SEQ_LEN), F32),
            pltpu.VMEM((DH, SEQ_LEN), F32),
        ],
        compiler_params=params(LIMIT),
        cost_estimate=cost(35_000_000_000),
        name="attention_backward",
    )(tok_p, mem_p, go_own, go_got, o, logs, rec_q, rec_m, row_attr, col_attr, *earlier)


def center_rows(rows):
    centered = rows - jnp.mean(rows, axis=1, keepdims=True)
    factor = lax.rsqrt(jnp.mean(centered * centered, axis=1, keepdims=True) + EPSILON)
    return centered * factor, factor


def mid_kernel(raw_ref, own_ref, got_ref, w_ref, gain_ref, _, mid_ref, x2_ref):
    width = own_ref.shape[1]
    mid = raw_ref[...].astype(F32) + (
        nn(own_ref[...], w_ref[:width, :]) + nn(got_ref[...], w_ref[width:, :])
    )
    unit, _ = center_rows(mid)
    mid_ref[...] = mid
    x2_ref[...] = (unit * gain_ref[...]).astype(BF)


def residual_mid(raw, o, o_got, w_out, gain, earlier):
    block = 256
    rows = lambda width: pl.BlockSpec((block, width), lambda i: (i, 0))
    return pl.pallas_call(
        mid_kernel,
        out_shape=(shape((HALF, D), F32), shape((HALF, D), BF)),
        grid=(HALF // block,),
        in_specs=[rows(D), rows(HEADS * DH), rows(HEADS * DH), whole((D, D)), whole((1, D)), ANY],
        out_specs=[rows(D), rows(D)],
        compiler_params=params(LIMIT),
        cost_estimate=cost(4 * HALF * D * D),
        name="residual_mid",
    )(raw, o, o_got, w_out, gain, earlier)


TILE = 256


def ffn_kernel(*refs):
    x_own, x_got, c_own, c_got = refs[:4]
    plain, far_up, far_down = refs[4:7], refs[7], refs[8]
    out_keep, out_send, gx_keep, gx_send = refs[9:13]
    grads = refs[13:18]
    x_ref, xt_ref, c_ref, ct_ref, out_ref, gx_ref, up_ref, down_ref = refs[18:]
    step, last = pl.program_id(0), pl.num_programs(0) - 1
    block = step // (pl.num_programs(0) // 4)

    @pl.when(step == 0)
    def _():
        out_ref[...] = jnp.zeros_like(out_ref)
        gx_ref[...] = jnp.zeros_like(gx_ref)
        for (own, got), full, turned in (
            ((x_own, x_got), x_ref, xt_ref),
            ((c_own, c_got), c_ref, ct_ref),
        ):
            for j, half in enumerate((own, got)):
                full[j * HALF : (j + 1) * HALF, :] = half[...]
                for i in range(0, HALF, 256):
                    turned[:, j * HALF + i : j * HALF + i + 256] = half[i : i + 256, :].T

    for k, ref in enumerate(plain):
        @pl.when(block == k)
        def _():
            up_ref[...] = ref[0].reshape(D, TILE)
            down_ref[...] = ref[1].reshape(D, TILE)

    @pl.when(block == 3)
    def _():
        up_ref[...] = far_up[...].reshape(D, TILE)
        down_ref[...] = far_down[...].reshape(D, TILE)

    w_up, w_down = up_ref[...], down_ref[...]
    v = nn(x_ref[...], w_up)
    g_act = nn(c_ref[...], w_down)
    c0, c1 = 0.7978845608028654, 0.044715
    v2 = v * v
    t = jnp.tanh(c0 * v * (1.0 + c1 * v2))
    half = 0.5 * (1.0 + t)
    act = (v * half).astype(BF)
    slope = half + (0.5 * c0) * v * (1.0 - t * t) * (1.0 + (3.0 * c1) * v2)
    g_pre = (g_act * slope).astype(BF)
    out_ref[...] += nt(act, w_down)
    gx_ref[...] += nt(g_pre, w_up)
    grad_up = nn(xt_ref[...], g_pre).astype(BF).reshape(4, QUARTER, TILE)
    grad_down = nn(ct_ref[...], act).astype(BF).reshape(4, QUARTER, TILE)

    for k in range(3):
        @pl.when(block == k)
        def _():
            grads[k][0] = grad_up
            grads[k][1] = grad_down

    @pl.when(block == 3)
    def _():
        grads[3][...] = grad_up
        grads[4][...] = grad_down

    @pl.when(step == last)
    def _():
        for total, keep, send in ((out_ref, out_keep, out_send), (gx_ref, gx_keep, gx_send)):
            keep[...] = total[:HALF, :]
            send[...] = total[HALF:, :].astype(BF)


def feed_forward(x2, x2_got, cot, cot_got, plain, far_up, far_down):
    width = far_up.shape[-1]
    tiles = width // TILE

    def tile(k, step):
        return jnp.clip(step - k * tiles, 0, tiles - 1)

    def pair(k):
        return pl.BlockSpec((2, 4, QUARTER, TILE), lambda i: (0, 0, 0, tile(k, i)))

    far = pl.BlockSpec((4, QUARTER, TILE), lambda i: (0, 0, tile(3, i)))
    blocks = [pair(0), pair(1), pair(2), far, far]
    once = pl.BlockSpec((HALF, D), lambda i: (0, 0), pipeline_mode=pl.Buffered(1))
    rows = whole((HALF, D))
    full, turned = pltpu.VMEM((SEQ_LEN, D), BF), pltpu.VMEM((D, SEQ_LEN), BF)
    total = pltpu.VMEM((SEQ_LEN, D), F32)
    return pl.pallas_call(
        ffn_kernel,
        out_shape=(
            shape((HALF, D), F32), shape((HALF, D), BF),
            shape((HALF, D), F32), shape((HALF, D), BF),
        )
        + (shape(plain[0].shape, BF),) * 3
        + (shape(far_up.shape, BF),) * 2,
        grid=(4 * tiles,),
        in_specs=[once] * 4 + blocks,
        out_specs=[rows] * 4 + blocks,
        scratch_shapes=[full, turned, full, turned, total, total] + [pltpu.VMEM((D, TILE), BF)] * 2,
        compiler_params=params(LIMIT),
        cost_estimate=cost(12 * SEQ_LEN * D * 4 * width),
        name="feed_forward",
    )(x2, x2_got, cot, cot_got, *plain, far_up, far_down)


def mid_back_kernel(gx_ref, got_ref, mid_ref, cot_ref, gain_ref, w_ref, gm_ref, ga_ref, keep_ref, send_ref, gn_ref):
    @pl.when(pl.program_id(0) == 0)
    def _():
        gn_ref[...] = jnp.zeros_like(gn_ref)

    unit, factor = center_rows(mid_ref[...])
    gx = gx_ref[...] + got_ref[...].astype(F32)
    gn_ref[...] += jnp.sum(gx * unit, axis=0, keepdims=True)
    s = gx * gain_ref[...]
    g_mid = cot_ref[...].astype(F32) + factor * (
        s - jnp.mean(s, axis=1, keepdims=True) - unit * jnp.mean(s * unit, axis=1, keepdims=True)
    )
    gm_ref[...] = g_mid
    low = g_mid.astype(BF)
    ga_ref[...] = low
    width = keep_ref.shape[1]
    send_ref[...] = nt(low, w_ref[width:, :]).astype(BF)
    keep_ref[...] = nt(low, w_ref[:width, :]).astype(BF)


def mid_back(gx, gx_got, mid, cot, gain, w_out):
    block = 256
    rows = lambda width: pl.BlockSpec((block, width), lambda i: (i, 0))
    half = shape((HALF, HEADS * DH), BF)
    return pl.pallas_call(
        mid_back_kernel,
        out_shape=(shape((HALF, D), F32), shape((HALF, D), BF), half, half, shape((1, D), F32)),
        grid=(HALF // block,),
        in_specs=[rows(D)] * 4 + [whole((1, D)), whole((D, D))],
        out_specs=[rows(D), rows(D), rows(HEADS * DH), rows(HEADS * DH), whole((1, D))],
        compiler_params=params(LIMIT),
        cost_estimate=cost(2 * HALF * D * D),
        name="mid_back",
    )(gx, gx_got, mid, cot, gain, w_out)


def tok_grad_kernel(g_ref, w_ref, raw_ref, *refs):
    keep_ref, send_ref, gn_ref = refs[-3:]
    step = pl.program_id(0)

    @pl.when(step == 0)
    def _():
        gn_ref[...] = jnp.zeros_like(gn_ref)

    gx = nn(g_ref[...], w_ref[...])
    unit, _ = center_rows(raw_ref[...].astype(F32))
    gn_ref[...] += jnp.sum(gx * unit, axis=0, keepdims=True)

    @pl.when(step < pl.num_programs(0) // 2)
    def _():
        send_ref[...] = gx.astype(BF)

    @pl.when(step >= pl.num_programs(0) // 2)
    def _():
        keep_ref[...] = gx


def tok_grad(g_tok, w_tok, raw, *earlier):
    block = 256
    steps, half = SEQ_LEN // block, HALF // block
    rows = lambda width: pl.BlockSpec((block, width), lambda i: ((i + half) % steps, 0))
    return pl.pallas_call(
        tok_grad_kernel,
        out_shape=(shape((HALF, D), F32), shape((HALF, D), BF), shape((1, D), F32)),
        grid=(steps,),
        in_specs=[rows(HEADS * 3 * DH), whole((HEADS * 3 * DH, D)), rows(D)]
        + [ANY] * len(earlier),
        out_specs=[
            pl.BlockSpec((block, D), lambda i: (jnp.maximum(i - half, 0), 0)),
            pl.BlockSpec((block, D), lambda i: (jnp.minimum(i, half - 1), 0)),
            whole((1, D)),
        ],
        compiler_params=params(LIMIT),
        cost_estimate=cost(2 * SEQ_LEN * HEADS * 3 * DH * D),
        name="tok_grad",
    )(g_tok, w_tok, raw, *earlier)


def input_grad_kernel(keep_ref, got_ref, raw_ref, gm_ref, gain_ref, *refs):
    out_ref = refs[-1]
    unit, factor = center_rows(raw_ref[...].astype(F32))
    got = [got_ref[:, block_of(k ^ 1)].astype(F32) for k in range(4)]
    s = (keep_ref[...] + jnp.concatenate(got, axis=1)) * gain_ref[...]
    g = gm_ref[...] + factor * (
        s - jnp.mean(s, axis=1, keepdims=True) - unit * jnp.mean(s * unit, axis=1, keepdims=True)
    )
    for k in range(4):
        out_ref[k] = g[:, k * QUARTER : (k + 1) * QUARTER].astype(BF)


def input_grad(keep, got, raw, g_mid, gain, *earlier):
    block = 256
    rows = pl.BlockSpec((block, D), lambda i: (i, 0))
    return pl.pallas_call(
        input_grad_kernel,
        out_shape=shape((4, HALF, QUARTER), BF),
        grid=(HALF // block,),
        in_specs=[rows, rows, rows, rows, whole((1, D))] + [ANY] * len(earlier),
        out_specs=pl.BlockSpec((4, block, QUARTER), lambda i: (0, i, 0)),
        compiler_params=params(LIMIT),
        cost_estimate=cost(2 * HALF * D * D),
        name="input_grad",
    )(keep, got, raw, g_mid, gain, *earlier)


def mem_grad_kernel(g_ref, w_ref, raw_ref, gain_ref, conv_ref, _, gn_ref, gc_ref, unit_ref):
    total = jnp.zeros((1, D), F32)
    for block in range(MROWS // 256):
        rows = slice(block * 256, block * 256 + 256)
        unit, _ = center_rows(raw_ref[rows, :].astype(F32))
        total = total + jnp.sum(nn(g_ref[rows, :], w_ref[...]) * unit, axis=0, keepdims=True)
        if block * 256 >= CMEM:
            start = block * 256 - CMEM
            for j in range(D // DH):
                unit_ref[j, start : start + 256, :] = unit[:, j * DH : j * DH + DH]
    gn_ref[...] = total
    packed = nn(g_ref[MROWS:, :], w_ref[...])
    for j in range(D // DH):
        lanes = slice(j * DH, j * DH + DH)
        for t in range(RATE):
            picked = unit_ref[j, pl.ds(t, NEWC, stride=RATE), :]
            term = jnp.sum(packed[:, lanes] * picked, axis=0, keepdims=True)
            gc_ref[t : t + 1, lanes] = term * gain_ref[:, lanes]
            gn_ref[:, lanes] += conv_ref[t : t + 1, lanes] * term


def mem_grad(g_mem, w_mem, raw, gain, conv, earlier):
    return pl.pallas_call(
        mem_grad_kernel,
        out_shape=(shape((1, D), F32), shape((RATE, D), F32)),
        grid=(1,),
        in_specs=[
            whole((KM, D)), whole((D, D)), whole((MROWS, D)), whole((1, D)), whole((RATE, D)), ANY,
        ],
        out_specs=[whole((1, D)), whole((RATE, D))],
        scratch_shapes=[pltpu.VMEM((D // DH, MEM, DH), F32)],
        compiler_params=params(LIMIT),
        name="mem_grad",
    )(g_mem, w_mem, raw, gain, conv, earlier)


def store_spans(grad, index, keep_ref, send_ref):
    span = DH // 4
    for x in range(2):
        for core, ref in enumerate((keep_ref, send_ref)):
            row = (2 * x + core) * span
            ref[(x,) + index] = grad[row : row + span, :].astype(BF)


def qkv_grad_kernel(gt_ref, xt_ref, gm_ref, xm_ref, *refs):
    for kind in range(3):
        grad = nn(gt_ref[:, kind * DH : (kind + 1) * DH].T, xt_ref[...])
        if kind > 0:
            grad = grad + nn(gm_ref[:, (kind - 1) * DH : kind * DH].T, xm_ref[...])
        store_spans(grad, (0, kind), *refs[-2:])


def qkv_grad(g_tok, x_tok, g_mem, x_mem, *earlier):
    out = shape((2, HEADS, 3, DH // 4, D), BF)
    block = pl.BlockSpec((2, 1, 3, DH // 4, D), lambda h: (0, h, 0, 0, 0))
    return pl.pallas_call(
        qkv_grad_kernel,
        out_shape=(out, out),
        grid=(HEADS,),
        in_specs=[
            pl.BlockSpec((SEQ_LEN, 3 * DH), lambda h: (0, h)),
            whole((SEQ_LEN, D)),
            pl.BlockSpec((KM, 2 * DH), lambda h: (0, h)),
            whole((KM, D)),
        ]
        + [ANY] * len(earlier),
        out_specs=[block, block],
        compiler_params=params(LIMIT),
        cost_estimate=cost(2 * HEADS * DH * D * (3 * SEQ_LEN + 2 * KM)),
        name="qkv_grad",
    )(g_tok, x_tok, g_mem, x_mem, *earlier)


def out_grad_kernel(own_ref, got_ref, g_ref, keep_ref, send_ref):
    for z, ref in enumerate((own_ref, got_ref)):
        store_spans(nn(ref[...].T, g_ref[...]), (z, 0), keep_ref, send_ref)


def out_grad(o, o_got, g_attn):
    out = shape((2, 2, HEADS, DH // 4, D), BF)
    block = pl.BlockSpec((2, 2, 1, DH // 4, D), lambda h: (0, 0, h, 0, 0))
    half = pl.BlockSpec((HALF, DH), lambda h: (0, h))
    return pl.pallas_call(
        out_grad_kernel,
        out_shape=(out, out),
        grid=(HEADS,),
        in_specs=[half, half, whole((HALF, D))],
        out_specs=[block, block],
        compiler_params=params(LIMIT),
        cost_estimate=cost(4 * HALF * HEADS * DH * D),
        name="out_grad",
    )(o, o_got, g_attn)


def pick(g, index, axis=0):
    return lax.dynamic_index_in_dim(g, index, axis, keepdims=False)


def after(value, *earlier):
    return pl.pallas_call(
        lambda *refs: None,
        out_shape=shape(value.shape, value.dtype),
        in_specs=[ANY] * (1 + len(earlier)),
        out_specs=ANY,
        input_output_aliases={0: 0},
        name="after",
    )(value, *earlier)


def doubled(g, axis, distance):
    return jnp.concatenate([g, swap(g, axis, distance)], axis=0)


def both(parts, axis, distance):
    return parts + [swap(p, axis, distance) for p in parts]


def doubled_cols(g, n_col, first=1):
    while first < n_col:
        g = doubled(g, "col", first)
        first *= 2
    return g


def halve_col(g, last=1):
    while g.shape[0] > 1:
        n = g.shape[0] // 2
        g = add_low(g[:n], swap(g[n:], "col", n * last))
    return g[0]


def halve_row(g):
    g = add_low(g[:2], swap(g[2:], "row", 2))
    return g[0].astype(F32) + swap(g[1], "row", 1).astype(F32)


def per_device(
    hidden, memory, compressed, seg_ids, positions, keep_mask, mem_seg, cotangent,
    w_qkv, w_out, w_up, w_down, norm_attn, norm_ffn, conv_w,
):
    n_col = lax.axis_size("col")
    heads_part = w_qkv.shape[2]
    part = max(heads_part // 2, 1)
    row, col = lax.axis_index("row"), lax.axis_index("col")
    z_high, z_low = row // 2, row % 2
    low_first = z_low == 0
    where = z_low.reshape(1).astype(jnp.int32)
    span = DH // 4

    def by_low(pair):
        return jnp.where(low_first, pair, jnp.flip(pair, axis=0))

    tokens = hidden.reshape(2, SEQ_LEN, QUARTER)
    tok_mine, tok_other = pick(tokens, z_high), pick(tokens, 1 - z_high)
    tok_far, tok_near = swap(tok_other, "row", 2), swap(tok_mine, "row", 1)
    tok_pieces = [tok_mine, tok_near, tok_far, swap(tok_far, "row", 1)]

    small = jnp.concatenate(
        [norm_attn, norm_ffn, conv_w.reshape(-1)]
        + [a.astype(F32) for a in (seg_ids, positions, keep_mask, mem_seg)]
    )
    small = after(small, tok_near)
    shared = jnp.stack([small] + [swap(small, "row", k) for k in (1, 2, 3)])
    gains = shared[:, : 5 * QUARTER].reshape(4, 5, QUARTER).transpose(1, 0, 2).reshape(5, D)
    gain1, gain2, conv = gains[0:1], gains[1:2], gains[2:5]
    spans = seg_ids.shape[0] // SEQ_LEN
    sequence = 2 * col + z_high
    ids = pick(shared, row ^ (sequence // spans))[5 * QUARTER :]
    ids = pick(ids.reshape(4, spans, SEQ_LEN), sequence % spans, 1)
    rolled = jnp.concatenate([ids[:3, HALF:], ids[:3, :HALF]], axis=1)
    seg, pos, keep = jnp.where(low_first, ids[:3], rolled)
    row_attr = jnp.stack([seg, pos])
    col_attr = jnp.stack([jnp.where(keep == 1, seg, -2.0), pos, ids[3]], axis=1)

    qkv = w_qkv.astype(BF).transpose(2, 1, 3, 0)
    outs = w_out.astype(BF)
    if heads_part % 2 == 0:
        qkv = by_low(qkv.reshape(2, part, 3, span, QUARTER))
        outs = by_low(outs.reshape(2, part, 1, span, QUARTER))
        near = jnp.concatenate([qkv[0], outs[0], outs[1]], axis=1)
        far = jnp.concatenate([qkv[1], outs[1], outs[0]], axis=1)
        heads = jnp.stack(
            [near, swap(far, "row", 1), swap(near, "row", 2), swap(far, "row", 3)]
        )
        heads = doubled_cols(heads[None], n_col)
    else:
        qkv = jnp.stack([qkv] + [swap(qkv, "row", k) for k in (1, 2, 3)])
        outs = jnp.stack([outs] + [swap(outs, "row", k) for k in (1, 2, 3)])
        qkv = doubled_cols(jnp.where(low_first, qkv, swap(qkv, "col", 1))[None], n_col, 2)
        outs = doubled_cols(outs[None], n_col, 2)
        outs = by_low(jnp.stack([outs, swap(outs, "col", 1)]))
        heads = jnp.concatenate([qkv, jnp.moveaxis(outs, 0, 3)], axis=3)
    heads = both(both([heads], "dp", 2), "dp", 1)
    w_tok, w_mem, w_back = join_weights([heads[0], heads[2], heads[1], heads[3]])

    own = after(jnp.stack([w_up.astype(BF), w_down.astype(BF).T]), tok_far, tok_near)
    w_far = swap(own, "row", 2)
    own = after(own, w_far, tok_pieces[3])
    w_near = swap(own, "row", 1)
    own = jnp.stack([own, w_near, w_far, swap(w_far, "row", 1)], axis=1)
    half_col = n_col // 2
    distance = 1
    while distance < half_col:
        own = jnp.concatenate([own, swap(own, "col", distance)], axis=3)
        distance *= 2
    own_y, own_x = swap(own, "col", half_col), swap(own, "dp", 2)
    far_up, far_down = swap(own_x[0], "col", half_col), swap(own_y[1], "dp", 2)

    memories = jnp.concatenate(
        [compressed.reshape(2, CMEM, QUARTER), memory.reshape(2, MEM, QUARTER)], axis=1
    )
    mem_other = after(pick(memories, 1 - z_high), w_far, tok_pieces[3])
    mem_far = swap(mem_other, "row", 2)
    mem_mine = after(pick(memories, z_high), mem_far, w_near)
    mem_near = swap(mem_mine, "row", 1)
    mem_pieces = [mem_mine, mem_near, mem_far, swap(mem_far, "row", 1)]

    x_tok, raw_tok = tok_norm(where, tok_pieces, gain1)
    tok_p = nt(x_tok, w_tok).astype(BF)
    x_mem, raw_mem = mem_norm(mem_pieces, gain1, conv)
    mem_p = nt(x_mem, w_mem).astype(BF)
    cots = after(cotangent.reshape(4, HALF, QUARTER), mem_p, tok_p)
    cot = jnp.concatenate(
        [pick(cots, row)] + [swap(pick(cots, row ^ k), "row", k) for k in (1, 2, 3)], axis=1
    )
    cot_got = swap(cot, "dp", 1)
    o, logs = attention_forward(tok_p, mem_p, row_attr, col_attr)
    o_got = swap(o[HALF:], "row", 1)
    rec_q, rec_m = reconstruction(tok_p, mem_p, cot)
    mid, x2 = residual_mid(raw_tok, o, o_got, w_back, gain2, rec_m)

    x2_got = swap(x2, "dp", 1)
    out_keep, out_send, gx_keep, gx_send, *grads = feed_forward(
        x2, x2_got, cot, cot_got, (own, own_y, own_x), far_up, far_down
    )
    gx_got = swap(gx_send, "dp", 1)
    g_mid, g_attn, go_keep, go_send, gain2_sum = mid_back(
        gx_keep, gx_got, mid, cot, gain2, w_back
    )
    go_got = swap(go_send, "row", 1)

    own, own_y, own_x, far_up, far_down = grads
    far_up, far_down = swap(far_up, "col", half_col), swap(far_down, "dp", 2)
    sum_x = own_x.at[0].set(add_low(own_x[0], far_up))
    sum_y = own_y.at[1].set(add_low(own_y[1], far_down))
    got_x, got_y = swap(sum_x, "dp", 2), swap(sum_y, "col", half_col)

    def to_owners(blocks):
        return [blocks[0]] + [swap(blocks[k], "row", k) for k in (1, 2, 3)]

    def in_order(blocks):
        blocks = [jnp.where(low_first, blocks[k], blocks[k ^ 1]) for k in range(4)]
        blocks = [jnp.where(z_high == 0, blocks[k], blocks[k ^ 2]) for k in range(4)]
        return jnp.concatenate(blocks, axis=0)

    out_got = swap(out_send, "dp", 1)
    out_low = (mid + (out_keep + out_got.astype(F32))).astype(BF)
    out_low = after(jnp.stack([out_low[:, block_of(k)] for k in range(4)]), go_got)
    outs = to_owners([out_low[k] for k in range(4)])
    g_out = out_grad(o, o_got, g_attn)

    g_tok, g_mem = attention_backward(
        tok_p, mem_p, go_keep, go_got, o, logs, rec_q, rec_m, row_attr, col_attr,
        sum_x, sum_y, out_low, g_out[0],
    )
    gx, gx_send, gain1_tok = tok_grad(g_tok, w_tok, raw_tok, *outs[1:])
    gx_got = swap(gx_send, "row", 1)

    total = (own.astype(F32) + got_x.astype(F32) + got_y.astype(F32)).astype(BF)
    distance = half_col
    while distance > 1:
        distance //= 2
        n = total.shape[3] // 2
        total = add_low(total[..., :n], swap(total[..., n:], "col", distance))
    odd = total[:, 1::2]
    g_qkv = qkv_grad(g_tok, x_tok, g_mem, x_mem, odd, gx_send)
    grad_qkv, grad_out = reduce_heads(g_qkv, g_out, n_col, heads_part, by_low, low_first)
    even = add_low(total[:, 0::2], swap(odd, "row", 1))
    grads = even[:, 0].astype(F32) + swap(even[:, 1], "row", 2).astype(F32)

    d_rows = input_grad(gx, gx_got, raw_tok, g_mid, gain1, even, g_qkv[0])
    d_input = in_order(to_owners([d_rows[k] for k in range(4)]))
    out = in_order(outs)
    gain1_mem, conv_sum = mem_grad(g_mem, w_mem, raw_mem, gain1, conv, g_qkv[0])
    total = jnp.concatenate([gain1_tok + gain1_mem, gain2_sum, conv_sum], axis=0)
    total = total.reshape(5, 4, QUARTER).transpose(1, 0, 2)
    for distance in (1, 2):
        total = total + swap(total, "dp", distance)
    distance = 1
    while distance < n_col:
        total = total + swap(total, "col", distance)
        distance *= 2
    total = total[:2] + swap(total[2:], "row", 2)
    total = total[0] + swap(total[1], "row", 1)
    return (
        out, d_input, grad_qkv, grad_out, grads[0], grads[1].T, total[0], total[1], total[2:]
    )


def reduce_heads(g_qkv, g_out, n_col, heads_part, by_low, low_first):
    span = DH // 4

    def over_dp(keep, send):
        g = add_low(keep, swap(send, "dp", 1))
        return add_low(g[0], swap(g[1], "dp", 2))

    def over_row(g):
        g = add_low(g[..., : D // 2], swap(g[..., D // 2 :], "row", 2))
        return g[..., :QUARTER], swap(g[..., QUARTER:], "row", 1)

    g_out = over_dp(*g_out)
    g_qkv = over_dp(*g_qkv)
    if heads_part % 2 == 0:
        part = heads_part // 2
        g_out = halve_col(jnp.swapaxes(g_out.reshape((2, n_col, part) + g_out.shape[2:]), 0, 1))
        g_qkv = halve_col(g_qkv.reshape((n_col, part) + g_qkv.shape[1:]))
        g_qkv = by_low(jnp.stack(over_row(g_qkv))).astype(F32)
        g_qkv = g_qkv.reshape(heads_part, 3, span, QUARTER)
        g_out, got = over_row(g_out)
        g_out = by_low(g_out.astype(F32) + jnp.flip(got, axis=0).astype(F32))
        g_out = g_out.reshape(heads_part, span, QUARTER)
    else:
        g_qkv = halve_col(g_qkv, 2)
        zeros = jnp.zeros_like(g_qkv)
        g_qkv = add_low(
            jnp.where(low_first, g_qkv, zeros), swap(jnp.where(low_first, zeros, g_qkv), "col", 1)
        )
        g_out = by_low(g_out)
        g_out = halve_col(add_low(g_out[0], swap(g_out[1], "col", 1)), 2)
        g_qkv = halve_row(jnp.moveaxis(g_qkv.reshape(3, span, 4, QUARTER), 2, 0))[None]
        g_out = halve_row(jnp.moveaxis(g_out.reshape(span, 4, QUARTER), 1, 0))[None]
    return g_qkv.transpose(3, 1, 0, 2), g_out


def solution(mesh):
    tokens, features = ("dp", "col"), "row"
    placed = (
        P(tokens, features),
        P(tokens, features),
        P(tokens, features),
        P(("dp", "row")),
        P(("dp", "row")),
        P(("dp", "row")),
        P(("dp", "row")),
        P(tokens, features),
        P("row", None, "col", "dp"),
        P("col", "dp", "row"),
        P("row", tokens),
        P(tokens, "row"),
        P("row"),
        P("row"),
        P(None, "row"),
    )
    return jax.shard_map(
        per_device,
        mesh=mesh,
        in_specs=placed,
        out_specs=(
            P(tokens, features),
            P(tokens, features),
            P("row", None, "col", "dp"),
            P("col", "dp", "row"),
            P("row", tokens),
            P(tokens, "row"),
            P("row"),
            P("row"),
            P(None, "row"),
        ),
        check_vma=False,
    )
```

```python
import functools

import jax
import jax.numpy as jnp
from jax import lax
from jax.experimental import pallas as pl
from jax.experimental.pallas import tpu as pltpu
from jax.sharding import PartitionSpec as P

D = 1024
DH = 128
MEM = 512
CMEM = 512
RATE = 3
NEWC = 128
SEQ_LEN = 1024
HALF = SEQ_LEN // 2
HEADS = 4
OLD = RATE * NEWC
MROWS = CMEM + MEM
KM = MROWS + NEWC
QUARTER = D // 4
CHUNK = 256
LIMIT = 60

EPSILON = 1e-05
MASKED = -1e30
LOG2E = 1.4426950408889634
SCALE = DH**-0.5
SCALE2 = SCALE * LOG2E
F32 = jnp.float32
BF = jnp.bfloat16


def nn(a, b):
    return lax.dot_general(a, b, (((1,), (0,)), ((), ())), preferred_element_type=F32)


def nt(a, b):
    return lax.dot_general(a, b, (((1,), (1,)), ((), ())), preferred_element_type=F32)


def tn(a, b):
    return lax.dot_general(a, b, (((0,), (0,)), ((), ())), preferred_element_type=F32)


def swap(x, axis, distance):
    n = lax.axis_size(axis)
    return lax.ppermute(x, axis, [(i, i ^ distance) for i in range(n)])


def add_low(a, b):
    return (a.astype(F32) + b.astype(F32)).astype(BF)


def params(limit_mb, dims=1):
    return pltpu.CompilerParams(
        dimension_semantics=("arbitrary",) * dims, vmem_limit_bytes=limit_mb << 20
    )


ANY = pl.BlockSpec(memory_space=pl.ANY)


def cost(flops):
    return pl.CostEstimate(flops=flops, transcendentals=0, bytes_accessed=flops // 1000)


def shape(dims, kind):
    return jax.ShapeDtypeStruct(dims, kind)


def whole(dims):
    zeros = (0,) * len(dims)
    return pl.BlockSpec(dims, lambda *_: zeros)


def norm_block(pieces, gain_ref):
    values = [p.astype(F32) for p in pieces]
    mean = sum(jnp.sum(v, axis=1, keepdims=True) for v in values) / D
    values = [v - mean for v in values]
    spread = sum(jnp.sum(v * v, axis=1, keepdims=True) for v in values) / D
    factor = lax.rsqrt(spread + EPSILON)
    return [values[k] * factor * gain_ref[:, block_of(k)] for k in range(4)]


def block_of(k):
    return slice(k * QUARTER, (k + 1) * QUARTER)


def tok_norm_kernel(where, p0, p1, p2, p3, gain_ref, low_ref, raw_ref):
    pieces = [p[...] for p in (p0, p1, p2, p3)]
    normed = norm_block(pieces, gain_ref)
    for k in range(4):
        low_ref[:, block_of(k)] = normed[k].astype(BF)
        raw_ref[:, block_of(k)] = pieces[k]


def tok_norm(where, pieces, gain):
    block = 256
    count = SEQ_LEN // block
    piece = pl.BlockSpec((block, QUARTER), lambda i, w: ((i + w[0] * (count // 2)) % count, 0))
    out = pl.BlockSpec((block, D), lambda i, w: (i, 0))
    return pl.pallas_call(
        tok_norm_kernel,
        out_shape=(shape((SEQ_LEN, D), BF), shape((SEQ_LEN, D), BF)),
        grid_spec=pltpu.PrefetchScalarGridSpec(
            num_scalar_prefetch=1,
            grid=(count,),
            in_specs=[piece] * 4 + [whole((1, D))],
            out_specs=[out, out],
        ),
        compiler_params=params(LIMIT),
        name="tok_norm",
    )(where, *pieces, gain)


def mem_norm_kernel(p0, p1, p2, p3, gain_ref, conv_ref, _, low_ref, raw_ref, keep_ref):
    for block in range(MROWS // 256):
        rows = slice(block * 256, block * 256 + 256)
        pieces = [p[rows, :] for p in (p0, p1, p2, p3)]
        normed = norm_block(pieces, gain_ref)
        for k in range(4):
            low_ref[rows, block_of(k)] = normed[k].astype(BF)
            raw_ref[rows, block_of(k)] = pieces[k]
            if block * 256 >= CMEM:
                start = block * 256 - CMEM
                for j in range(2):
                    keep_ref[k * 2 + j, start : start + 256, :] = normed[k][:, j * DH : j * DH + DH]
    for j in range(D // DH):
        lanes = slice(j * DH, j * DH + DH)
        packed = 0.0
        for t in range(RATE):
            picked = keep_ref[j, pl.ds(t, NEWC, stride=RATE), :]
            packed = packed + conv_ref[t : t + 1, lanes] * picked
        low_ref[MROWS:, lanes] = packed.astype(BF)


def mem_norm(pieces, gain, conv, earlier):
    return pl.pallas_call(
        mem_norm_kernel,
        out_shape=(shape((KM, D), BF), shape((MROWS, D), BF)),
        grid=(1,),
        in_specs=[whole((MROWS, QUARTER))] * 4 + [whole((1, D)), whole((RATE, D)), ANY],
        out_specs=[whole((KM, D)), whole((MROWS, D))],
        scratch_shapes=[pltpu.VMEM((D // DH, MEM, DH), F32)],
        compiler_params=params(LIMIT),
        name="mem_norm",
    )(*pieces, gain, conv, earlier)


def join_kernel(*refs):
    parts, (tok_ref, mem_ref, back_ref) = refs[:4], refs[4:]
    cols, _, part, _, span, _ = parts[0].shape
    for head in range(HEADS):
        c, i = head // part, head % part
        for kind in range(5):
            for dp, ref in enumerate(parts):
                low = dp * span
                for k in range(4):
                    value = ref[c, k, i, kind]
                    if kind < 3:
                        row = (head * 3 + kind) * DH + low
                        tok_ref[row : row + span, block_of(k)] = value
                    if 0 < kind < 3:
                        row = (head * 2 + kind - 1) * DH + low
                        mem_ref[row : row + span, block_of(k)] = value
                    if kind > 2:
                        row = ((kind - 3) * HEADS + head) * DH + low
                        back_ref[row : row + span, block_of(k)] = value


def join_weights(parts):
    dims = ((HEADS * 3 * DH, D), (HEADS * 2 * DH, D), (HEADS * 2 * DH, D))
    return pl.pallas_call(
        join_kernel,
        out_shape=tuple(shape(d, BF) for d in dims),
        grid=(1,),
        in_specs=[whole(p.shape) for p in parts],
        out_specs=[whole(d) for d in dims],
        compiler_params=params(LIMIT),
        name="join_weights",
    )(*parts)


def fill_bias(bias_ref, row_ref, col_ref):
    seg_q, pos_q = row_ref[0:1, :], row_ref[1:2, :]

    def memory_chunk(c, carry):
        rows = pl.ds(pl.multiple_of(c * CHUNK, CHUNK), CHUNK)
        bias_ref[rows, :] = jnp.where(col_ref[rows, 2:3] == seg_q, 0.0, MASKED)
        return carry

    def token_chunk(c, carry):
        start = pl.multiple_of(c * CHUNK, CHUNK)
        rows = pl.ds(start, CHUNK)
        same = (col_ref[rows, 0:1] == seg_q) & (col_ref[rows, 1:2] <= pos_q)
        key_id = lax.broadcasted_iota(jnp.int32, (CHUNK, SEQ_LEN), 0) + start
        query_id = lax.broadcasted_iota(jnp.int32, (CHUNK, SEQ_LEN), 1)
        target = pl.ds(pl.multiple_of(MROWS + c * CHUNK, CHUNK), CHUNK)
        bias_ref[target, :] = jnp.where(same | (key_id == query_id), 0.0, MASKED)
        return carry

    lax.fori_loop(0, MROWS // CHUNK, memory_chunk, 0)
    lax.fori_loop(0, SEQ_LEN // CHUNK, token_chunk, 0)


def forward_kernel(tok_ref, mem_ref, row_ref, col_ref, o_ref, log_ref, bias_ref, s_ref, acc_ref):
    @pl.when(pl.program_id(0) == 0)
    def _():
        fill_bias(bias_ref, row_ref, col_ref)

    queries = tok_ref[:, :DH]

    def scores(key_ref, columns, offset):
        def step(c, top):
            rows = pl.ds(pl.multiple_of(c * CHUNK, CHUNK), CHUNK)
            target = pl.ds(pl.multiple_of(offset + c * CHUNK, CHUNK), CHUNK)
            s = nt(key_ref[rows, columns], queries) * SCALE2 + bias_ref[target, :]
            s_ref[target, :] = s
            return jnp.maximum(top, jnp.max(s.reshape(CHUNK // 8, 8, SEQ_LEN), axis=0))

        return step

    top = jnp.full((8, SEQ_LEN), -3.0e38, F32)
    top = lax.fori_loop(0, MROWS // CHUNK, scores(mem_ref, slice(0, DH), 0), top)
    top = lax.fori_loop(0, SEQ_LEN // CHUNK, scores(tok_ref, slice(DH, 2 * DH), MROWS), top)
    top = jnp.max(top, axis=0, keepdims=True)
    acc_ref[...] = jnp.zeros_like(acc_ref)

    def values(value_ref, columns, offset):
        def step(c, total):
            rows = pl.ds(pl.multiple_of(c * CHUNK, CHUNK), CHUNK)
            target = pl.ds(pl.multiple_of(offset + c * CHUNK, CHUNK), CHUNK)
            p = jnp.exp2(s_ref[target, :] - top)
            acc_ref[...] += nn(value_ref[rows, columns].T, p.astype(BF))
            return total + jnp.sum(p.reshape(CHUNK // 8, 8, SEQ_LEN), axis=0)

        return step

    total = jnp.zeros((8, SEQ_LEN), F32)
    total = lax.fori_loop(0, MROWS // CHUNK, values(mem_ref, slice(DH, 2 * DH), 0), total)
    total = lax.fori_loop(
        0, SEQ_LEN // CHUNK, values(tok_ref, slice(2 * DH, 3 * DH), MROWS), total
    )
    total = jnp.sum(total, axis=0, keepdims=True)
    o_ref[...] = (acc_ref[...] / total).T.astype(BF)
    log_ref[...] = (top + jnp.log2(total)).reshape(1, 1, SEQ_LEN)


def attention_forward(tok_p, mem_p, row_attr, col_attr):
    return pl.pallas_call(
        forward_kernel,
        out_shape=(shape((SEQ_LEN, HEADS * DH), BF), shape((HEADS, 1, SEQ_LEN), F32)),
        grid=(HEADS,),
        in_specs=[
            pl.BlockSpec((SEQ_LEN, 3 * DH), lambda h: (0, h)),
            pl.BlockSpec((KM, 2 * DH), lambda h: (0, h)),
            whole(row_attr.shape),
            whole(col_attr.shape),
        ],
        out_specs=[
            pl.BlockSpec((SEQ_LEN, DH), lambda h: (0, h)),
            pl.BlockSpec((1, 1, SEQ_LEN), lambda h: (h, 0, 0)),
        ],
        scratch_shapes=[
            pltpu.VMEM((MROWS + SEQ_LEN, SEQ_LEN), F32),
            pltpu.VMEM((MROWS + SEQ_LEN, SEQ_LEN), F32),
            pltpu.VMEM((DH, SEQ_LEN), F32),
        ],
        compiler_params=params(LIMIT),
        cost_estimate=cost(25_000_000_000),
        name="attention_forward",
    )(tok_p, mem_p, row_attr, col_attr)


def recon_kernel(tok_ref, mem_ref, *refs):
    gq_ref, gm_ref = refs[-2:]
    q = tok_ref[:, :DH]
    old, new = slice(CMEM, CMEM + OLD), slice(MROWS, KM)
    keys, values = slice(0, DH), slice(DH, 2 * DH)

    def softmax_rows(key_rows):
        s = nt(key_rows, q) * SCALE2
        p = jnp.exp2(s - jnp.max(s, axis=0, keepdims=True))
        return p / jnp.sum(p, axis=0, keepdims=True)

    ko, vo, kn, vn = mem_ref[old, keys], mem_ref[old, values], mem_ref[new, keys], mem_ref[new, values]
    po, pn = softmax_rows(ko), softmax_rows(kn)
    po_low, pn_low = po.astype(BF), pn.astype(BF)
    out_o, out_n = nn(vo.T, po_low), nn(vn.T, pn_low)
    gap = (out_o - out_n).astype(BF)
    gap32 = gap.astype(F32)
    do = (po * (nn(vo, gap) - jnp.sum(gap32 * out_o, axis=0, keepdims=True))).astype(BF)
    dn = (pn * (jnp.sum(gap32 * out_n, axis=0, keepdims=True) - nn(vn, gap))).astype(BF)
    gq_ref[...] = ((nn(ko.T, do) + nn(kn.T, dn)) * SCALE).reshape(1, DH, SEQ_LEN)
    gap_t = gap32.T.astype(BF)
    gm_ref[:OLD, keys] = nn(do, q) * SCALE
    gm_ref[:OLD, values] = nn(po_low, gap_t)
    gm_ref[OLD:MEM, :] = jnp.zeros((MEM - OLD, 2 * DH), F32)
    gm_ref[MEM:, keys] = nn(dn, q) * SCALE
    gm_ref[MEM:, values] = -nn(pn_low, gap_t)


def reconstruction(tok_p, mem_p, *earlier):
    return pl.pallas_call(
        recon_kernel,
        out_shape=(
            shape((HEADS, DH, SEQ_LEN), F32),
            shape((MEM + NEWC, HEADS * 2 * DH), F32),
        ),
        grid=(HEADS,),
        in_specs=[
            pl.BlockSpec((SEQ_LEN, 3 * DH), lambda h: (0, h)),
            pl.BlockSpec((KM, 2 * DH), lambda h: (0, h)),
        ]
        + [ANY] * len(earlier),
        out_specs=[
            pl.BlockSpec((1, DH, SEQ_LEN), lambda h: (h, 0, 0)),
            pl.BlockSpec((MEM + NEWC, 2 * DH), lambda h: (0, h)),
        ],
        compiler_params=params(LIMIT),
        cost_estimate=cost(10_000_000_000),
        name="reconstruction",
    )(tok_p, mem_p, *earlier)


def backward_kernel(
    tok_ref, mem_ref, own_ref, got_ref, o_ref, log_ref, rq_ref, rm_ref, row_ref, col_ref,
    *refs,
):
    gt_ref, gm_ref, bias_ref, acc_ref = refs[-4:]

    @pl.when(pl.program_id(0) == 0)
    def _():
        fill_bias(bias_ref, row_ref, col_ref)

    q = tok_ref[:, :DH]
    go = jnp.concatenate([own_ref[...], got_ref[...]], axis=0)
    product = go.astype(F32) * o_ref[...].astype(F32)
    delta = jnp.sum(product.T, axis=0, keepdims=True)
    log_total = log_ref[...].reshape(1, SEQ_LEN)
    acc_ref[...] = rq_ref[...].reshape(DH, SEQ_LEN)

    def piece(k, v, offset):
        s = nt(k, q) * SCALE2 + bias_ref[offset, :]
        p = jnp.exp2(s - log_total)
        d = (p * (nt(v, go) - delta)).astype(BF)
        acc_ref[...] += nn(k.T, d) * SCALE
        return nn(d, q) * SCALE, nn(p.astype(BF), go)

    def memory_chunk(c, carry):
        rows = pl.ds(pl.multiple_of(c * CHUNK, CHUNK), CHUNK)
        gk, gv = piece(mem_ref[rows, :DH], mem_ref[rows, DH:], rows)
        gm_ref[rows, :DH] = gk.astype(BF)
        gm_ref[rows, DH:] = gv.astype(BF)
        return carry

    def shared_chunk(c, carry):
        rows = pl.ds(pl.multiple_of(c * CHUNK, CHUNK), CHUNK)
        extra = pl.ds(pl.multiple_of(c * CHUNK - CMEM, CHUNK), CHUNK)
        gk, gv = piece(mem_ref[rows, :DH], mem_ref[rows, DH:], rows)
        gm_ref[rows, :DH] = (gk + rm_ref[extra, :DH]).astype(BF)
        gm_ref[rows, DH:] = (gv + rm_ref[extra, DH:]).astype(BF)
        return carry

    def token_chunk(c, carry):
        rows = pl.ds(pl.multiple_of(c * CHUNK, CHUNK), CHUNK)
        target = pl.ds(pl.multiple_of(MROWS + c * CHUNK, CHUNK), CHUNK)
        gk, gv = piece(tok_ref[rows, DH : 2 * DH], tok_ref[rows, 2 * DH :], target)
        gt_ref[rows, DH : 2 * DH] = gk.astype(BF)
        gt_ref[rows, 2 * DH :] = gv.astype(BF)
        return carry

    lax.fori_loop(0, CMEM // CHUNK, memory_chunk, 0)
    lax.fori_loop(CMEM // CHUNK, MROWS // CHUNK, shared_chunk, 0)
    lax.fori_loop(0, SEQ_LEN // CHUNK, token_chunk, 0)
    gm_ref[MROWS:, :] = rm_ref[MEM:, :].astype(BF)
    gt_ref[:, :DH] = acc_ref[...].T.astype(BF)


def attention_backward(
    tok_p, mem_p, go_own, go_got, o, logs, rec_q, rec_m, row_attr, col_attr, *earlier
):
    half = pl.BlockSpec((HALF, DH), lambda h: (0, h))
    return pl.pallas_call(
        backward_kernel,
        out_shape=(
            shape((SEQ_LEN, HEADS * 3 * DH), BF),
            shape((KM, HEADS * 2 * DH), BF),
        ),
        grid=(HEADS,),
        in_specs=[
            pl.BlockSpec((SEQ_LEN, 3 * DH), lambda h: (0, h)),
            pl.BlockSpec((KM, 2 * DH), lambda h: (0, h)),
            half,
            half,
            pl.BlockSpec((SEQ_LEN, DH), lambda h: (0, h)),
            pl.BlockSpec((1, 1, SEQ_LEN), lambda h: (h, 0, 0)),
            pl.BlockSpec((1, DH, SEQ_LEN), lambda h: (h, 0, 0)),
            pl.BlockSpec((MEM + NEWC, 2 * DH), lambda h: (0, h)),
            whole(row_attr.shape),
            whole(col_attr.shape),
        ]
        + [ANY] * len(earlier),
        out_specs=[
            pl.BlockSpec((SEQ_LEN, 3 * DH), lambda h: (0, h)),
            pl.BlockSpec((KM, 2 * DH), lambda h: (0, h)),
        ],
        scratch_shapes=[
            pltpu.VMEM((MROWS + SEQ_LEN, SEQ_LEN), F32),
            pltpu.VMEM((DH, SEQ_LEN), F32),
        ],
        compiler_params=params(LIMIT),
        cost_estimate=cost(35_000_000_000),
        name="attention_backward",
    )(tok_p, mem_p, go_own, go_got, o, logs, rec_q, rec_m, row_attr, col_attr, *earlier)


def center_rows(rows):
    centered = rows - jnp.mean(rows, axis=1, keepdims=True)
    factor = lax.rsqrt(jnp.mean(centered * centered, axis=1, keepdims=True) + EPSILON)
    return centered * factor, factor


def mid_kernel(raw_ref, own_ref, got_ref, w_ref, gain_ref, _, mid_ref, x2_ref):
    width = own_ref.shape[1]
    mid = raw_ref[...].astype(F32) + (
        nn(own_ref[...], w_ref[:width, :]) + nn(got_ref[...], w_ref[width:, :])
    )
    unit, _ = center_rows(mid)
    mid_ref[...] = mid
    x2_ref[...] = (unit * gain_ref[...]).astype(BF)


def residual_mid(raw, o, o_got, w_out, gain, earlier):
    block = 256
    rows = lambda width: pl.BlockSpec((block, width), lambda i: (i, 0))
    return pl.pallas_call(
        mid_kernel,
        out_shape=(shape((HALF, D), F32), shape((HALF, D), BF)),
        grid=(HALF // block,),
        in_specs=[rows(D), rows(HEADS * DH), rows(HEADS * DH), whole((D, D)), whole((1, D)), ANY],
        out_specs=[rows(D), rows(D)],
        compiler_params=params(LIMIT),
        cost_estimate=cost(4 * HALF * D * D),
        name="residual_mid",
    )(raw, o, o_got, w_out, gain, earlier)


TILE = 256


def ffn_kernel(*refs):
    x_own, x_got, c_own, c_got = refs[:4]
    plain, far_up, far_down = refs[4:7], refs[7], refs[8]
    out_keep, out_send, gx_keep, gx_send = refs[9:13]
    grads = refs[13:18]
    x_ref, xt_ref, c_ref, ct_ref, out_ref, gx_ref, up_ref, down_ref = refs[18:]
    step, last = pl.program_id(0), pl.num_programs(0) - 1
    block = step // (pl.num_programs(0) // 4)

    @pl.when(step == 0)
    def _():
        out_ref[...] = jnp.zeros_like(out_ref)
        gx_ref[...] = jnp.zeros_like(gx_ref)
        for (own, got), full, turned in (
            ((x_own, x_got), x_ref, xt_ref),
            ((c_own, c_got), c_ref, ct_ref),
        ):
            for j, half in enumerate((own, got)):
                full[j * HALF : (j + 1) * HALF, :] = half[...]
                for i in range(0, HALF, 256):
                    turned[:, j * HALF + i : j * HALF + i + 256] = half[i : i + 256, :].T

    for k, ref in enumerate(plain):
        @pl.when(block == k)
        def _():
            up_ref[...] = ref[0].reshape(D, TILE)
            down_ref[...] = ref[1].reshape(D, TILE)

    @pl.when(block == 3)
    def _():
        up_ref[...] = far_up[...].reshape(D, TILE)
        down_ref[...] = far_down[...].reshape(D, TILE)

    w_up, w_down = up_ref[...], down_ref[...]
    v = nn(x_ref[...], w_up)
    g_act = nn(c_ref[...], w_down)
    c0, c1 = 0.7978845608028654, 0.044715
    v2 = v * v
    t = jnp.tanh(c0 * v * (1.0 + c1 * v2))
    half = 0.5 * (1.0 + t)
    act = (v * half).astype(BF)
    slope = half + (0.5 * c0) * v * (1.0 - t * t) * (1.0 + (3.0 * c1) * v2)
    g_pre = (g_act * slope).astype(BF)
    out_ref[...] += nt(act, w_down)
    gx_ref[...] += nt(g_pre, w_up)
    grad_up = nn(xt_ref[...], g_pre).astype(BF)
    grad_down = nn(ct_ref[...], act).astype(BF)

    for k in range(3):
        @pl.when(block == k)
        def _():
            for j, row in enumerate((0, 2, 1, 3)):
                grads[k][0, j] = grad_up[block_of(row), :]
                grads[k][1, j] = grad_down[block_of(row), :]

    @pl.when(block == 3)
    def _():
        for j, row in enumerate((0, 2, 1, 3)):
            grads[3][j] = grad_up[block_of(row), :]
            grads[4][j] = grad_down[block_of(row), :]

    @pl.when(step == last)
    def _():
        for total, keep, send in ((out_ref, out_keep, out_send), (gx_ref, gx_keep, gx_send)):
            keep[...] = total[:HALF, :]
            send[...] = total[HALF:, :].astype(BF)


def feed_forward(x2, x2_got, cot, cot_got, plain, far_up, far_down):
    width = far_up.shape[-1]
    tiles = width // TILE

    def tile(k, step):
        return jnp.clip(step - k * tiles, 0, tiles - 1)

    def pair(k):
        return pl.BlockSpec((2, 4, QUARTER, TILE), lambda i: (0, 0, 0, tile(k, i)))

    far = pl.BlockSpec((4, QUARTER, TILE), lambda i: (0, 0, tile(3, i)))
    blocks = [pair(0), pair(1), pair(2), far, far]
    once = pl.BlockSpec((HALF, D), lambda i: (0, 0), pipeline_mode=pl.Buffered(1))
    rows = whole((HALF, D))
    full, turned = pltpu.VMEM((SEQ_LEN, D), BF), pltpu.VMEM((D, SEQ_LEN), BF)
    total = pltpu.VMEM((SEQ_LEN, D), F32)
    return pl.pallas_call(
        ffn_kernel,
        out_shape=(
            shape((HALF, D), F32), shape((HALF, D), BF),
            shape((HALF, D), F32), shape((HALF, D), BF),
        )
        + (shape(plain[0].shape, BF),) * 3
        + (shape(far_up.shape, BF),) * 2,
        grid=(4 * tiles,),
        in_specs=[once] * 4 + blocks,
        out_specs=[rows] * 4 + blocks,
        scratch_shapes=[full, turned, full, turned, total, total] + [pltpu.VMEM((D, TILE), BF)] * 2,
        compiler_params=params(LIMIT),
        cost_estimate=cost(12 * SEQ_LEN * D * 4 * width),
        name="feed_forward",
    )(x2, x2_got, cot, cot_got, *plain, far_up, far_down)


def out_sum_kernel(mid_ref, keep_ref, got_ref, *refs):
    total = mid_ref[...] + (keep_ref[...] + got_ref[...].astype(F32))
    for k, ref in enumerate(refs[-4:]):
        ref[...] = total[:, block_of(k)].astype(BF)


def out_sum(mid, keep, got, *earlier):
    block = 256
    rows = lambda width: pl.BlockSpec((block, width), lambda i: (i, 0))
    return pl.pallas_call(
        out_sum_kernel,
        out_shape=(shape((HALF, QUARTER), BF),) * 4,
        grid=(HALF // block,),
        in_specs=[rows(D)] * 3 + [ANY] * len(earlier),
        out_specs=[rows(QUARTER)] * 4,
        compiler_params=params(LIMIT),
        name="out_sum",
    )(mid, keep, got, *earlier)


def mid_back_kernel(gx_ref, got_ref, mid_ref, cot_ref, gain_ref, w_ref, gm_ref, ga_ref, keep_ref, send_ref, gn_ref):
    @pl.when(pl.program_id(0) == 0)
    def _():
        gn_ref[...] = jnp.zeros_like(gn_ref)

    unit, factor = center_rows(mid_ref[...])
    gx = gx_ref[...] + got_ref[...].astype(F32)
    gn_ref[...] += jnp.sum(gx * unit, axis=0, keepdims=True)
    s = gx * gain_ref[...]
    g_mid = cot_ref[...].astype(F32) + factor * (
        s - jnp.mean(s, axis=1, keepdims=True) - unit * jnp.mean(s * unit, axis=1, keepdims=True)
    )
    gm_ref[...] = g_mid
    low = g_mid.astype(BF)
    ga_ref[...] = low
    width = keep_ref.shape[1]
    send_ref[...] = nt(low, w_ref[width:, :]).astype(BF)
    keep_ref[...] = nt(low, w_ref[:width, :]).astype(BF)


def mid_back(gx, gx_got, mid, cot, gain, w_out):
    block = 256
    rows = lambda width: pl.BlockSpec((block, width), lambda i: (i, 0))
    half = shape((HALF, HEADS * DH), BF)
    return pl.pallas_call(
        mid_back_kernel,
        out_shape=(shape((HALF, D), F32), shape((HALF, D), BF), half, half, shape((1, D), F32)),
        grid=(HALF // block,),
        in_specs=[rows(D)] * 4 + [whole((1, D)), whole((D, D))],
        out_specs=[rows(D), rows(D), rows(HEADS * DH), rows(HEADS * DH), whole((1, D))],
        compiler_params=params(LIMIT),
        cost_estimate=cost(2 * HALF * D * D),
        name="mid_back",
    )(gx, gx_got, mid, cot, gain, w_out)


def tok_grad_kernel(g_ref, w_ref, raw_ref, *refs):
    keep_ref, send_ref, gn_ref = refs[-3:]
    step = pl.program_id(0)

    @pl.when(step == 0)
    def _():
        gn_ref[...] = jnp.zeros_like(gn_ref)

    gx = nn(g_ref[...], w_ref[...])
    unit, _ = center_rows(raw_ref[...].astype(F32))
    gn_ref[...] += jnp.sum(gx * unit, axis=0, keepdims=True)

    @pl.when(step < pl.num_programs(0) // 2)
    def _():
        send_ref[...] = gx.astype(BF)

    @pl.when(step >= pl.num_programs(0) // 2)
    def _():
        keep_ref[...] = gx


def tok_grad(g_tok, w_tok, raw, *earlier):
    block = 256
    steps, half = SEQ_LEN // block, HALF // block
    rows = lambda width: pl.BlockSpec((block, width), lambda i: ((i + half) % steps, 0))
    return pl.pallas_call(
        tok_grad_kernel,
        out_shape=(shape((HALF, D), F32), shape((HALF, D), BF), shape((1, D), F32)),
        grid=(steps,),
        in_specs=[rows(HEADS * 3 * DH), whole((HEADS * 3 * DH, D)), rows(D)]
        + [ANY] * len(earlier),
        out_specs=[
            pl.BlockSpec((block, D), lambda i: (jnp.maximum(i - half, 0), 0)),
            pl.BlockSpec((block, D), lambda i: (jnp.minimum(i, half - 1), 0)),
            whole((1, D)),
        ],
        compiler_params=params(LIMIT),
        name="tok_grad",
    )(g_tok, w_tok, raw, *earlier)


def input_grad_kernel(keep_ref, got_ref, raw_ref, gm_ref, gain_ref, *refs):
    unit, factor = center_rows(raw_ref[...].astype(F32))
    got = [got_ref[:, block_of(k ^ 1)].astype(F32) for k in range(4)]
    s = (keep_ref[...] + jnp.concatenate(got, axis=1)) * gain_ref[...]
    g = gm_ref[...] + factor * (
        s - jnp.mean(s, axis=1, keepdims=True) - unit * jnp.mean(s * unit, axis=1, keepdims=True)
    )
    for k, ref in enumerate(refs[-4:]):
        ref[...] = g[:, block_of(k)].astype(BF)


def input_grad(keep, got, raw, g_mid, gain, *earlier):
    block = 256
    rows = pl.BlockSpec((block, D), lambda i: (i, 0))
    return pl.pallas_call(
        input_grad_kernel,
        out_shape=(shape((HALF, QUARTER), BF),) * 4,
        grid=(HALF // block,),
        in_specs=[rows, rows, rows, rows, whole((1, D))] + [ANY] * len(earlier),
        out_specs=[pl.BlockSpec((block, QUARTER), lambda i: (i, 0))] * 4,
        compiler_params=params(LIMIT),
        name="input_grad",
    )(keep, got, raw, g_mid, gain, *earlier)


def mem_grad_kernel(g_ref, w_ref, raw_ref, gain_ref, conv_ref, *refs):
    gn_ref, gc_ref, unit_ref = refs[-3:]
    total = jnp.zeros((1, D), F32)
    for block in range(MROWS // 256):
        rows = slice(block * 256, block * 256 + 256)
        unit, _ = center_rows(raw_ref[rows, :].astype(F32))
        total = total + jnp.sum(nn(g_ref[rows, :], w_ref[...]) * unit, axis=0, keepdims=True)
        if block * 256 >= CMEM:
            start = block * 256 - CMEM
            for j in range(D // DH):
                unit_ref[j, start : start + 256, :] = unit[:, j * DH : j * DH + DH]
    gn_ref[...] = total
    packed = nn(g_ref[MROWS:, :], w_ref[...])
    for j in range(D // DH):
        lanes = slice(j * DH, j * DH + DH)
        for t in range(RATE):
            picked = unit_ref[j, pl.ds(t, NEWC, stride=RATE), :]
            term = jnp.sum(packed[:, lanes] * picked, axis=0, keepdims=True)
            gc_ref[t : t + 1, lanes] = term * gain_ref[:, lanes]
            gn_ref[:, lanes] += conv_ref[t : t + 1, lanes] * term


def mem_grad(g_mem, w_mem, raw, gain, conv, *earlier):
    return pl.pallas_call(
        mem_grad_kernel,
        out_shape=(shape((1, D), F32), shape((RATE, D), F32)),
        grid=(1,),
        in_specs=[
            whole((KM, D)), whole((D, D)), whole((MROWS, D)), whole((1, D)), whole((RATE, D)),
        ]
        + [ANY] * len(earlier),
        out_specs=[whole((1, D)), whole((RATE, D))],
        scratch_shapes=[pltpu.VMEM((D // DH, MEM, DH), F32)],
        compiler_params=params(LIMIT),
        name="mem_grad",
    )(g_mem, w_mem, raw, gain, conv, *earlier)


def store_spans(grad, index, keep_ref, send_ref):
    span = DH // 4
    for x in range(2):
        for core, ref in enumerate((keep_ref, send_ref)):
            row = (2 * x + core) * span
            ref[(x,) + index] = grad[row : row + span, :].astype(BF)


def qkv_grad_kernel(gt_ref, xt_ref, gm_ref, xm_ref, *refs):
    for kind in range(3):
        grad = nn(gt_ref[:, kind * DH : (kind + 1) * DH].T, xt_ref[...])
        if kind > 0:
            grad = grad + nn(gm_ref[:, (kind - 1) * DH : kind * DH].T, xm_ref[...])
        store_spans(grad, (0, kind), *refs[-2:])


def qkv_grad(g_tok, x_tok, g_mem, x_mem, *earlier):
    out = shape((2, HEADS, 3, DH // 4, D), BF)
    block = pl.BlockSpec((2, 1, 3, DH // 4, D), lambda h: (0, h, 0, 0, 0))
    return pl.pallas_call(
        qkv_grad_kernel,
        out_shape=(out, out),
        grid=(HEADS,),
        in_specs=[
            pl.BlockSpec((SEQ_LEN, 3 * DH), lambda h: (0, h)),
            whole((SEQ_LEN, D)),
            pl.BlockSpec((KM, 2 * DH), lambda h: (0, h)),
            whole((KM, D)),
        ]
        + [ANY] * len(earlier),
        out_specs=[block, block],
        compiler_params=params(LIMIT),
        name="qkv_grad",
    )(g_tok, x_tok, g_mem, x_mem, *earlier)


def out_grad_kernel(own_ref, got_ref, g_ref, keep_ref, send_ref):
    for z, ref in enumerate((own_ref, got_ref)):
        store_spans(nn(ref[...].T, g_ref[...]), (0, z), keep_ref, send_ref)


def out_grad(o, o_got, g_attn):
    out = shape((2, HEADS, 2, DH // 4, D), BF)
    block = pl.BlockSpec((2, 1, 2, DH // 4, D), lambda h: (0, h, 0, 0, 0))
    half = pl.BlockSpec((HALF, DH), lambda h: (0, h))
    return pl.pallas_call(
        out_grad_kernel,
        out_shape=(out, out),
        grid=(HEADS,),
        in_specs=[half, half, whole((HALF, D))],
        out_specs=[block, block],
        compiler_params=params(LIMIT),
        name="out_grad",
    )(o, o_got, g_attn)


def merge_kernel(count, lanes, *refs):
    outs = refs[-2:]
    for j, out in enumerate(outs):
        if lanes:
            half = slice(j * out.shape[-1], (j + 1) * out.shape[-1])
            parts = [ref[:, half] for ref in refs[:count]]
        else:
            parts = [ref[...] for ref in refs[j * count : (j + 1) * count]]
        out[...] = sum(part.astype(F32) for part in parts).astype(BF)


def merge(arrays, *earlier, lanes=False, axis=0, work=0):
    dims = arrays[0].shape
    count = len(arrays)
    if lanes:
        out = dims[:-1] + (dims[-1] // 2,)
        flat = [a.reshape(-1, dims[-1]) for a in arrays]
        rows = flat[0].shape[0]
        grid, out_dims = (1,), (rows, out[-1])
        ins, blocks = [whole(flat[0].shape)] * count, [whole(out_dims)] * 2
    else:
        out = dims[:axis] + (dims[axis] // 2,) + dims[axis + 1 :]
        outer = dims[0] if axis else 1
        flat = [a.reshape(2 * outer, -1, dims[-1]) for a in arrays]
        block = (1,) + flat[0].shape[1:]
        grid, out_dims = (outer,), (outer,) + block[1:]
        low = pl.BlockSpec(block, lambda i: (2 * i, 0, 0))
        high = pl.BlockSpec(block, lambda i: (2 * i + 1, 0, 0))
        same = pl.BlockSpec(block, lambda i: (i, 0, 0))
        ins, blocks, flat = [low] * count + [high] * count, [same] * 2, flat * 2
    pair = pl.pallas_call(
        functools.partial(merge_kernel, count, lanes),
        out_shape=(shape(out_dims, BF),) * 2,
        grid=grid,
        in_specs=ins + [ANY] * len(earlier),
        out_specs=blocks,
        compiler_params=params(LIMIT),
        cost_estimate=cost(work) if work else None,
        name="merge",
    )(*flat, *earlier)
    return [g.reshape(out) for g in pair]


def pick(g, index, axis=0):
    return lax.dynamic_index_in_dim(g, index, axis, keepdims=False)


def after(value, *earlier):
    return pl.pallas_call(
        lambda *refs: None,
        out_shape=shape(value.shape, value.dtype),
        in_specs=[ANY] * (1 + len(earlier)),
        out_specs=ANY,
        input_output_aliases={0: 0},
        name="after",
    )(value, *earlier)


def doubled(g, axis, distance):
    return jnp.concatenate([g, swap(g, axis, distance)], axis=0)


def both(parts, axis, distance):
    return parts + [swap(p, axis, distance) for p in parts]


def doubled_cols(g, n_col, first=1):
    while first < n_col:
        g = doubled(g, "col", first)
        first *= 2
    return g


def halve_col(g, last=1):
    while g.shape[0] > 1:
        n = g.shape[0] // 2
        g = add_low(g[:n], swap(g[n:], "col", n * last))
    return g[0]


def halve_row(g):
    g = add_low(g[:2], swap(g[2:], "row", 2))
    return g[0].astype(F32) + swap(g[1], "row", 1).astype(F32)


def per_device(
    hidden, memory, compressed, seg_ids, positions, keep_mask, mem_seg, cotangent,
    w_qkv, w_out, w_up, w_down, norm_attn, norm_ffn, conv_w,
):
    n_col = lax.axis_size("col")
    heads_part = w_qkv.shape[2]
    part = max(heads_part // 2, 1)
    row, col = lax.axis_index("row"), lax.axis_index("col")
    z_high, z_low = row // 2, row % 2
    low_first = z_low == 0
    where = z_low.reshape(1).astype(jnp.int32)
    span = DH // 4

    def by_low(pair):
        return jnp.where(low_first, pair, jnp.flip(pair, axis=0))

    tokens = hidden.reshape(2, SEQ_LEN, QUARTER)
    tok_mine, tok_other = pick(tokens, z_high), pick(tokens, 1 - z_high)
    tok_far, tok_near = swap(tok_other, "row", 2), swap(tok_mine, "row", 1)
    tok_pieces = [tok_mine, tok_near, tok_far, swap(tok_far, "row", 1)]

    qkv = w_qkv.astype(BF).transpose(2, 1, 3, 0)
    outs = w_out.astype(BF)
    if heads_part % 2 == 0:
        qkv = by_low(qkv.reshape(2, part, 3, span, QUARTER))
        outs = by_low(outs.reshape(2, part, 1, span, QUARTER))
        near = jnp.concatenate([qkv[0], outs[0], outs[1]], axis=1)
        far = jnp.concatenate([qkv[1], outs[1], outs[0]], axis=1)
        heads = jnp.stack(
            [near, swap(far, "row", 1), swap(near, "row", 2), swap(far, "row", 3)]
        )
        heads = doubled_cols(after(heads[None], tok_near), n_col)
    else:
        qkv = jnp.stack([qkv] + [swap(qkv, "row", k) for k in (1, 2, 3)])
        outs = jnp.stack([outs] + [swap(outs, "row", k) for k in (1, 2, 3)])
        qkv = doubled_cols(jnp.where(low_first, qkv, swap(qkv, "col", 1))[None], n_col, 2)
        outs = doubled_cols(outs[None], n_col, 2)
        outs = by_low(jnp.stack([outs, swap(outs, "col", 1)]))
        heads = jnp.concatenate([qkv, jnp.moveaxis(outs, 0, 3)], axis=3)
    own = after(jnp.stack([w_up.astype(BF), w_down.astype(BF).T]), tok_far, tok_near)
    w_far = swap(own, "row", 2)
    heads = both([after(heads, w_far, tok_pieces[3])], "dp", 2)
    own = after(own, w_far, tok_pieces[3])
    w_near = swap(own, "row", 1)
    w_both = swap(w_far, "row", 1)
    small = jnp.concatenate(
        [norm_attn, norm_ffn, conv_w.reshape(-1)]
        + [a.astype(F32) for a in (seg_ids, positions, keep_mask, mem_seg)]
    )
    small = after(small, tok_near)
    shared = jnp.stack([small, swap(small, "row", 2)])
    shared = jnp.stack([shared, swap(shared, "row", 1)], axis=1).reshape(4, -1)
    gains = shared[:, : 5 * QUARTER].reshape(4, 5, QUARTER).transpose(1, 0, 2).reshape(5, D)
    gain1, gain2, conv = gains[0:1], gains[1:2], gains[2:5]
    spans = seg_ids.shape[0] // SEQ_LEN
    sequence = 2 * col + z_high
    ids = pick(shared, row ^ (sequence // spans))[5 * QUARTER :]
    ids = pick(ids.reshape(4, spans, SEQ_LEN), sequence % spans, 1)
    rolled = jnp.concatenate([ids[:3, HALF:], ids[:3, :HALF]], axis=1)
    seg, pos, keep = jnp.where(low_first, ids[:3], rolled)
    row_attr = jnp.stack([seg, pos])
    col_attr = jnp.stack([jnp.where(keep == 1, seg, -2.0), pos, ids[3]], axis=1)

    memories = jnp.concatenate(
        [compressed.reshape(2, CMEM, QUARTER), memory.reshape(2, MEM, QUARTER)], axis=1
    )
    mem_other = after(pick(memories, 1 - z_high), w_far, tok_pieces[3])
    mem_far = swap(mem_other, "row", 2)
    heads = both([after(h, mem_far, w_near, w_both) for h in heads], "dp", 1)
    w_tok, w_mem, w_back = join_weights([heads[0], heads[2], heads[1], heads[3]])
    own = jnp.stack([own, after(w_near, mem_far, heads[2], heads[3]), w_far, w_both], axis=1)
    half_col = n_col // 2
    distance = 1
    while distance < half_col:
        own = jnp.concatenate([own, swap(own, "col", distance)], axis=3)
        distance *= 2
    own_y, own_x = swap(own, "col", half_col), swap(own, "dp", 2)
    far_up, far_down = swap(own_x[0], "col", half_col), swap(own_y[1], "dp", 2)

    mem_mine = after(pick(memories, z_high), mem_far, w_near)
    mem_near = swap(mem_mine, "row", 1)
    mem_pieces = [mem_mine, mem_near, mem_far, swap(mem_far, "row", 1)]

    x_tok, raw_tok = tok_norm(where, tok_pieces, after(gain1, heads[2]))
    tok_p = nt(x_tok, w_tok).astype(BF)
    x_mem, raw_mem = mem_norm(mem_pieces, gain1, conv, tok_p)
    mem_p = nt(x_mem, w_mem).astype(BF)
    cots = cotangent.reshape(4, HALF, QUARTER)
    cots = [after(pick(cots, row ^ k), mem_p, tok_p) for k in range(4)]
    cot = jnp.concatenate([cots[0]] + [swap(cots[k], "row", k) for k in (1, 2, 3)], axis=1)
    cot_got = swap(cot, "dp", 1)
    o, logs = attention_forward(tok_p, mem_p, row_attr, col_attr)
    o_got = swap(o[HALF:], "row", 1)
    rec_q, rec_m = reconstruction(tok_p, mem_p, cot, own_x, own_y)
    mid, x2 = residual_mid(raw_tok, o, o_got, w_back, gain2, rec_m)

    x2_got = swap(x2, "dp", 1)
    out_keep, out_send, gx_keep, gx_send, *grads = feed_forward(
        x2, x2_got, cot, cot_got, (own, own_y, own_x), far_up, far_down
    )
    gx_got = swap(gx_send, "dp", 1)
    g_mid, g_attn, go_keep, go_send, gain2_sum = mid_back(
        gx_keep, gx_got, mid, cot, gain2, w_back
    )
    go_got = swap(go_send, "row", 1)

    own, own_y, own_x, far_up, far_down = grads
    far_up = after(swap(far_up, "col", half_col), go_got)
    far_down = after(swap(far_down, "dp", 2), go_got)
    sum_x = own_x.at[0].set(add_low(own_x[0], far_up))
    sum_y = own_y.at[1].set(add_low(own_y[1], far_down))
    got_x, got_y = swap(sum_x, "dp", 2), swap(sum_y, "col", half_col)

    def to_owners(blocks):
        return [blocks[0]] + [swap(blocks[k], "row", k) for k in (1, 2, 3)]

    def in_order(blocks):
        blocks = [jnp.where(low_first, blocks[k], blocks[k ^ 1]) for k in range(4)]
        blocks = [jnp.where(z_high == 0, blocks[k], blocks[k ^ 2]) for k in range(4)]
        return jnp.concatenate(blocks, axis=0)

    out_got = swap(out_send, "dp", 1)
    g_out = out_grad(o, o_got, g_attn)
    outs = out_sum(mid, out_keep, out_got, g_out[1])
    outs = to_owners([outs[0]] + [after(piece, go_got) for piece in outs[1:]])

    g_tok, g_mem = attention_backward(
        tok_p, mem_p, go_keep, go_got, o, logs, rec_q, rec_m, row_attr, col_attr,
        sum_x, sum_y, outs[0],
    )
    gx, gx_send, gain1_tok = tok_grad(g_tok, w_tok, raw_tok, *outs[1:])
    gx_got = swap(gx_send, "row", 1)
    distance = half_col
    if distance > 1:
        total = (own.astype(F32) + got_x.astype(F32) + got_y.astype(F32)).astype(BF)
        while distance > 1:
            distance //= 2
            n = total.shape[3] // 2
            total = add_low(total[..., :n], swap(total[..., n:], "col", distance))
        even, odd = total[:, :2], total[:, 2:]
    else:
        even, odd = merge([own, got_x, got_y], gx_send, axis=1)

    def halves(g):
        return g.reshape((n_col, part) + g.shape[1:])

    g_qkv = qkv_grad(g_tok, x_tok, g_mem, x_mem, odd)
    g_out, out_send = merge([g_out[0], swap(g_out[1], "dp", 1)], g_qkv[1])
    out_got = swap(out_send, "dp", 2)
    gain1_mem, conv_sum = mem_grad(g_mem, w_mem, raw_mem, gain1, conv, out_send)
    d_rows = input_grad(gx, gx_got, raw_tok, g_mid, gain1, gain1_mem)
    d_input = to_owners(d_rows)
    if heads_part % 2 == 0:
        g_out, out_send = merge([halves(g_out[0]), halves(out_got[0])], d_rows[0])
    even, even_send = merge([even, swap(odd, "row", 1)], out_send, axis=1, work=20_000_000_000)
    even_got = swap(even_send[:, 0], "row", 2)
    g_qkv, qkv_send = merge([g_qkv[0], swap(g_qkv[1], "dp", 1)], even_send)
    qkv_got = swap(qkv_send, "dp", 2)
    if heads_part % 2 == 0:
        def over_row(g, got, first, second):
            g, send = merge([g, got], first, lanes=True)
            g, last = merge([g, swap(send, "row", 2)], second, lanes=True)
            return g, swap(last, "row", 1), send

        out_pair = over_row(g_out[0], swap(out_send[0], "col", 1), qkv_send, *d_input[3:])
        g_qkv, qkv_send = merge(
            [halves(g_qkv[0]), halves(qkv_got[0])], out_pair[2], *d_input[1:]
        )
        g_qkv, got, last = over_row(
            g_qkv[0], swap(qkv_send[0], "col", 1), out_pair[0], out_pair[0]
        )
        grad_qkv = by_low(jnp.stack([g_qkv, got])).astype(F32)
        grad_qkv = grad_qkv.reshape(heads_part, 3, span, QUARTER)
        g_out, got, _ = out_pair
        g_out, got = jnp.swapaxes(g_out, 0, 1), jnp.swapaxes(got, 0, 1)
        grad_out = by_low(g_out.astype(F32) + jnp.flip(got, axis=0).astype(F32))
        grad_out = grad_out.reshape(heads_part, span, QUARTER)
    else:
        g_out, g_qkv = add_low(g_out[0], out_got[0]), add_low(g_qkv[0], qkv_got[0])
        g_qkv = halve_col(g_qkv, 2)
        qkv_send = g_qkv
        grad_qkv, grad_out = reduce_heads(g_qkv, g_out, by_low, low_first)
        last = d_rows[0]
    vectors = jnp.concatenate([gain1_tok + gain1_mem, gain2_sum, conv_sum], axis=0)
    vectors = after(vectors, qkv_send)
    vectors = vectors.reshape(5, 4, QUARTER).transpose(1, 0, 2)
    for distance in (1, 2):
        vectors = vectors + swap(vectors, "dp", distance)
    distance = 1
    while distance < n_col:
        vectors = vectors + swap(vectors, "col", distance)
        distance *= 2
    vectors = after(vectors, last, even_got)
    vectors = vectors[:2] + swap(vectors[2:], "row", 2)
    vectors = vectors[0] + swap(vectors[1], "row", 1)
    grad_qkv = grad_qkv.transpose(3, 1, 0, 2)
    grads = even[:, 0].astype(F32) + even_got.astype(F32)
    d_input, out = in_order(d_input), in_order(outs)
    return (
        out, d_input, grad_qkv, grad_out, grads[0], grads[1].T, vectors[0], vectors[1], vectors[2:]
    )


def reduce_heads(g_qkv, g_out, by_low, low_first):
    span = DH // 4
    zeros = jnp.zeros_like(g_qkv)
    g_qkv = add_low(
        jnp.where(low_first, g_qkv, zeros), swap(jnp.where(low_first, zeros, g_qkv), "col", 1)
    )
    g_out = by_low(jnp.swapaxes(g_out, 0, 1))
    g_out = halve_col(add_low(g_out[0], swap(g_out[1], "col", 1)), 2)
    g_qkv = halve_row(jnp.moveaxis(g_qkv.reshape(3, span, 4, QUARTER), 2, 0))[None]
    g_out = halve_row(jnp.moveaxis(g_out.reshape(span, 4, QUARTER), 1, 0))[None]
    return g_qkv, g_out


def solution(mesh):
    tokens, features = ("dp", "col"), "row"
    placed = (
        P(tokens, features),
        P(tokens, features),
        P(tokens, features),
        P(("dp", "row")),
        P(("dp", "row")),
        P(("dp", "row")),
        P(("dp", "row")),
        P(tokens, features),
        P("row", None, "col", "dp"),
        P("col", "dp", "row"),
        P("row", tokens),
        P(tokens, "row"),
        P("row"),
        P("row"),
        P(None, "row"),
    )
    return jax.shard_map(
        per_device,
        mesh=mesh,
        in_specs=placed,
        out_specs=(
            P(tokens, features),
            P(tokens, features),
            P("row", None, "col", "dp"),
            P("col", "dp", "row"),
            P("row", tokens),
            P(tokens, "row"),
            P("row"),
            P("row"),
            P(None, "row"),
        ),
        check_vma=False,
    )
```

```python
import functools

import jax
import jax.numpy as jnp
from jax import lax
from jax.experimental import pallas as pl
from jax.experimental.pallas import tpu as pltpu
from jax.sharding import PartitionSpec as P

D = 1024
DH = 128
MEM = 512
CMEM = 512
RATE = 3
NEWC = 128
SEQ_LEN = 1024
HALF = SEQ_LEN // 2
HEADS = 4
OLD = RATE * NEWC
MROWS = CMEM + MEM
KM = MROWS + NEWC
QUARTER = D // 4
CHUNK = 256
LIMIT = 60

EPSILON = 1e-05
MASKED = -1e30
LOG2E = 1.4426950408889634
SCALE = DH**-0.5
SCALE2 = SCALE * LOG2E
F32 = jnp.float32
BF = jnp.bfloat16


def nn(a, b):
    return lax.dot_general(a, b, (((1,), (0,)), ((), ())), preferred_element_type=F32)


def nt(a, b):
    return lax.dot_general(a, b, (((1,), (1,)), ((), ())), preferred_element_type=F32)


def tn(a, b):
    return lax.dot_general(a, b, (((0,), (0,)), ((), ())), preferred_element_type=F32)


def swap(x, axis, distance):
    n = lax.axis_size(axis)
    return lax.ppermute(x, axis, [(i, i ^ distance) for i in range(n)])


def add_low(a, b):
    return (a.astype(F32) + b.astype(F32)).astype(BF)


def params(limit_mb, dims=1):
    return pltpu.CompilerParams(
        dimension_semantics=("arbitrary",) * dims, vmem_limit_bytes=limit_mb << 20
    )


ANY = pl.BlockSpec(memory_space=pl.ANY)


def cost(flops):
    return pl.CostEstimate(flops=flops, transcendentals=0, bytes_accessed=flops // 1000)


def shape(dims, kind):
    return jax.ShapeDtypeStruct(dims, kind)


def whole(dims):
    zeros = (0,) * len(dims)
    return pl.BlockSpec(dims, lambda *_: zeros)


def norm_block(pieces, gain_ref):
    values = [p.astype(F32) for p in pieces]
    mean = sum(jnp.sum(v, axis=1, keepdims=True) for v in values) / D
    values = [v - mean for v in values]
    spread = sum(jnp.sum(v * v, axis=1, keepdims=True) for v in values) / D
    factor = lax.rsqrt(spread + EPSILON)
    return [values[k] * factor * gain_ref[:, block_of(k)] for k in range(4)]


def block_of(k):
    return slice(k * QUARTER, (k + 1) * QUARTER)


def tok_norm_kernel(where, p0, p1, p2, p3, gain_ref, low_ref, raw_ref):
    pieces = [p[...] for p in (p0, p1, p2, p3)]
    normed = norm_block(pieces, gain_ref)
    for k in range(4):
        low_ref[:, block_of(k)] = normed[k].astype(BF)
        raw_ref[:, block_of(k)] = pieces[k]


def tok_norm(where, pieces, gain):
    block = 256
    count = SEQ_LEN // block
    piece = pl.BlockSpec((block, QUARTER), lambda i, w: ((i + w[0] * (count // 2)) % count, 0))
    out = pl.BlockSpec((block, D), lambda i, w: (i, 0))
    return pl.pallas_call(
        tok_norm_kernel,
        out_shape=(shape((SEQ_LEN, D), BF), shape((SEQ_LEN, D), BF)),
        grid_spec=pltpu.PrefetchScalarGridSpec(
            num_scalar_prefetch=1,
            grid=(count,),
            in_specs=[piece] * 4 + [whole((1, D))],
            out_specs=[out, out],
        ),
        compiler_params=params(LIMIT),
        name="tok_norm",
    )(where, *pieces, gain)


def mem_norm_kernel(p0, p1, p2, p3, gain_ref, conv_ref, _, low_ref, raw_ref, keep_ref):
    for block in range(MROWS // 256):
        rows = slice(block * 256, block * 256 + 256)
        pieces = [p[rows, :] for p in (p0, p1, p2, p3)]
        normed = norm_block(pieces, gain_ref)
        for k in range(4):
            low_ref[rows, block_of(k)] = normed[k].astype(BF)
            raw_ref[rows, block_of(k)] = pieces[k]
            if block * 256 >= CMEM:
                start = block * 256 - CMEM
                for j in range(2):
                    keep_ref[k * 2 + j, start : start + 256, :] = normed[k][:, j * DH : j * DH + DH]
    for j in range(D // DH):
        lanes = slice(j * DH, j * DH + DH)
        packed = 0.0
        for t in range(RATE):
            picked = keep_ref[j, pl.ds(t, NEWC, stride=RATE), :]
            packed = packed + conv_ref[t : t + 1, lanes] * picked
        low_ref[MROWS:, lanes] = packed.astype(BF)


def mem_norm(pieces, gain, conv, earlier):
    return pl.pallas_call(
        mem_norm_kernel,
        out_shape=(shape((KM, D), BF), shape((MROWS, D), BF)),
        grid=(1,),
        in_specs=[whole((MROWS, QUARTER))] * 4 + [whole((1, D)), whole((RATE, D)), ANY],
        out_specs=[whole((KM, D)), whole((MROWS, D))],
        scratch_shapes=[pltpu.VMEM((D // DH, MEM, DH), F32)],
        compiler_params=params(LIMIT),
        name="mem_norm",
    )(*pieces, gain, conv, earlier)


def join_kernel(*refs):
    parts, (tok_ref, mem_ref, back_ref) = refs[:4], refs[4:]
    cols, _, part, _, span, _ = parts[0].shape
    for head in range(HEADS):
        c, i = head // part, head % part
        for kind in range(5):
            for dp, ref in enumerate(parts):
                low = dp * span
                for k in range(4):
                    value = ref[c, k, i, kind]
                    if kind < 3:
                        row = (head * 3 + kind) * DH + low
                        tok_ref[row : row + span, block_of(k)] = value
                    if 0 < kind < 3:
                        row = (head * 2 + kind - 1) * DH + low
                        mem_ref[row : row + span, block_of(k)] = value
                    if kind > 2:
                        row = ((kind - 3) * HEADS + head) * DH + low
                        back_ref[row : row + span, block_of(k)] = value


def join_weights(parts):
    dims = ((HEADS * 3 * DH, D), (HEADS * 2 * DH, D), (HEADS * 2 * DH, D))
    return pl.pallas_call(
        join_kernel,
        out_shape=tuple(shape(d, BF) for d in dims),
        grid=(1,),
        in_specs=[whole(p.shape) for p in parts],
        out_specs=[whole(d) for d in dims],
        compiler_params=params(LIMIT),
        name="join_weights",
    )(*parts)


def fill_bias(bias_ref, row_ref, col_ref):
    seg_q, pos_q = row_ref[0:1, :], row_ref[1:2, :]

    def memory_chunk(c, carry):
        rows = pl.ds(pl.multiple_of(c * CHUNK, CHUNK), CHUNK)
        bias_ref[rows, :] = jnp.where(col_ref[rows, 2:3] == seg_q, 0.0, MASKED)
        return carry

    def token_chunk(c, carry):
        start = pl.multiple_of(c * CHUNK, CHUNK)
        rows = pl.ds(start, CHUNK)
        same = (col_ref[rows, 0:1] == seg_q) & (col_ref[rows, 1:2] <= pos_q)
        key_id = lax.broadcasted_iota(jnp.int32, (CHUNK, SEQ_LEN), 0) + start
        query_id = lax.broadcasted_iota(jnp.int32, (CHUNK, SEQ_LEN), 1)
        target = pl.ds(pl.multiple_of(MROWS + c * CHUNK, CHUNK), CHUNK)
        bias_ref[target, :] = jnp.where(same | (key_id == query_id), 0.0, MASKED)
        return carry

    lax.fori_loop(0, MROWS // CHUNK, memory_chunk, 0)
    lax.fori_loop(0, SEQ_LEN // CHUNK, token_chunk, 0)


def forward_kernel(tok_ref, mem_ref, row_ref, col_ref, o_ref, log_ref, bias_ref, s_ref, acc_ref):
    @pl.when(pl.program_id(0) == 0)
    def _():
        fill_bias(bias_ref, row_ref, col_ref)

    queries = tok_ref[:, :DH]

    def scores(key_ref, columns, offset):
        def step(c, top):
            rows = pl.ds(pl.multiple_of(c * CHUNK, CHUNK), CHUNK)
            target = pl.ds(pl.multiple_of(offset + c * CHUNK, CHUNK), CHUNK)
            s = nt(key_ref[rows, columns], queries) * SCALE2 + bias_ref[target, :]
            s_ref[target, :] = s
            return jnp.maximum(top, jnp.max(s.reshape(CHUNK // 8, 8, SEQ_LEN), axis=0))

        return step

    top = jnp.full((8, SEQ_LEN), -3.0e38, F32)
    top = lax.fori_loop(0, MROWS // CHUNK, scores(mem_ref, slice(0, DH), 0), top)
    top = lax.fori_loop(0, SEQ_LEN // CHUNK, scores(tok_ref, slice(DH, 2 * DH), MROWS), top)
    top = jnp.max(top, axis=0, keepdims=True)
    acc_ref[...] = jnp.zeros_like(acc_ref)

    def values(value_ref, columns, offset):
        def step(c, total):
            rows = pl.ds(pl.multiple_of(c * CHUNK, CHUNK), CHUNK)
            target = pl.ds(pl.multiple_of(offset + c * CHUNK, CHUNK), CHUNK)
            p = jnp.exp2(s_ref[target, :] - top)
            acc_ref[...] += nn(value_ref[rows, columns].T, p.astype(BF))
            return total + jnp.sum(p.reshape(CHUNK // 8, 8, SEQ_LEN), axis=0)

        return step

    total = jnp.zeros((8, SEQ_LEN), F32)
    total = lax.fori_loop(0, MROWS // CHUNK, values(mem_ref, slice(DH, 2 * DH), 0), total)
    total = lax.fori_loop(
        0, SEQ_LEN // CHUNK, values(tok_ref, slice(2 * DH, 3 * DH), MROWS), total
    )
    total = jnp.sum(total, axis=0, keepdims=True)
    o_ref[...] = (acc_ref[...] / total).T.astype(BF)
    log_ref[...] = (top + jnp.log2(total)).reshape(1, 1, SEQ_LEN)


def attention_forward(tok_p, mem_p, row_attr, col_attr):
    return pl.pallas_call(
        forward_kernel,
        out_shape=(shape((SEQ_LEN, HEADS * DH), BF), shape((HEADS, 1, SEQ_LEN), F32)),
        grid=(HEADS,),
        in_specs=[
            pl.BlockSpec((SEQ_LEN, 3 * DH), lambda h: (0, h)),
            pl.BlockSpec((KM, 2 * DH), lambda h: (0, h)),
            whole(row_attr.shape),
            whole(col_attr.shape),
        ],
        out_specs=[
            pl.BlockSpec((SEQ_LEN, DH), lambda h: (0, h)),
            pl.BlockSpec((1, 1, SEQ_LEN), lambda h: (h, 0, 0)),
        ],
        scratch_shapes=[
            pltpu.VMEM((MROWS + SEQ_LEN, SEQ_LEN), F32),
            pltpu.VMEM((MROWS + SEQ_LEN, SEQ_LEN), F32),
            pltpu.VMEM((DH, SEQ_LEN), F32),
        ],
        compiler_params=params(LIMIT),
        cost_estimate=cost(25_000_000_000),
        name="attention_forward",
    )(tok_p, mem_p, row_attr, col_attr)


def recon_kernel(tok_ref, mem_ref, *refs):
    gq_ref, gm_ref = refs[-2:]
    q = tok_ref[:, :DH]
    old, new = slice(CMEM, CMEM + OLD), slice(MROWS, KM)
    keys, values = slice(0, DH), slice(DH, 2 * DH)

    def softmax_rows(key_rows):
        s = nt(key_rows, q) * SCALE2
        p = jnp.exp2(s - jnp.max(s, axis=0, keepdims=True))
        return p / jnp.sum(p, axis=0, keepdims=True)

    ko, vo, kn, vn = mem_ref[old, keys], mem_ref[old, values], mem_ref[new, keys], mem_ref[new, values]
    po, pn = softmax_rows(ko), softmax_rows(kn)
    po_low, pn_low = po.astype(BF), pn.astype(BF)
    out_o, out_n = nn(vo.T, po_low), nn(vn.T, pn_low)
    gap = (out_o - out_n).astype(BF)
    gap32 = gap.astype(F32)
    do = (po * (nn(vo, gap) - jnp.sum(gap32 * out_o, axis=0, keepdims=True))).astype(BF)
    dn = (pn * (jnp.sum(gap32 * out_n, axis=0, keepdims=True) - nn(vn, gap))).astype(BF)
    gq_ref[...] = ((nn(ko.T, do) + nn(kn.T, dn)) * SCALE).reshape(1, DH, SEQ_LEN)
    gap_t = gap32.T.astype(BF)
    gm_ref[:OLD, keys] = nn(do, q) * SCALE
    gm_ref[:OLD, values] = nn(po_low, gap_t)
    gm_ref[OLD:MEM, :] = jnp.zeros((MEM - OLD, 2 * DH), F32)
    gm_ref[MEM:, keys] = nn(dn, q) * SCALE
    gm_ref[MEM:, values] = -nn(pn_low, gap_t)


def reconstruction(tok_p, mem_p, *earlier):
    return pl.pallas_call(
        recon_kernel,
        out_shape=(
            shape((HEADS, DH, SEQ_LEN), F32),
            shape((MEM + NEWC, HEADS * 2 * DH), F32),
        ),
        grid=(HEADS,),
        in_specs=[
            pl.BlockSpec((SEQ_LEN, 3 * DH), lambda h: (0, h)),
            pl.BlockSpec((KM, 2 * DH), lambda h: (0, h)),
        ]
        + [ANY] * len(earlier),
        out_specs=[
            pl.BlockSpec((1, DH, SEQ_LEN), lambda h: (h, 0, 0)),
            pl.BlockSpec((MEM + NEWC, 2 * DH), lambda h: (0, h)),
        ],
        compiler_params=params(LIMIT),
        cost_estimate=cost(10_000_000_000),
        name="reconstruction",
    )(tok_p, mem_p, *earlier)


def backward_kernel(
    tok_ref, mem_ref, own_ref, got_ref, o_ref, log_ref, rq_ref, rm_ref, row_ref, col_ref,
    *refs,
):
    gt_ref, gm_ref, bias_ref, acc_ref = refs[-4:]

    @pl.when(pl.program_id(0) == 0)
    def _():
        fill_bias(bias_ref, row_ref, col_ref)

    q = tok_ref[:, :DH]
    go = jnp.concatenate([own_ref[...], got_ref[...]], axis=0)
    product = go.astype(F32) * o_ref[...].astype(F32)
    delta = jnp.sum(product.T, axis=0, keepdims=True)
    log_total = log_ref[...].reshape(1, SEQ_LEN)
    acc_ref[...] = rq_ref[...].reshape(DH, SEQ_LEN)

    def piece(k, v, offset):
        s = nt(k, q) * SCALE2 + bias_ref[offset, :]
        p = jnp.exp2(s - log_total)
        d = (p * (nt(v, go) - delta)).astype(BF)
        acc_ref[...] += nn(k.T, d) * SCALE
        return nn(d, q) * SCALE, nn(p.astype(BF), go)

    def memory_chunk(c, carry):
        rows = pl.ds(pl.multiple_of(c * CHUNK, CHUNK), CHUNK)
        gk, gv = piece(mem_ref[rows, :DH], mem_ref[rows, DH:], rows)
        gm_ref[rows, :DH] = gk.astype(BF)
        gm_ref[rows, DH:] = gv.astype(BF)
        return carry

    def shared_chunk(c, carry):
        rows = pl.ds(pl.multiple_of(c * CHUNK, CHUNK), CHUNK)
        extra = pl.ds(pl.multiple_of(c * CHUNK - CMEM, CHUNK), CHUNK)
        gk, gv = piece(mem_ref[rows, :DH], mem_ref[rows, DH:], rows)
        gm_ref[rows, :DH] = (gk + rm_ref[extra, :DH]).astype(BF)
        gm_ref[rows, DH:] = (gv + rm_ref[extra, DH:]).astype(BF)
        return carry

    def token_chunk(c, carry):
        rows = pl.ds(pl.multiple_of(c * CHUNK, CHUNK), CHUNK)
        target = pl.ds(pl.multiple_of(MROWS + c * CHUNK, CHUNK), CHUNK)
        gk, gv = piece(tok_ref[rows, DH : 2 * DH], tok_ref[rows, 2 * DH :], target)
        gt_ref[rows, DH : 2 * DH] = gk.astype(BF)
        gt_ref[rows, 2 * DH :] = gv.astype(BF)
        return carry

    lax.fori_loop(0, CMEM // CHUNK, memory_chunk, 0)
    lax.fori_loop(CMEM // CHUNK, MROWS // CHUNK, shared_chunk, 0)
    lax.fori_loop(0, SEQ_LEN // CHUNK, token_chunk, 0)
    gm_ref[MROWS:, :] = rm_ref[MEM:, :].astype(BF)
    gt_ref[:, :DH] = acc_ref[...].T.astype(BF)


def attention_backward(
    tok_p, mem_p, go_own, go_got, o, logs, rec_q, rec_m, row_attr, col_attr, *earlier
):
    half = pl.BlockSpec((HALF, DH), lambda h: (0, h))
    return pl.pallas_call(
        backward_kernel,
        out_shape=(
            shape((SEQ_LEN, HEADS * 3 * DH), BF),
            shape((KM, HEADS * 2 * DH), BF),
        ),
        grid=(HEADS,),
        in_specs=[
            pl.BlockSpec((SEQ_LEN, 3 * DH), lambda h: (0, h)),
            pl.BlockSpec((KM, 2 * DH), lambda h: (0, h)),
            half,
            half,
            pl.BlockSpec((SEQ_LEN, DH), lambda h: (0, h)),
            pl.BlockSpec((1, 1, SEQ_LEN), lambda h: (h, 0, 0)),
            pl.BlockSpec((1, DH, SEQ_LEN), lambda h: (h, 0, 0)),
            pl.BlockSpec((MEM + NEWC, 2 * DH), lambda h: (0, h)),
            whole(row_attr.shape),
            whole(col_attr.shape),
        ]
        + [ANY] * len(earlier),
        out_specs=[
            pl.BlockSpec((SEQ_LEN, 3 * DH), lambda h: (0, h)),
            pl.BlockSpec((KM, 2 * DH), lambda h: (0, h)),
        ],
        scratch_shapes=[
            pltpu.VMEM((MROWS + SEQ_LEN, SEQ_LEN), F32),
            pltpu.VMEM((DH, SEQ_LEN), F32),
        ],
        compiler_params=params(LIMIT),
        cost_estimate=cost(35_000_000_000),
        name="attention_backward",
    )(tok_p, mem_p, go_own, go_got, o, logs, rec_q, rec_m, row_attr, col_attr, *earlier)


def center_rows(rows):
    centered = rows - jnp.mean(rows, axis=1, keepdims=True)
    factor = lax.rsqrt(jnp.mean(centered * centered, axis=1, keepdims=True) + EPSILON)
    return centered * factor, factor


def mid_kernel(raw_ref, own_ref, got_ref, w_ref, gain_ref, _, mid_ref, x2_ref):
    width = own_ref.shape[1]
    mid = raw_ref[...].astype(F32) + (
        nn(own_ref[...], w_ref[:width, :]) + nn(got_ref[...], w_ref[width:, :])
    )
    unit, _ = center_rows(mid)
    mid_ref[...] = mid
    x2_ref[...] = (unit * gain_ref[...]).astype(BF)


def residual_mid(raw, o, o_got, w_out, gain, earlier):
    block = 256
    rows = lambda width: pl.BlockSpec((block, width), lambda i: (i, 0))
    return pl.pallas_call(
        mid_kernel,
        out_shape=(shape((HALF, D), F32), shape((HALF, D), BF)),
        grid=(HALF // block,),
        in_specs=[rows(D), rows(HEADS * DH), rows(HEADS * DH), whole((D, D)), whole((1, D)), ANY],
        out_specs=[rows(D), rows(D)],
        compiler_params=params(LIMIT),
        cost_estimate=cost(4 * HALF * D * D),
        name="residual_mid",
    )(raw, o, o_got, w_out, gain, earlier)


TILE = 256


def ffn_kernel(*refs):
    x_own, x_got, c_own, c_got = refs[:4]
    plain, far_up, far_down = refs[4:7], refs[7], refs[8]
    out_keep, out_send, gx_keep, gx_send = refs[9:13]
    grads = refs[13:18]
    x_ref, xt_ref, c_ref, ct_ref, out_ref, gx_ref, up_ref, down_ref = refs[18:]
    step, last = pl.program_id(0), pl.num_programs(0) - 1
    block = step // (pl.num_programs(0) // 4)

    @pl.when(step == 0)
    def _():
        out_ref[...] = jnp.zeros_like(out_ref)
        gx_ref[...] = jnp.zeros_like(gx_ref)
        for (own, got), full, turned in (
            ((x_own, x_got), x_ref, xt_ref),
            ((c_own, c_got), c_ref, ct_ref),
        ):
            for j, half in enumerate((own, got)):
                full[j * HALF : (j + 1) * HALF, :] = half[...]
                for i in range(0, HALF, 256):
                    turned[:, j * HALF + i : j * HALF + i + 256] = half[i : i + 256, :].T

    for k, ref in enumerate(plain):
        @pl.when(block == k)
        def _():
            up_ref[...] = ref[0].reshape(D, TILE)
            down_ref[...] = ref[1].reshape(D, TILE)

    @pl.when(block == 3)
    def _():
        up_ref[...] = far_up[...].reshape(D, TILE)
        down_ref[...] = far_down[...].reshape(D, TILE)

    w_up, w_down = up_ref[...], down_ref[...]
    v = nn(x_ref[...], w_up)
    g_act = nn(c_ref[...], w_down)
    c0, c1 = 0.7978845608028654, 0.044715
    v2 = v * v
    t = jnp.tanh(c0 * v * (1.0 + c1 * v2))
    half = 0.5 * (1.0 + t)
    act = (v * half).astype(BF)
    slope = half + (0.5 * c0) * v * (1.0 - t * t) * (1.0 + (3.0 * c1) * v2)
    g_pre = (g_act * slope).astype(BF)
    out_ref[...] += nt(act, w_down)
    gx_ref[...] += nt(g_pre, w_up)
    grad_up = nn(xt_ref[...], g_pre).astype(BF)
    grad_down = nn(ct_ref[...], act).astype(BF)

    for k in range(3):
        @pl.when(block == k)
        def _():
            for j, row in enumerate((0, 2, 1, 3)):
                grads[k][0, j] = grad_up[block_of(row), :]
                grads[k][1, j] = grad_down[block_of(row), :]

    @pl.when(block == 3)
    def _():
        for j, row in enumerate((0, 2, 1, 3)):
            grads[3][j] = grad_up[block_of(row), :]
            grads[4][j] = grad_down[block_of(row), :]

    @pl.when(step == last)
    def _():
        for total, keep, send in ((out_ref, out_keep, out_send), (gx_ref, gx_keep, gx_send)):
            keep[...] = total[:HALF, :]
            send[...] = total[HALF:, :].astype(BF)


def feed_forward(x2, x2_got, cot, cot_got, plain, far_up, far_down):
    width = far_up.shape[-1]
    tiles = width // TILE

    def tile(k, step):
        return jnp.clip(step - k * tiles, 0, tiles - 1)

    def pair(k):
        return pl.BlockSpec((2, 4, QUARTER, TILE), lambda i: (0, 0, 0, tile(k, i)))

    far = pl.BlockSpec((4, QUARTER, TILE), lambda i: (0, 0, tile(3, i)))
    blocks = [pair(0), pair(1), pair(2), far, far]
    once = pl.BlockSpec((HALF, D), lambda i: (0, 0), pipeline_mode=pl.Buffered(1))
    rows = whole((HALF, D))
    full, turned = pltpu.VMEM((SEQ_LEN, D), BF), pltpu.VMEM((D, SEQ_LEN), BF)
    total = pltpu.VMEM((SEQ_LEN, D), F32)
    return pl.pallas_call(
        ffn_kernel,
        out_shape=(
            shape((HALF, D), F32), shape((HALF, D), BF),
            shape((HALF, D), F32), shape((HALF, D), BF),
        )
        + (shape(plain[0].shape, BF),) * 3
        + (shape(far_up.shape, BF),) * 2,
        grid=(4 * tiles,),
        in_specs=[once] * 4 + blocks,
        out_specs=[rows] * 4 + blocks,
        scratch_shapes=[full, turned, full, turned, total, total] + [pltpu.VMEM((D, TILE), BF)] * 2,
        compiler_params=params(LIMIT),
        cost_estimate=cost(12 * SEQ_LEN * D * 4 * width),
        name="feed_forward",
    )(x2, x2_got, cot, cot_got, *plain, far_up, far_down)


def out_sum_kernel(mid_ref, keep_ref, got_ref, *refs):
    total = mid_ref[...] + (keep_ref[...] + got_ref[...].astype(F32))
    for k, ref in enumerate(refs[-4:]):
        ref[...] = total[:, block_of(k)].astype(BF)


def out_sum(mid, keep, got, *earlier):
    block = 256
    rows = lambda width: pl.BlockSpec((block, width), lambda i: (i, 0))
    return pl.pallas_call(
        out_sum_kernel,
        out_shape=(shape((HALF, QUARTER), BF),) * 4,
        grid=(HALF // block,),
        in_specs=[rows(D)] * 3 + [ANY] * len(earlier),
        out_specs=[rows(QUARTER)] * 4,
        compiler_params=params(LIMIT),
        name="out_sum",
    )(mid, keep, got, *earlier)


def mid_back_kernel(gx_ref, got_ref, mid_ref, cot_ref, gain_ref, w_ref, gm_ref, ga_ref, keep_ref, send_ref, gn_ref):
    @pl.when(pl.program_id(0) == 0)
    def _():
        gn_ref[...] = jnp.zeros_like(gn_ref)

    unit, factor = center_rows(mid_ref[...])
    gx = gx_ref[...] + got_ref[...].astype(F32)
    gn_ref[...] += jnp.sum(gx * unit, axis=0, keepdims=True)
    s = gx * gain_ref[...]
    g_mid = cot_ref[...].astype(F32) + factor * (
        s - jnp.mean(s, axis=1, keepdims=True) - unit * jnp.mean(s * unit, axis=1, keepdims=True)
    )
    gm_ref[...] = g_mid
    low = g_mid.astype(BF)
    ga_ref[...] = low
    width = keep_ref.shape[1]
    send_ref[...] = nt(low, w_ref[width:, :]).astype(BF)
    keep_ref[...] = nt(low, w_ref[:width, :]).astype(BF)


def mid_back(gx, gx_got, mid, cot, gain, w_out):
    block = 256
    rows = lambda width: pl.BlockSpec((block, width), lambda i: (i, 0))
    half = shape((HALF, HEADS * DH), BF)
    return pl.pallas_call(
        mid_back_kernel,
        out_shape=(shape((HALF, D), F32), shape((HALF, D), BF), half, half, shape((1, D), F32)),
        grid=(HALF // block,),
        in_specs=[rows(D)] * 4 + [whole((1, D)), whole((D, D))],
        out_specs=[rows(D), rows(D), rows(HEADS * DH), rows(HEADS * DH), whole((1, D))],
        compiler_params=params(LIMIT),
        cost_estimate=cost(2 * HALF * D * D),
        name="mid_back",
    )(gx, gx_got, mid, cot, gain, w_out)


def tok_grad_kernel(g_ref, w_ref, raw_ref, *refs):
    keep_ref, send_ref, gn_ref = refs[-3:]
    step = pl.program_id(0)

    @pl.when(step == 0)
    def _():
        gn_ref[...] = jnp.zeros_like(gn_ref)

    gx = nn(g_ref[...], w_ref[...])
    unit, _ = center_rows(raw_ref[...].astype(F32))
    gn_ref[...] += jnp.sum(gx * unit, axis=0, keepdims=True)

    @pl.when(step < pl.num_programs(0) // 2)
    def _():
        send_ref[...] = gx.astype(BF)

    @pl.when(step >= pl.num_programs(0) // 2)
    def _():
        keep_ref[...] = gx


def tok_grad(g_tok, w_tok, raw, *earlier):
    block = 256
    steps, half = SEQ_LEN // block, HALF // block
    rows = lambda width: pl.BlockSpec((block, width), lambda i: ((i + half) % steps, 0))
    return pl.pallas_call(
        tok_grad_kernel,
        out_shape=(shape((HALF, D), F32), shape((HALF, D), BF), shape((1, D), F32)),
        grid=(steps,),
        in_specs=[rows(HEADS * 3 * DH), whole((HEADS * 3 * DH, D)), rows(D)]
        + [ANY] * len(earlier),
        out_specs=[
            pl.BlockSpec((block, D), lambda i: (jnp.maximum(i - half, 0), 0)),
            pl.BlockSpec((block, D), lambda i: (jnp.minimum(i, half - 1), 0)),
            whole((1, D)),
        ],
        compiler_params=params(LIMIT),
        name="tok_grad",
    )(g_tok, w_tok, raw, *earlier)


def input_grad_kernel(keep_ref, got_ref, raw_ref, gm_ref, gain_ref, *refs):
    unit, factor = center_rows(raw_ref[...].astype(F32))
    got = [got_ref[:, block_of(k ^ 1)].astype(F32) for k in range(4)]
    s = (keep_ref[...] + jnp.concatenate(got, axis=1)) * gain_ref[...]
    g = gm_ref[...] + factor * (
        s - jnp.mean(s, axis=1, keepdims=True) - unit * jnp.mean(s * unit, axis=1, keepdims=True)
    )
    for k, ref in enumerate(refs[-4:]):
        ref[...] = g[:, block_of(k)].astype(BF)


def input_grad(keep, got, raw, g_mid, gain, *earlier):
    block = 256
    rows = pl.BlockSpec((block, D), lambda i: (i, 0))
    return pl.pallas_call(
        input_grad_kernel,
        out_shape=(shape((HALF, QUARTER), BF),) * 4,
        grid=(HALF // block,),
        in_specs=[rows, rows, rows, rows, whole((1, D))] + [ANY] * len(earlier),
        out_specs=[pl.BlockSpec((block, QUARTER), lambda i: (i, 0))] * 4,
        compiler_params=params(LIMIT),
        cost_estimate=cost(20_000_000_000),
        name="input_grad",
    )(keep, got, raw, g_mid, gain, *earlier)


def mem_grad_kernel(g_ref, w_ref, raw_ref, gain_ref, conv_ref, *refs):
    gn_ref, gc_ref, unit_ref = refs[-3:]
    total = jnp.zeros((1, D), F32)
    for block in range(MROWS // 256):
        rows = slice(block * 256, block * 256 + 256)
        unit, _ = center_rows(raw_ref[rows, :].astype(F32))
        total = total + jnp.sum(nn(g_ref[rows, :], w_ref[...]) * unit, axis=0, keepdims=True)
        if block * 256 >= CMEM:
            start = block * 256 - CMEM
            for j in range(D // DH):
                unit_ref[j, start : start + 256, :] = unit[:, j * DH : j * DH + DH]
    gn_ref[...] = total
    packed = nn(g_ref[MROWS:, :], w_ref[...])
    for j in range(D // DH):
        lanes = slice(j * DH, j * DH + DH)
        for t in range(RATE):
            picked = unit_ref[j, pl.ds(t, NEWC, stride=RATE), :]
            term = jnp.sum(packed[:, lanes] * picked, axis=0, keepdims=True)
            gc_ref[t : t + 1, lanes] = term * gain_ref[:, lanes]
            gn_ref[:, lanes] += conv_ref[t : t + 1, lanes] * term


def mem_grad(g_mem, w_mem, raw, gain, conv, *earlier):
    return pl.pallas_call(
        mem_grad_kernel,
        out_shape=(shape((1, D), F32), shape((RATE, D), F32)),
        grid=(1,),
        in_specs=[
            whole((KM, D)), whole((D, D)), whole((MROWS, D)), whole((1, D)), whole((RATE, D)),
        ]
        + [ANY] * len(earlier),
        out_specs=[whole((1, D)), whole((RATE, D))],
        scratch_shapes=[pltpu.VMEM((D // DH, MEM, DH), F32)],
        compiler_params=params(LIMIT),
        name="mem_grad",
    )(g_mem, w_mem, raw, gain, conv, *earlier)


def store_spans(grad, index, keep_ref, send_ref):
    span = DH // 4
    for x in range(2):
        for core, ref in enumerate((keep_ref, send_ref)):
            row = (2 * x + core) * span
            ref[(x,) + index] = grad[row : row + span, :].astype(BF)


def qkv_grad_kernel(gt_ref, xt_ref, gm_ref, xm_ref, *refs):
    for kind in range(3):
        grad = nn(gt_ref[:, kind * DH : (kind + 1) * DH].T, xt_ref[...])
        if kind > 0:
            grad = grad + nn(gm_ref[:, (kind - 1) * DH : kind * DH].T, xm_ref[...])
        store_spans(grad, (0, kind), *refs[-2:])


def qkv_grad(g_tok, x_tok, g_mem, x_mem, *earlier):
    out = shape((2, HEADS, 3, DH // 4, D), BF)
    block = pl.BlockSpec((2, 1, 3, DH // 4, D), lambda h: (0, h, 0, 0, 0))
    return pl.pallas_call(
        qkv_grad_kernel,
        out_shape=(out, out),
        grid=(HEADS,),
        in_specs=[
            pl.BlockSpec((SEQ_LEN, 3 * DH), lambda h: (0, h)),
            whole((SEQ_LEN, D)),
            pl.BlockSpec((KM, 2 * DH), lambda h: (0, h)),
            whole((KM, D)),
        ]
        + [ANY] * len(earlier),
        out_specs=[block, block],
        compiler_params=params(LIMIT),
        name="qkv_grad",
    )(g_tok, x_tok, g_mem, x_mem, *earlier)


def out_grad_kernel(own_ref, got_ref, g_ref, keep_ref, send_ref):
    for z, ref in enumerate((own_ref, got_ref)):
        store_spans(nn(ref[...].T, g_ref[...]), (0, z), keep_ref, send_ref)


def out_grad(o, o_got, g_attn):
    out = shape((2, HEADS, 2, DH // 4, D), BF)
    block = pl.BlockSpec((2, 1, 2, DH // 4, D), lambda h: (0, h, 0, 0, 0))
    half = pl.BlockSpec((HALF, DH), lambda h: (0, h))
    return pl.pallas_call(
        out_grad_kernel,
        out_shape=(out, out),
        grid=(HEADS,),
        in_specs=[half, half, whole((HALF, D))],
        out_specs=[block, block],
        compiler_params=params(LIMIT),
        name="out_grad",
    )(o, o_got, g_attn)


def merge_kernel(count, lanes, *refs):
    outs = refs[-2:]
    for j, out in enumerate(outs):
        if lanes:
            half = slice(j * out.shape[-1], (j + 1) * out.shape[-1])
            parts = [ref[:, half] for ref in refs[:count]]
        else:
            parts = [ref[...] for ref in refs[j * count : (j + 1) * count]]
        out[...] = sum(part.astype(F32) for part in parts).astype(BF)


def merge(arrays, *earlier, lanes=False, axis=0, work=0):
    dims = arrays[0].shape
    count = len(arrays)
    if lanes:
        out = dims[:-1] + (dims[-1] // 2,)
        flat = [a.reshape(-1, dims[-1]) for a in arrays]
        rows = flat[0].shape[0]
        grid, out_dims = (1,), (rows, out[-1])
        ins, blocks = [whole(flat[0].shape)] * count, [whole(out_dims)] * 2
    else:
        out = dims[:axis] + (dims[axis] // 2,) + dims[axis + 1 :]
        outer = dims[0] if axis else 1
        flat = [a.reshape(2 * outer, -1, dims[-1]) for a in arrays]
        block = (1,) + flat[0].shape[1:]
        grid, out_dims = (outer,), (outer,) + block[1:]
        low = pl.BlockSpec(block, lambda i: (2 * i, 0, 0))
        high = pl.BlockSpec(block, lambda i: (2 * i + 1, 0, 0))
        same = pl.BlockSpec(block, lambda i: (i, 0, 0))
        ins, blocks, flat = [low] * count + [high] * count, [same] * 2, flat * 2
    pair = pl.pallas_call(
        functools.partial(merge_kernel, count, lanes),
        out_shape=(shape(out_dims, BF),) * 2,
        grid=grid,
        in_specs=ins + [ANY] * len(earlier),
        out_specs=blocks,
        compiler_params=params(LIMIT),
        cost_estimate=cost(work) if work else None,
        name="merge",
    )(*flat, *earlier)
    return [g.reshape(out) for g in pair]


def pick(g, index, axis=0):
    return lax.dynamic_index_in_dim(g, index, axis, keepdims=False)


def after(value, *earlier):
    return pl.pallas_call(
        lambda *refs: None,
        out_shape=shape(value.shape, value.dtype),
        in_specs=[ANY] * (1 + len(earlier)),
        out_specs=ANY,
        input_output_aliases={0: 0},
        name="after",
    )(value, *earlier)


def doubled(g, axis, distance):
    return jnp.concatenate([g, swap(g, axis, distance)], axis=0)


def both(parts, axis, distance):
    return parts + [swap(p, axis, distance) for p in parts]


def doubled_cols(g, n_col, first=1):
    while first < n_col:
        g = doubled(g, "col", first)
        first *= 2
    return g


def halve_col(g, last=1):
    while g.shape[0] > 1:
        n = g.shape[0] // 2
        g = add_low(g[:n], swap(g[n:], "col", n * last))
    return g[0]


def halve_row(g):
    g = add_low(g[:2], swap(g[2:], "row", 2))
    return g[0].astype(F32) + swap(g[1], "row", 1).astype(F32)


def per_device(
    hidden, memory, compressed, seg_ids, positions, keep_mask, mem_seg, cotangent,
    w_qkv, w_out, w_up, w_down, norm_attn, norm_ffn, conv_w,
):
    n_col = lax.axis_size("col")
    heads_part = w_qkv.shape[2]
    part = max(heads_part // 2, 1)
    row, col = lax.axis_index("row"), lax.axis_index("col")
    z_high, z_low = row // 2, row % 2
    low_first = z_low == 0
    where = z_low.reshape(1).astype(jnp.int32)
    span = DH // 4

    def by_low(pair):
        return jnp.where(low_first, pair, jnp.flip(pair, axis=0))

    tokens = hidden.reshape(2, SEQ_LEN, QUARTER)
    tok_mine, tok_other = pick(tokens, z_high), pick(tokens, 1 - z_high)
    tok_far, tok_near = swap(tok_other, "row", 2), swap(tok_mine, "row", 1)
    tok_pieces = [tok_mine, tok_near, tok_far, swap(tok_far, "row", 1)]

    qkv = w_qkv.astype(BF).transpose(2, 1, 3, 0)
    outs = w_out.astype(BF)
    if heads_part % 2 == 0:
        qkv = by_low(qkv.reshape(2, part, 3, span, QUARTER))
        outs = by_low(outs.reshape(2, part, 1, span, QUARTER))
        near = jnp.concatenate([qkv[0], outs[0], outs[1]], axis=1)
        far = jnp.concatenate([qkv[1], outs[1], outs[0]], axis=1)
        heads = jnp.stack(
            [near, swap(far, "row", 1), swap(near, "row", 2), swap(far, "row", 3)]
        )
        heads = doubled_cols(after(heads[None], tok_near), n_col)
    else:
        qkv = jnp.stack([qkv] + [swap(qkv, "row", k) for k in (1, 2, 3)])
        outs = jnp.stack([outs] + [swap(outs, "row", k) for k in (1, 2, 3)])
        qkv = doubled_cols(jnp.where(low_first, qkv, swap(qkv, "col", 1))[None], n_col, 2)
        outs = doubled_cols(outs[None], n_col, 2)
        outs = by_low(jnp.stack([outs, swap(outs, "col", 1)]))
        heads = jnp.concatenate([qkv, jnp.moveaxis(outs, 0, 3)], axis=3)
    own = after(jnp.stack([w_up.astype(BF), w_down.astype(BF).T]), tok_far, tok_near)
    w_far = swap(own, "row", 2)
    heads = both([after(heads, w_far, tok_pieces[3])], "dp", 2)
    own = after(own, w_far, tok_pieces[3])
    w_near = swap(own, "row", 1)
    w_both = swap(w_far, "row", 1)
    small = jnp.concatenate(
        [norm_attn, norm_ffn, conv_w.reshape(-1)]
        + [a.astype(F32) for a in (seg_ids, positions, keep_mask, mem_seg)]
    )
    small = after(small, tok_near)
    shared = jnp.stack([small, swap(small, "row", 2)])
    shared = jnp.stack([shared, swap(shared, "row", 1)], axis=1).reshape(4, -1)
    gains = shared[:, : 5 * QUARTER].reshape(4, 5, QUARTER).transpose(1, 0, 2).reshape(5, D)
    gain1, gain2, conv = gains[0:1], gains[1:2], gains[2:5]
    spans = seg_ids.shape[0] // SEQ_LEN
    sequence = 2 * col + z_high
    ids = pick(shared, row ^ (sequence // spans))[5 * QUARTER :]
    ids = pick(ids.reshape(4, spans, SEQ_LEN), sequence % spans, 1)
    rolled = jnp.concatenate([ids[:3, HALF:], ids[:3, :HALF]], axis=1)
    seg, pos, keep = jnp.where(low_first, ids[:3], rolled)
    row_attr = jnp.stack([seg, pos])
    col_attr = jnp.stack([jnp.where(keep == 1, seg, -2.0), pos, ids[3]], axis=1)

    memories = jnp.concatenate(
        [compressed.reshape(2, CMEM, QUARTER), memory.reshape(2, MEM, QUARTER)], axis=1
    )
    mem_other = after(pick(memories, 1 - z_high), w_far, tok_pieces[3])
    mem_far = swap(mem_other, "row", 2)
    heads = both([after(h, mem_far, w_near, w_both) for h in heads], "dp", 1)
    w_tok, w_mem, w_back = join_weights([heads[0], heads[2], heads[1], heads[3]])
    own = jnp.stack([own, after(w_near, mem_far, heads[2], heads[3]), w_far, w_both], axis=1)
    half_col = n_col // 2
    distance = 1
    while distance < half_col:
        own = jnp.concatenate([own, swap(own, "col", distance)], axis=3)
        distance *= 2
    own_y, own_x = swap(own, "col", half_col), swap(own, "dp", 2)
    far_up, far_down = swap(own_x[0], "col", half_col), swap(own_y[1], "dp", 2)

    mem_mine = after(pick(memories, z_high), mem_far, w_near)
    mem_near = swap(mem_mine, "row", 1)
    mem_pieces = [mem_mine, mem_near, mem_far, swap(mem_far, "row", 1)]

    x_tok, raw_tok = tok_norm(where, tok_pieces, after(gain1, heads[2]))
    tok_p = nt(x_tok, w_tok).astype(BF)
    x_mem, raw_mem = mem_norm(mem_pieces, gain1, conv, tok_p)
    mem_p = nt(x_mem, w_mem).astype(BF)
    cots = cotangent.reshape(4, HALF, QUARTER)
    cots = [after(pick(cots, row ^ k), mem_p, tok_p) for k in range(4)]
    cot = jnp.concatenate([cots[0]] + [swap(cots[k], "row", k) for k in (1, 2, 3)], axis=1)
    cot_got = swap(cot, "dp", 1)
    o, logs = attention_forward(tok_p, mem_p, row_attr, col_attr)
    o_got = swap(o[HALF:], "row", 1)
    rec_q, rec_m = reconstruction(tok_p, mem_p, cot, own_x, own_y)
    mid, x2 = residual_mid(raw_tok, o, o_got, w_back, gain2, rec_m)

    x2_got = swap(x2, "dp", 1)
    out_keep, out_send, gx_keep, gx_send, *grads = feed_forward(
        x2, x2_got, cot, cot_got, (own, own_y, own_x), far_up, far_down
    )
    gx_got = swap(gx_send, "dp", 1)
    g_mid, g_attn, go_keep, go_send, gain2_sum = mid_back(
        gx_keep, gx_got, mid, cot, gain2, w_back
    )
    go_got = swap(go_send, "row", 1)

    own, own_y, own_x, far_up, far_down = grads
    far_up = after(swap(far_up, "col", half_col), go_got)
    far_down = after(swap(far_down, "dp", 2), go_got)
    sum_x = own_x.at[0].set(add_low(own_x[0], far_up))
    sum_y = own_y.at[1].set(add_low(own_y[1], far_down))
    got_x, got_y = swap(sum_x, "dp", 2), swap(sum_y, "col", half_col)

    def to_owners(blocks):
        return [blocks[0]] + [swap(blocks[k], "row", k) for k in (1, 2, 3)]

    def in_order(blocks):
        blocks = [jnp.where(low_first, blocks[k], blocks[k ^ 1]) for k in range(4)]
        blocks = [jnp.where(z_high == 0, blocks[k], blocks[k ^ 2]) for k in range(4)]
        return jnp.concatenate(blocks, axis=0)

    out_got = swap(out_send, "dp", 1)
    g_out = out_grad(o, o_got, g_attn)
    outs = out_sum(mid, out_keep, out_got, g_out[1])
    outs = to_owners([outs[0]] + [after(piece, go_got) for piece in outs[1:]])

    g_tok, g_mem = attention_backward(
        tok_p, mem_p, go_keep, go_got, o, logs, rec_q, rec_m, row_attr, col_attr,
        sum_x, sum_y, outs[0],
    )
    gx, gx_send, gain1_tok = tok_grad(g_tok, w_tok, raw_tok, *outs[1:])
    gx_got = swap(gx_send, "row", 1)
    distance = half_col
    if distance > 1:
        total = (own.astype(F32) + got_x.astype(F32) + got_y.astype(F32)).astype(BF)
        while distance > 1:
            distance //= 2
            n = total.shape[3] // 2
            total = add_low(total[..., :n], swap(total[..., n:], "col", distance))
        even, odd = total[:, :2], total[:, 2:]
    else:
        even, odd = merge([own, got_x, got_y], gx_send, axis=1)

    def halves(g):
        return g.reshape((n_col, part) + g.shape[1:])

    g_qkv = qkv_grad(g_tok, x_tok, g_mem, x_mem, odd)
    g_out, out_send = merge([g_out[0], swap(g_out[1], "dp", 1)], g_qkv[1])
    out_got = swap(out_send, "dp", 2)
    gain1_mem, conv_sum = mem_grad(g_mem, w_mem, raw_mem, gain1, conv, out_send)
    d_rows = input_grad(gx, gx_got, raw_tok, g_mid, gain1, gain1_mem)
    d_input = to_owners(d_rows)
    if heads_part % 2 == 0:
        g_out, out_send = merge([halves(g_out[0]), halves(out_got[0])], d_rows[0])
    g_qkv, qkv_send = merge([g_qkv[0], swap(g_qkv[1], "dp", 1)], out_send)
    qkv_got = swap(qkv_send, "dp", 2)
    even, even_send = merge([even, swap(odd, "row", 1)], qkv_send, axis=1)
    even_got = swap(even_send[:, 0], "row", 2)
    if heads_part % 2 == 0:
        def over_row(g, got, first, second):
            g, send = merge([g, got], first, lanes=True)
            g, last = merge([g, swap(send, "row", 2)], second, lanes=True)
            return g, swap(last, "row", 1), send

        g_qkv, qkv_send = merge(
            [halves(g_qkv[0]), halves(qkv_got[0])], even_send, *d_input[1:]
        )
        out_pair = over_row(g_out[0], swap(out_send[0], "col", 1), qkv_send, qkv_send)
        g_qkv, got, last = over_row(
            g_qkv[0], swap(qkv_send[0], "col", 1), out_pair[2], out_pair[2]
        )
        grad_qkv = by_low(jnp.stack([g_qkv, got])).astype(F32)
        grad_qkv = grad_qkv.reshape(heads_part, 3, span, QUARTER)
        g_out, got, _ = out_pair
        g_out, got = jnp.swapaxes(g_out, 0, 1), jnp.swapaxes(got, 0, 1)
        grad_out = by_low(g_out.astype(F32) + jnp.flip(got, axis=0).astype(F32))
        grad_out = grad_out.reshape(heads_part, span, QUARTER)
    else:
        g_out, g_qkv = add_low(g_out[0], out_got[0]), add_low(g_qkv[0], qkv_got[0])
        g_qkv = halve_col(g_qkv, 2)
        qkv_send = g_qkv
        grad_qkv, grad_out = reduce_heads(g_qkv, g_out, by_low, low_first)
        last = d_rows[0]
    vectors = jnp.concatenate([gain1_tok + gain1_mem, gain2_sum, conv_sum], axis=0)
    vectors = after(vectors, qkv_send)
    vectors = vectors.reshape(5, 4, QUARTER).transpose(1, 0, 2)
    for distance in (1, 2):
        vectors = vectors + swap(vectors, "dp", distance)
    distance = 1
    while distance < n_col:
        vectors = vectors + swap(vectors, "col", distance)
        distance *= 2
    vectors = after(vectors, g_qkv, even_got)
    vectors = vectors[:2] + swap(vectors[2:], "row", 2)
    vectors = vectors[0] + swap(vectors[1], "row", 1)
    grad_qkv = grad_qkv.transpose(3, 1, 0, 2)
    grads = even[:, 0].astype(F32) + even_got.astype(F32)
    d_input, out = in_order(d_input), in_order(outs)
    return (
        out, d_input, grad_qkv, grad_out, grads[0], grads[1].T, vectors[0], vectors[1], vectors[2:]
    )


def reduce_heads(g_qkv, g_out, by_low, low_first):
    span = DH // 4
    zeros = jnp.zeros_like(g_qkv)
    g_qkv = add_low(
        jnp.where(low_first, g_qkv, zeros), swap(jnp.where(low_first, zeros, g_qkv), "col", 1)
    )
    g_out = by_low(jnp.swapaxes(g_out, 0, 1))
    g_out = halve_col(add_low(g_out[0], swap(g_out[1], "col", 1)), 2)
    g_qkv = halve_row(jnp.moveaxis(g_qkv.reshape(3, span, 4, QUARTER), 2, 0))[None]
    g_out = halve_row(jnp.moveaxis(g_out.reshape(span, 4, QUARTER), 1, 0))[None]
    return g_qkv, g_out


def solution(mesh):
    tokens, features = ("dp", "col"), "row"
    placed = (
        P(tokens, features),
        P(tokens, features),
        P(tokens, features),
        P(("dp", "row")),
        P(("dp", "row")),
        P(("dp", "row")),
        P(("dp", "row")),
        P(tokens, features),
        P("row", None, "col", "dp"),
        P("col", "dp", "row"),
        P("row", tokens),
        P(tokens, "row"),
        P("row"),
        P("row"),
        P(None, "row"),
    )
    return jax.shard_map(
        per_device,
        mesh=mesh,
        in_specs=placed,
        out_specs=(
            P(tokens, features),
            P(tokens, features),
            P("row", None, "col", "dp"),
            P("col", "dp", "row"),
            P("row", tokens),
            P(tokens, "row"),
            P("row"),
            P("row"),
            P(None, "row"),
        ),
        check_vma=False,
    )
```

```python
import functools

import jax
import jax.numpy as jnp
from jax import lax
from jax.experimental import pallas as pl
from jax.experimental.pallas import tpu as pltpu
from jax.sharding import PartitionSpec as P

D = 1024
DH = 128
MEM = 512
CMEM = 512
RATE = 3
NEWC = 128
SEQ_LEN = 1024
HALF = SEQ_LEN // 2
HEADS = 4
OLD = RATE * NEWC
MROWS = CMEM + MEM
KM = MROWS + NEWC
QUARTER = D // 4
CHUNK = 256
LIMIT = 60

EPSILON = 1e-05
MASKED = -1e30
LOG2E = 1.4426950408889634
SCALE = DH**-0.5
SCALE2 = SCALE * LOG2E
F32 = jnp.float32
BF = jnp.bfloat16


def nn(a, b):
    return lax.dot_general(a, b, (((1,), (0,)), ((), ())), preferred_element_type=F32)


def nt(a, b):
    return lax.dot_general(a, b, (((1,), (1,)), ((), ())), preferred_element_type=F32)


def tn(a, b):
    return lax.dot_general(a, b, (((0,), (0,)), ((), ())), preferred_element_type=F32)


def swap(x, axis, distance):
    n = lax.axis_size(axis)
    return lax.ppermute(x, axis, [(i, i ^ distance) for i in range(n)])


def add_low(a, b):
    return (a.astype(F32) + b.astype(F32)).astype(BF)


def params(limit_mb, dims=1):
    return pltpu.CompilerParams(
        dimension_semantics=("arbitrary",) * dims, vmem_limit_bytes=limit_mb << 20
    )


ANY = pl.BlockSpec(memory_space=pl.ANY)


def cost(flops):
    return pl.CostEstimate(flops=flops, transcendentals=0, bytes_accessed=flops // 1000)


def shape(dims, kind):
    return jax.ShapeDtypeStruct(dims, kind)


def whole(dims):
    zeros = (0,) * len(dims)
    return pl.BlockSpec(dims, lambda *_: zeros)


def norm_block(pieces, gain_ref):
    values = [p.astype(F32) for p in pieces]
    mean = sum(jnp.sum(v, axis=1, keepdims=True) for v in values) / D
    values = [v - mean for v in values]
    spread = sum(jnp.sum(v * v, axis=1, keepdims=True) for v in values) / D
    factor = lax.rsqrt(spread + EPSILON)
    return [values[k] * factor * gain_ref[:, block_of(k)] for k in range(4)]


def block_of(k):
    return slice(k * QUARTER, (k + 1) * QUARTER)


def tok_norm_kernel(where, p0, p1, p2, p3, gain_ref, low_ref, raw_ref):
    pieces = [p[...] for p in (p0, p1, p2, p3)]
    normed = norm_block(pieces, gain_ref)
    for k in range(4):
        low_ref[:, block_of(k)] = normed[k].astype(BF)
        raw_ref[:, block_of(k)] = pieces[k]


def tok_norm(where, pieces, gain):
    block = 128
    count = SEQ_LEN // block
    piece = pl.BlockSpec((block, QUARTER), lambda i, w: ((i + w[0] * (count // 2)) % count, 0))
    out = pl.BlockSpec((block, D), lambda i, w: (i, 0))
    return pl.pallas_call(
        tok_norm_kernel,
        out_shape=(shape((SEQ_LEN, D), BF), shape((SEQ_LEN, D), BF)),
        grid_spec=pltpu.PrefetchScalarGridSpec(
            num_scalar_prefetch=1,
            grid=(count,),
            in_specs=[piece] * 4 + [whole((1, D))],
            out_specs=[out, out],
        ),
        compiler_params=params(LIMIT),
        name="tok_norm",
    )(where, *pieces, gain)


def mem_norm_kernel(p0, p1, p2, p3, gain_ref, conv_ref, _, low_ref, raw_ref, keep_ref):
    def norm_rows(block, carry):
        rows = pl.ds(pl.multiple_of(block * 256, 256), 256)
        pieces = [p[rows, :] for p in (p0, p1, p2, p3)]
        normed = norm_block(pieces, gain_ref)
        for k in range(4):
            low_ref[rows, block_of(k)] = normed[k].astype(BF)
            raw_ref[rows, block_of(k)] = pieces[k]
            for j in range(2):
                keep_ref[k * 2 + j, rows, :] = normed[k][:, j * DH : j * DH + DH]
        return carry

    lax.fori_loop(0, MROWS // 256, norm_rows, 0)
    for j in range(D // DH):
        lanes = slice(j * DH, j * DH + DH)
        packed = 0.0
        for t in range(RATE):
            picked = keep_ref[j, pl.ds(CMEM + t, NEWC, stride=RATE), :]
            packed = packed + conv_ref[t : t + 1, lanes] * picked
        low_ref[MROWS:, lanes] = packed.astype(BF)


def mem_norm(pieces, gain, conv, earlier):
    return pl.pallas_call(
        mem_norm_kernel,
        out_shape=(shape((KM, D), BF), shape((MROWS, D), BF)),
        grid=(1,),
        in_specs=[whole((MROWS, QUARTER))] * 4 + [whole((1, D)), whole((RATE, D)), ANY],
        out_specs=[whole((KM, D)), whole((MROWS, D))],
        scratch_shapes=[pltpu.VMEM((D // DH, MROWS, DH), F32)],
        compiler_params=params(LIMIT),
        name="mem_norm",
    )(*pieces, gain, conv, earlier)


def join_kernel(*refs):
    parts, (tok_ref, mem_ref, back_ref) = refs[:4], refs[4:]
    cols, _, part, _, span, _ = parts[0].shape
    for head in range(HEADS):
        c, i = head // part, head % part
        for kind in range(5):
            for dp, ref in enumerate(parts):
                low = dp * span
                for k in range(4):
                    value = ref[c, k, i, kind]
                    if kind < 3:
                        row = (head * 3 + kind) * DH + low
                        tok_ref[row : row + span, block_of(k)] = value
                    if 0 < kind < 3:
                        row = (head * 2 + kind - 1) * DH + low
                        mem_ref[row : row + span, block_of(k)] = value
                    if kind > 2:
                        row = ((kind - 3) * HEADS + head) * DH + low
                        back_ref[row : row + span, block_of(k)] = value


def join_weights(parts):
    dims = ((HEADS * 3 * DH, D), (HEADS * 2 * DH, D), (HEADS * 2 * DH, D))
    return pl.pallas_call(
        join_kernel,
        out_shape=tuple(shape(d, BF) for d in dims),
        grid=(1,),
        in_specs=[whole(p.shape) for p in parts],
        out_specs=[whole(d) for d in dims],
        compiler_params=params(LIMIT),
        name="join_weights",
    )(*parts)


def fill_bias(bias_ref, row_ref, col_ref):
    seg_q, pos_q = row_ref[0:1, :], row_ref[1:2, :]

    def memory_chunk(c, carry):
        rows = pl.ds(pl.multiple_of(c * CHUNK, CHUNK), CHUNK)
        bias_ref[rows, :] = jnp.where(col_ref[rows, 2:3] == seg_q, 0.0, MASKED)
        return carry

    def token_chunk(c, carry):
        start = pl.multiple_of(c * CHUNK, CHUNK)
        rows = pl.ds(start, CHUNK)
        same = (col_ref[rows, 0:1] == seg_q) & (col_ref[rows, 1:2] <= pos_q)
        key_id = lax.broadcasted_iota(jnp.int32, (CHUNK, SEQ_LEN), 0) + start
        query_id = lax.broadcasted_iota(jnp.int32, (CHUNK, SEQ_LEN), 1)
        target = pl.ds(pl.multiple_of(MROWS + c * CHUNK, CHUNK), CHUNK)
        bias_ref[target, :] = jnp.where(same | (key_id == query_id), 0.0, MASKED)
        return carry

    lax.fori_loop(0, MROWS // CHUNK, memory_chunk, 0)
    lax.fori_loop(0, SEQ_LEN // CHUNK, token_chunk, 0)


def forward_kernel(tok_ref, mem_ref, row_ref, col_ref, o_ref, log_ref, bias_ref, s_ref, acc_ref):
    @pl.when(pl.program_id(0) == 0)
    def _():
        fill_bias(bias_ref, row_ref, col_ref)

    queries = tok_ref[:, :DH]

    def scores(key_ref, columns, offset):
        def step(c, top):
            rows = pl.ds(pl.multiple_of(c * CHUNK, CHUNK), CHUNK)
            target = pl.ds(pl.multiple_of(offset + c * CHUNK, CHUNK), CHUNK)
            s = nt(key_ref[rows, columns], queries) * SCALE2 + bias_ref[target, :]
            s_ref[target, :] = s
            return jnp.maximum(top, jnp.max(s.reshape(CHUNK // 8, 8, SEQ_LEN), axis=0))

        return step

    top = jnp.full((8, SEQ_LEN), -3.0e38, F32)
    top = lax.fori_loop(0, MROWS // CHUNK, scores(mem_ref, slice(0, DH), 0), top)
    top = lax.fori_loop(0, SEQ_LEN // CHUNK, scores(tok_ref, slice(DH, 2 * DH), MROWS), top)
    top = jnp.max(top, axis=0, keepdims=True)
    acc_ref[...] = jnp.zeros_like(acc_ref)

    def values(value_ref, columns, offset):
        def step(c, total):
            rows = pl.ds(pl.multiple_of(c * CHUNK, CHUNK), CHUNK)
            target = pl.ds(pl.multiple_of(offset + c * CHUNK, CHUNK), CHUNK)
            p = jnp.exp2(s_ref[target, :] - top)
            acc_ref[...] += nn(value_ref[rows, columns].T, p.astype(BF))
            return total + jnp.sum(p.reshape(CHUNK // 8, 8, SEQ_LEN), axis=0)

        return step

    total = jnp.zeros((8, SEQ_LEN), F32)
    total = lax.fori_loop(0, MROWS // CHUNK, values(mem_ref, slice(DH, 2 * DH), 0), total)
    total = lax.fori_loop(
        0, SEQ_LEN // CHUNK, values(tok_ref, slice(2 * DH, 3 * DH), MROWS), total
    )
    total = jnp.sum(total, axis=0, keepdims=True)
    o_ref[...] = (acc_ref[...] / total).T.astype(BF)
    log_ref[...] = (top + jnp.log2(total)).reshape(1, 1, SEQ_LEN)


def attention_forward(tok_p, mem_p, row_attr, col_attr):
    return pl.pallas_call(
        forward_kernel,
        out_shape=(shape((SEQ_LEN, HEADS * DH), BF), shape((HEADS, 1, SEQ_LEN), F32)),
        grid=(HEADS,),
        in_specs=[
            pl.BlockSpec((SEQ_LEN, 3 * DH), lambda h: (0, h)),
            pl.BlockSpec((KM, 2 * DH), lambda h: (0, h)),
            whole(row_attr.shape),
            whole(col_attr.shape),
        ],
        out_specs=[
            pl.BlockSpec((SEQ_LEN, DH), lambda h: (0, h)),
            pl.BlockSpec((1, 1, SEQ_LEN), lambda h: (h, 0, 0)),
        ],
        scratch_shapes=[
            pltpu.VMEM((MROWS + SEQ_LEN, SEQ_LEN), F32),
            pltpu.VMEM((MROWS + SEQ_LEN, SEQ_LEN), F32),
            pltpu.VMEM((DH, SEQ_LEN), F32),
        ],
        compiler_params=params(LIMIT),
        cost_estimate=cost(25_000_000_000),
        name="attention_forward",
    )(tok_p, mem_p, row_attr, col_attr)


def recon_kernel(tok_ref, mem_ref, *refs):
    gq_ref, gm_ref = refs[-2:]
    q = tok_ref[:, :DH]
    old, new = slice(CMEM, CMEM + OLD), slice(MROWS, KM)
    keys, values = slice(0, DH), slice(DH, 2 * DH)

    def softmax_rows(key_rows):
        s = nt(key_rows, q) * SCALE2
        p = jnp.exp2(s - jnp.max(s, axis=0, keepdims=True))
        return p / jnp.sum(p, axis=0, keepdims=True)

    ko, vo, kn, vn = mem_ref[old, keys], mem_ref[old, values], mem_ref[new, keys], mem_ref[new, values]
    po, pn = softmax_rows(ko), softmax_rows(kn)
    po_low, pn_low = po.astype(BF), pn.astype(BF)
    out_o, out_n = nn(vo.T, po_low), nn(vn.T, pn_low)
    gap = (out_o - out_n).astype(BF)
    gap32 = gap.astype(F32)
    do = (po * (nn(vo, gap) - jnp.sum(gap32 * out_o, axis=0, keepdims=True))).astype(BF)
    dn = (pn * (jnp.sum(gap32 * out_n, axis=0, keepdims=True) - nn(vn, gap))).astype(BF)
    gq_ref[...] = ((nn(ko.T, do) + nn(kn.T, dn)) * SCALE).reshape(1, DH, SEQ_LEN)
    gap_t = gap32.T.astype(BF)
    gm_ref[:OLD, keys] = nn(do, q) * SCALE
    gm_ref[:OLD, values] = nn(po_low, gap_t)
    gm_ref[OLD:MEM, :] = jnp.zeros((MEM - OLD, 2 * DH), F32)
    gm_ref[MEM:, keys] = nn(dn, q) * SCALE
    gm_ref[MEM:, values] = -nn(pn_low, gap_t)


def reconstruction(tok_p, mem_p, *earlier):
    return pl.pallas_call(
        recon_kernel,
        out_shape=(
            shape((HEADS, DH, SEQ_LEN), F32),
            shape((MEM + NEWC, HEADS * 2 * DH), F32),
        ),
        grid=(HEADS,),
        in_specs=[
            pl.BlockSpec((SEQ_LEN, 3 * DH), lambda h: (0, h)),
            pl.BlockSpec((KM, 2 * DH), lambda h: (0, h)),
        ]
        + [ANY] * len(earlier),
        out_specs=[
            pl.BlockSpec((1, DH, SEQ_LEN), lambda h: (h, 0, 0)),
            pl.BlockSpec((MEM + NEWC, 2 * DH), lambda h: (0, h)),
        ],
        compiler_params=params(LIMIT),
        cost_estimate=cost(10_000_000_000),
        name="reconstruction",
    )(tok_p, mem_p, *earlier)


def backward_kernel(
    tok_ref, mem_ref, own_ref, got_ref, o_ref, log_ref, rq_ref, rm_ref, row_ref, col_ref,
    *refs,
):
    gt_ref, gm_ref, bias_ref, acc_ref = refs[-4:]

    @pl.when(pl.program_id(0) == 0)
    def _():
        fill_bias(bias_ref, row_ref, col_ref)

    q = tok_ref[:, :DH]
    go = jnp.concatenate([own_ref[...], got_ref[...]], axis=0)
    product = go.astype(F32) * o_ref[...].astype(F32)
    delta = jnp.sum(product.T, axis=0, keepdims=True)
    log_total = log_ref[...].reshape(1, SEQ_LEN)
    acc_ref[...] = rq_ref[...].reshape(DH, SEQ_LEN)

    def piece(k, v, offset):
        s = nt(k, q) * SCALE2 + bias_ref[offset, :]
        p = jnp.exp2(s - log_total)
        d = (p * (nt(v, go) - delta)).astype(BF)
        acc_ref[...] += nn(k.T, d) * SCALE
        return nn(d, q) * SCALE, nn(p.astype(BF), go)

    def memory_chunk(c, carry):
        rows = pl.ds(pl.multiple_of(c * CHUNK, CHUNK), CHUNK)
        gk, gv = piece(mem_ref[rows, :DH], mem_ref[rows, DH:], rows)
        gm_ref[rows, :DH] = gk.astype(BF)
        gm_ref[rows, DH:] = gv.astype(BF)
        return carry

    def shared_chunk(c, carry):
        rows = pl.ds(pl.multiple_of(c * CHUNK, CHUNK), CHUNK)
        extra = pl.ds(pl.multiple_of(c * CHUNK - CMEM, CHUNK), CHUNK)
        gk, gv = piece(mem_ref[rows, :DH], mem_ref[rows, DH:], rows)
        gm_ref[rows, :DH] = (gk + rm_ref[extra, :DH]).astype(BF)
        gm_ref[rows, DH:] = (gv + rm_ref[extra, DH:]).astype(BF)
        return carry

    def token_chunk(c, carry):
        rows = pl.ds(pl.multiple_of(c * CHUNK, CHUNK), CHUNK)
        target = pl.ds(pl.multiple_of(MROWS + c * CHUNK, CHUNK), CHUNK)
        gk, gv = piece(tok_ref[rows, DH : 2 * DH], tok_ref[rows, 2 * DH :], target)
        gt_ref[rows, DH : 2 * DH] = gk.astype(BF)
        gt_ref[rows, 2 * DH :] = gv.astype(BF)
        return carry

    lax.fori_loop(0, CMEM // CHUNK, memory_chunk, 0)
    lax.fori_loop(CMEM // CHUNK, MROWS // CHUNK, shared_chunk, 0)
    lax.fori_loop(0, SEQ_LEN // CHUNK, token_chunk, 0)
    gm_ref[MROWS:, :] = rm_ref[MEM:, :].astype(BF)
    gt_ref[:, :DH] = acc_ref[...].T.astype(BF)


def attention_backward(
    tok_p, mem_p, go_own, go_got, o, logs, rec_q, rec_m, row_attr, col_attr, *earlier
):
    half = pl.BlockSpec((HALF, DH), lambda h: (0, h))
    return pl.pallas_call(
        backward_kernel,
        out_shape=(
            shape((SEQ_LEN, HEADS * 3 * DH), BF),
            shape((KM, HEADS * 2 * DH), BF),
        ),
        grid=(HEADS,),
        in_specs=[
            pl.BlockSpec((SEQ_LEN, 3 * DH), lambda h: (0, h)),
            pl.BlockSpec((KM, 2 * DH), lambda h: (0, h)),
            half,
            half,
            pl.BlockSpec((SEQ_LEN, DH), lambda h: (0, h)),
            pl.BlockSpec((1, 1, SEQ_LEN), lambda h: (h, 0, 0)),
            pl.BlockSpec((1, DH, SEQ_LEN), lambda h: (h, 0, 0)),
            pl.BlockSpec((MEM + NEWC, 2 * DH), lambda h: (0, h)),
            whole(row_attr.shape),
            whole(col_attr.shape),
        ]
        + [ANY] * len(earlier),
        out_specs=[
            pl.BlockSpec((SEQ_LEN, 3 * DH), lambda h: (0, h)),
            pl.BlockSpec((KM, 2 * DH), lambda h: (0, h)),
        ],
        scratch_shapes=[
            pltpu.VMEM((MROWS + SEQ_LEN, SEQ_LEN), F32),
            pltpu.VMEM((DH, SEQ_LEN), F32),
        ],
        compiler_params=params(LIMIT),
        cost_estimate=cost(35_000_000_000),
        name="attention_backward",
    )(tok_p, mem_p, go_own, go_got, o, logs, rec_q, rec_m, row_attr, col_attr, *earlier)


def center_rows(rows):
    centered = rows - jnp.mean(rows, axis=1, keepdims=True)
    factor = lax.rsqrt(jnp.mean(centered * centered, axis=1, keepdims=True) + EPSILON)
    return centered * factor, factor


def mid_kernel(raw_ref, own_ref, got_ref, w_ref, gain_ref, _, mid_ref, x2_ref):
    width = own_ref.shape[1]
    mid = raw_ref[...].astype(F32) + (
        nn(own_ref[...], w_ref[:width, :]) + nn(got_ref[...], w_ref[width:, :])
    )
    unit, _ = center_rows(mid)
    mid_ref[...] = mid
    x2_ref[...] = (unit * gain_ref[...]).astype(BF)


def residual_mid(raw, o, o_got, w_out, gain, earlier):
    block = 128
    rows = lambda width: pl.BlockSpec((block, width), lambda i: (i, 0))
    return pl.pallas_call(
        mid_kernel,
        out_shape=(shape((HALF, D), F32), shape((HALF, D), BF)),
        grid=(HALF // block,),
        in_specs=[rows(D), rows(HEADS * DH), rows(HEADS * DH), whole((D, D)), whole((1, D)), ANY],
        out_specs=[rows(D), rows(D)],
        compiler_params=params(LIMIT),
        cost_estimate=cost(4 * HALF * D * D),
        name="residual_mid",
    )(raw, o, o_got, w_out, gain, earlier)


TILE = 256


def ffn_kernel(*refs):
    x_own, x_got, c_own, c_got = refs[:4]
    plain, far_up, far_down = refs[4:7], refs[7], refs[8]
    out_keep, out_send, gx_keep, gx_send = refs[9:13]
    grads = refs[13:18]
    x_ref, xt_ref, c_ref, ct_ref, out_ref, gx_ref, up_ref, down_ref = refs[18:]
    step, last = pl.program_id(0), pl.num_programs(0) - 1
    block = step // (pl.num_programs(0) // 4)

    @pl.when(step == 0)
    def _():
        out_ref[...] = jnp.zeros_like(out_ref)
        gx_ref[...] = jnp.zeros_like(gx_ref)

        def turn(i, carry):
            rows = pl.ds(pl.multiple_of(i * 256, 256), 256)
            for halves, full, turned in (
                ((x_own, x_got), x_ref, xt_ref),
                ((c_own, c_got), c_ref, ct_ref),
            ):
                for j, half in enumerate(halves):
                    target = pl.ds(pl.multiple_of(j * HALF + i * 256, 256), 256)
                    full[target, :] = half[rows, :]
                    turned[:, target] = half[rows, :].T
            return carry

        lax.fori_loop(0, HALF // 256, turn, 0)

    for k, ref in enumerate(plain):
        @pl.when(block == k)
        def _():
            up_ref[...] = ref[0].reshape(D, TILE)
            down_ref[...] = ref[1].reshape(D, TILE)

    @pl.when(block == 3)
    def _():
        up_ref[...] = far_up[...].reshape(D, TILE)
        down_ref[...] = far_down[...].reshape(D, TILE)

    w_up, w_down = up_ref[...], down_ref[...]
    v = nn(x_ref[...], w_up)
    g_act = nn(c_ref[...], w_down)
    c0, c1 = 0.7978845608028654, 0.044715
    v2 = v * v
    t = jnp.tanh(c0 * v * (1.0 + c1 * v2))
    half = 0.5 * (1.0 + t)
    act = (v * half).astype(BF)
    slope = half + (0.5 * c0) * v * (1.0 - t * t) * (1.0 + (3.0 * c1) * v2)
    g_pre = (g_act * slope).astype(BF)
    out_ref[...] += nt(act, w_down)
    gx_ref[...] += nt(g_pre, w_up)
    grad_up = nn(xt_ref[...], g_pre).astype(BF)
    grad_down = nn(ct_ref[...], act).astype(BF)

    for k in range(3):
        @pl.when(block == k)
        def _():
            for j, row in enumerate((0, 2, 1, 3)):
                grads[k][0, j] = grad_up[block_of(row), :]
                grads[k][1, j] = grad_down[block_of(row), :]

    @pl.when(block == 3)
    def _():
        for j, row in enumerate((0, 2, 1, 3)):
            grads[3][j] = grad_up[block_of(row), :]
            grads[4][j] = grad_down[block_of(row), :]

    @pl.when(step == last)
    def _():
        for total, keep, send in ((out_ref, out_keep, out_send), (gx_ref, gx_keep, gx_send)):
            keep[...] = total[:HALF, :]
            send[...] = total[HALF:, :].astype(BF)


def feed_forward(x2, x2_got, cot, cot_got, plain, far_up, far_down):
    width = far_up.shape[-1]
    tiles = width // TILE

    def tile(k, step):
        return jnp.clip(step - k * tiles, 0, tiles - 1)

    def pair(k):
        return pl.BlockSpec((2, 4, QUARTER, TILE), lambda i: (0, 0, 0, tile(k, i)))

    far = pl.BlockSpec((4, QUARTER, TILE), lambda i: (0, 0, tile(3, i)))
    blocks = [pair(0), pair(1), pair(2), far, far]
    once = pl.BlockSpec((HALF, D), lambda i: (0, 0), pipeline_mode=pl.Buffered(1))
    rows = whole((HALF, D))
    full, turned = pltpu.VMEM((SEQ_LEN, D), BF), pltpu.VMEM((D, SEQ_LEN), BF)
    total = pltpu.VMEM((SEQ_LEN, D), F32)
    return pl.pallas_call(
        ffn_kernel,
        out_shape=(
            shape((HALF, D), F32), shape((HALF, D), BF),
            shape((HALF, D), F32), shape((HALF, D), BF),
        )
        + (shape(plain[0].shape, BF),) * 3
        + (shape(far_up.shape, BF),) * 2,
        grid=(4 * tiles,),
        in_specs=[once] * 4 + blocks,
        out_specs=[rows] * 4 + blocks,
        scratch_shapes=[full, turned, full, turned, total, total] + [pltpu.VMEM((D, TILE), BF)] * 2,
        compiler_params=params(LIMIT),
        cost_estimate=cost(12 * SEQ_LEN * D * 4 * width),
        name="feed_forward",
    )(x2, x2_got, cot, cot_got, *plain, far_up, far_down)


def out_sum_kernel(mid_ref, keep_ref, got_ref, *refs):
    total = mid_ref[...] + (keep_ref[...] + got_ref[...].astype(F32))
    for k, ref in enumerate(refs[-4:]):
        ref[...] = total[:, block_of(k)].astype(BF)


def out_sum(mid, keep, got, *earlier):
    block = 128
    rows = lambda width: pl.BlockSpec((block, width), lambda i: (i, 0))
    return pl.pallas_call(
        out_sum_kernel,
        out_shape=(shape((HALF, QUARTER), BF),) * 4,
        grid=(HALF // block,),
        in_specs=[rows(D)] * 3 + [ANY] * len(earlier),
        out_specs=[rows(QUARTER)] * 4,
        compiler_params=params(LIMIT),
        name="out_sum",
    )(mid, keep, got, *earlier)


def mid_back_kernel(gx_ref, got_ref, mid_ref, cot_ref, gain_ref, w_ref, gm_ref, ga_ref, keep_ref, send_ref, gn_ref):
    @pl.when(pl.program_id(0) == 0)
    def _():
        gn_ref[...] = jnp.zeros_like(gn_ref)

    unit, factor = center_rows(mid_ref[...])
    gx = gx_ref[...] + got_ref[...].astype(F32)
    gn_ref[...] += jnp.sum(gx * unit, axis=0, keepdims=True)
    s = gx * gain_ref[...]
    g_mid = cot_ref[...].astype(F32) + factor * (
        s - jnp.mean(s, axis=1, keepdims=True) - unit * jnp.mean(s * unit, axis=1, keepdims=True)
    )
    gm_ref[...] = g_mid
    low = g_mid.astype(BF)
    ga_ref[...] = low
    width = keep_ref.shape[1]
    send_ref[...] = nt(low, w_ref[width:, :]).astype(BF)
    keep_ref[...] = nt(low, w_ref[:width, :]).astype(BF)


def mid_back(gx, gx_got, mid, cot, gain, w_out):
    block = 128
    rows = lambda width: pl.BlockSpec((block, width), lambda i: (i, 0))
    half = shape((HALF, HEADS * DH), BF)
    return pl.pallas_call(
        mid_back_kernel,
        out_shape=(shape((HALF, D), F32), shape((HALF, D), BF), half, half, shape((1, D), F32)),
        grid=(HALF // block,),
        in_specs=[rows(D)] * 4 + [whole((1, D)), whole((D, D))],
        out_specs=[rows(D), rows(D), rows(HEADS * DH), rows(HEADS * DH), whole((1, D))],
        compiler_params=params(LIMIT),
        cost_estimate=cost(2 * HALF * D * D),
        name="mid_back",
    )(gx, gx_got, mid, cot, gain, w_out)


def tok_grad_kernel(g_ref, w_ref, raw_ref, *refs):
    keep_ref, send_ref, gn_ref = refs[-3:]
    step = pl.program_id(0)

    @pl.when(step == 0)
    def _():
        gn_ref[...] = jnp.zeros_like(gn_ref)

    gx = nn(g_ref[...], w_ref[...])
    unit, _ = center_rows(raw_ref[...].astype(F32))
    gn_ref[...] += jnp.sum(gx * unit, axis=0, keepdims=True)

    @pl.when(step < pl.num_programs(0) // 2)
    def _():
        send_ref[...] = gx.astype(BF)

    @pl.when(step >= pl.num_programs(0) // 2)
    def _():
        keep_ref[...] = gx


def tok_grad(g_tok, w_tok, raw, *earlier):
    block = 128
    steps, half = SEQ_LEN // block, HALF // block
    rows = lambda width: pl.BlockSpec((block, width), lambda i: ((i + half) % steps, 0))
    return pl.pallas_call(
        tok_grad_kernel,
        out_shape=(shape((HALF, D), F32), shape((HALF, D), BF), shape((1, D), F32)),
        grid=(steps,),
        in_specs=[rows(HEADS * 3 * DH), whole((HEADS * 3 * DH, D)), rows(D)]
        + [ANY] * len(earlier),
        out_specs=[
            pl.BlockSpec((block, D), lambda i: (jnp.maximum(i - half, 0), 0)),
            pl.BlockSpec((block, D), lambda i: (jnp.minimum(i, half - 1), 0)),
            whole((1, D)),
        ],
        compiler_params=params(LIMIT),
        name="tok_grad",
    )(g_tok, w_tok, raw, *earlier)


def input_grad_kernel(keep_ref, got_ref, raw_ref, gm_ref, gain_ref, *refs):
    unit, factor = center_rows(raw_ref[...].astype(F32))
    got = [got_ref[:, block_of(k ^ 1)].astype(F32) for k in range(4)]
    s = (keep_ref[...] + jnp.concatenate(got, axis=1)) * gain_ref[...]
    g = gm_ref[...] + factor * (
        s - jnp.mean(s, axis=1, keepdims=True) - unit * jnp.mean(s * unit, axis=1, keepdims=True)
    )
    for k, ref in enumerate(refs[-4:]):
        ref[...] = g[:, block_of(k)].astype(BF)


def input_grad(keep, got, raw, g_mid, gain, *earlier):
    block = 128
    rows = pl.BlockSpec((block, D), lambda i: (i, 0))
    return pl.pallas_call(
        input_grad_kernel,
        out_shape=(shape((HALF, QUARTER), BF),) * 4,
        grid=(HALF // block,),
        in_specs=[rows, rows, rows, rows, whole((1, D))] + [ANY] * len(earlier),
        out_specs=[pl.BlockSpec((block, QUARTER), lambda i: (i, 0))] * 4,
        compiler_params=params(LIMIT),
        cost_estimate=cost(20_000_000_000),
        name="input_grad",
    )(keep, got, raw, g_mid, gain, *earlier)


def mem_grad_kernel(g_ref, w_ref, raw_ref, gain_ref, conv_ref, *refs):
    gn_ref, gc_ref, unit_ref = refs[-3:]
    def rows_sum(block, total):
        rows = pl.ds(pl.multiple_of(block * 256, 256), 256)
        unit, _ = center_rows(raw_ref[rows, :].astype(F32))
        for j in range(D // DH):
            unit_ref[j, rows, :] = unit[:, j * DH : j * DH + DH]
        return total + jnp.sum(nn(g_ref[rows, :], w_ref[...]) * unit, axis=0, keepdims=True)

    gn_ref[...] = lax.fori_loop(0, MROWS // 256, rows_sum, jnp.zeros((1, D), F32))
    packed = nn(g_ref[MROWS:, :], w_ref[...])
    for j in range(D // DH):
        lanes = slice(j * DH, j * DH + DH)
        for t in range(RATE):
            picked = unit_ref[j, pl.ds(CMEM + t, NEWC, stride=RATE), :]
            term = jnp.sum(packed[:, lanes] * picked, axis=0, keepdims=True)
            gc_ref[t : t + 1, lanes] = term * gain_ref[:, lanes]
            gn_ref[:, lanes] += conv_ref[t : t + 1, lanes] * term


def mem_grad(g_mem, w_mem, raw, gain, conv, *earlier):
    return pl.pallas_call(
        mem_grad_kernel,
        out_shape=(shape((1, D), F32), shape((RATE, D), F32)),
        grid=(1,),
        in_specs=[
            whole((KM, D)), whole((D, D)), whole((MROWS, D)), whole((1, D)), whole((RATE, D)),
        ]
        + [ANY] * len(earlier),
        out_specs=[whole((1, D)), whole((RATE, D))],
        scratch_shapes=[pltpu.VMEM((D // DH, MROWS, DH), F32)],
        compiler_params=params(LIMIT),
        name="mem_grad",
    )(g_mem, w_mem, raw, gain, conv, *earlier)


def store_spans(grad, index, keep_ref, send_ref):
    span = DH // 4
    for x in range(2):
        for core, ref in enumerate((keep_ref, send_ref)):
            row = (2 * x + core) * span
            ref[(x,) + index] = grad[row : row + span, :].astype(BF)


def qkv_grad_kernel(gt_ref, xt_ref, gm_ref, xm_ref, *refs):
    for kind in range(3):
        grad = nn(gt_ref[:, kind * DH : (kind + 1) * DH].T, xt_ref[...])
        if kind > 0:
            grad = grad + nn(gm_ref[:, (kind - 1) * DH : kind * DH].T, xm_ref[...])
        store_spans(grad, (0, kind), *refs[-2:])


def qkv_grad(g_tok, x_tok, g_mem, x_mem, *earlier):
    out = shape((2, HEADS, 3, DH // 4, D), BF)
    block = pl.BlockSpec((2, 1, 3, DH // 4, D), lambda h: (0, h, 0, 0, 0))
    return pl.pallas_call(
        qkv_grad_kernel,
        out_shape=(out, out),
        grid=(HEADS,),
        in_specs=[
            pl.BlockSpec((SEQ_LEN, 3 * DH), lambda h: (0, h)),
            whole((SEQ_LEN, D)),
            pl.BlockSpec((KM, 2 * DH), lambda h: (0, h)),
            whole((KM, D)),
        ]
        + [ANY] * len(earlier),
        out_specs=[block, block],
        compiler_params=params(LIMIT),
        name="qkv_grad",
    )(g_tok, x_tok, g_mem, x_mem, *earlier)


def out_grad_kernel(own_ref, got_ref, g_ref, keep_ref, send_ref):
    for z, ref in enumerate((own_ref, got_ref)):
        store_spans(nn(ref[...].T, g_ref[...]), (0, z), keep_ref, send_ref)


def out_grad(o, o_got, g_attn):
    out = shape((2, HEADS, 2, DH // 4, D), BF)
    block = pl.BlockSpec((2, 1, 2, DH // 4, D), lambda h: (0, h, 0, 0, 0))
    half = pl.BlockSpec((HALF, DH), lambda h: (0, h))
    return pl.pallas_call(
        out_grad_kernel,
        out_shape=(out, out),
        grid=(HEADS,),
        in_specs=[half, half, whole((HALF, D))],
        out_specs=[block, block],
        compiler_params=params(LIMIT),
        name="out_grad",
    )(o, o_got, g_attn)


def merge_kernel(count, lanes, *refs):
    outs = refs[-2:]
    for j, out in enumerate(outs):
        if lanes:
            half = slice(j * out.shape[-1], (j + 1) * out.shape[-1])
            parts = [ref[:, half] for ref in refs[:count]]
        else:
            parts = [ref[...] for ref in refs[j * count : (j + 1) * count]]
        out[...] = sum(part.astype(F32) for part in parts).astype(BF)


def merge(arrays, *earlier, lanes=False, axis=0, work=0):
    dims = arrays[0].shape
    count = len(arrays)
    if lanes:
        out = dims[:-1] + (dims[-1] // 2,)
        flat = [a.reshape(-1, dims[-1]) for a in arrays]
        rows = flat[0].shape[0]
        grid, out_dims = (1,), (rows, out[-1])
        ins, blocks = [whole(flat[0].shape)] * count, [whole(out_dims)] * 2
    else:
        out = dims[:axis] + (dims[axis] // 2,) + dims[axis + 1 :]
        outer = dims[0] if axis else 1
        flat = [a.reshape(2 * outer, -1, dims[-1]) for a in arrays]
        block = (1,) + flat[0].shape[1:]
        grid, out_dims = (outer,), (outer,) + block[1:]
        low = pl.BlockSpec(block, lambda i: (2 * i, 0, 0))
        high = pl.BlockSpec(block, lambda i: (2 * i + 1, 0, 0))
        same = pl.BlockSpec(block, lambda i: (i, 0, 0))
        ins, blocks, flat = [low] * count + [high] * count, [same] * 2, flat * 2
    pair = pl.pallas_call(
        functools.partial(merge_kernel, count, lanes),
        out_shape=(shape(out_dims, BF),) * 2,
        grid=grid,
        in_specs=ins + [ANY] * len(earlier),
        out_specs=blocks,
        compiler_params=params(LIMIT),
        cost_estimate=cost(work) if work else None,
        name="merge",
    )(*flat, *earlier)
    return [g.reshape(out) for g in pair]


def pick(g, index, axis=0):
    return lax.dynamic_index_in_dim(g, index, axis, keepdims=False)


def after(value, *earlier):
    return pl.pallas_call(
        lambda *refs: None,
        out_shape=shape(value.shape, value.dtype),
        in_specs=[ANY] * (1 + len(earlier)),
        out_specs=ANY,
        input_output_aliases={0: 0},
        name="after",
    )(value, *earlier)


def doubled(g, axis, distance):
    return jnp.concatenate([g, swap(g, axis, distance)], axis=0)


def both(parts, axis, distance):
    return parts + [swap(p, axis, distance) for p in parts]


def doubled_cols(g, n_col, first=1):
    while first < n_col:
        g = doubled(g, "col", first)
        first *= 2
    return g


def halve_col(g, last=1):
    while g.shape[0] > 1:
        n = g.shape[0] // 2
        g = add_low(g[:n], swap(g[n:], "col", n * last))
    return g[0]


def halve_row(g):
    g = add_low(g[:2], swap(g[2:], "row", 2))
    return g[0].astype(F32) + swap(g[1], "row", 1).astype(F32)


def per_device(
    hidden, memory, compressed, seg_ids, positions, keep_mask, mem_seg, cotangent,
    w_qkv, w_out, w_up, w_down, norm_attn, norm_ffn, conv_w,
):
    n_col = lax.axis_size("col")
    heads_part = w_qkv.shape[2]
    part = max(heads_part // 2, 1)
    row, col = lax.axis_index("row"), lax.axis_index("col")
    z_high, z_low = row // 2, row % 2
    low_first = z_low == 0
    where = z_low.reshape(1).astype(jnp.int32)
    span = DH // 4

    def by_low(pair):
        return jnp.where(low_first, pair, jnp.flip(pair, axis=0))

    tokens = hidden.reshape(2, SEQ_LEN, QUARTER)
    tok_mine, tok_other = pick(tokens, z_high), pick(tokens, 1 - z_high)
    tok_far, tok_near = swap(tok_other, "row", 2), swap(tok_mine, "row", 1)
    tok_pieces = [tok_mine, tok_near, tok_far, swap(tok_far, "row", 1)]

    qkv = w_qkv.astype(BF).transpose(2, 1, 3, 0)
    outs = w_out.astype(BF)
    if heads_part % 2 == 0:
        qkv = by_low(qkv.reshape(2, part, 3, span, QUARTER))
        outs = by_low(outs.reshape(2, part, 1, span, QUARTER))
        near = jnp.concatenate([qkv[0], outs[0], outs[1]], axis=1)
        far = jnp.concatenate([qkv[1], outs[1], outs[0]], axis=1)
        heads = jnp.stack(
            [near, swap(far, "row", 1), swap(near, "row", 2), swap(far, "row", 3)]
        )
        heads = doubled_cols(after(heads[None], tok_near), n_col)
    else:
        qkv = jnp.stack([qkv] + [swap(qkv, "row", k) for k in (1, 2, 3)])
        outs = jnp.stack([outs] + [swap(outs, "row", k) for k in (1, 2, 3)])
        qkv = doubled_cols(jnp.where(low_first, qkv, swap(qkv, "col", 1))[None], n_col, 2)
        outs = doubled_cols(outs[None], n_col, 2)
        outs = by_low(jnp.stack([outs, swap(outs, "col", 1)]))
        heads = jnp.concatenate([qkv, jnp.moveaxis(outs, 0, 3)], axis=3)
    own = after(jnp.stack([w_up.astype(BF), w_down.astype(BF).T]), tok_far, tok_near)
    w_far = swap(own, "row", 2)
    heads = both([after(heads, w_far, tok_pieces[3])], "dp", 2)
    own = after(own, w_far, tok_pieces[3])
    w_near = swap(own, "row", 1)
    w_both = swap(w_far, "row", 1)
    small = jnp.concatenate(
        [norm_attn, norm_ffn, conv_w.reshape(-1)]
        + [a.astype(F32) for a in (seg_ids, positions, keep_mask, mem_seg)]
    )
    small = after(small, tok_near)
    shared = jnp.stack([small, swap(small, "row", 2)])
    shared = jnp.stack([shared, swap(shared, "row", 1)], axis=1).reshape(4, -1)
    gains = shared[:, : 5 * QUARTER].reshape(4, 5, QUARTER).transpose(1, 0, 2).reshape(5, D)
    gain1, gain2, conv = gains[0:1], gains[1:2], gains[2:5]
    spans = seg_ids.shape[0] // SEQ_LEN
    sequence = 2 * col + z_high
    ids = pick(shared, row ^ (sequence // spans))[5 * QUARTER :]
    ids = pick(ids.reshape(4, spans, SEQ_LEN), sequence % spans, 1)
    rolled = jnp.concatenate([ids[:3, HALF:], ids[:3, :HALF]], axis=1)
    seg, pos, keep = jnp.where(low_first, ids[:3], rolled)
    row_attr = jnp.stack([seg, pos])
    col_attr = jnp.stack([jnp.where(keep == 1, seg, -2.0), pos, ids[3]], axis=1)

    memories = jnp.concatenate(
        [compressed.reshape(2, CMEM, QUARTER), memory.reshape(2, MEM, QUARTER)], axis=1
    )
    mem_other = after(pick(memories, 1 - z_high), w_far, tok_pieces[3])
    mem_far = swap(mem_other, "row", 2)
    heads = both([after(h, mem_far, w_near, w_both) for h in heads], "dp", 1)
    w_tok, w_mem, w_back = join_weights([heads[0], heads[2], heads[1], heads[3]])
    own = jnp.stack([own, after(w_near, mem_far, heads[2], heads[3]), w_far, w_both], axis=1)
    half_col = n_col // 2
    distance = 1
    while distance < half_col:
        own = jnp.concatenate([own, swap(own, "col", distance)], axis=3)
        distance *= 2
    own_y, own_x = swap(own, "col", half_col), swap(own, "dp", 2)
    far_up, far_down = swap(own_x[0], "col", half_col), swap(own_y[1], "dp", 2)

    mem_mine = after(pick(memories, z_high), mem_far, w_near)
    mem_near = swap(mem_mine, "row", 1)
    mem_pieces = [mem_mine, mem_near, mem_far, swap(mem_far, "row", 1)]

    x_tok, raw_tok = tok_norm(where, tok_pieces, after(gain1, heads[2]))
    tok_p = nt(x_tok, w_tok).astype(BF)
    x_mem, raw_mem = mem_norm(mem_pieces, gain1, conv, tok_p)
    mem_p = nt(x_mem, w_mem).astype(BF)
    cots = cotangent.reshape(4, HALF, QUARTER)
    cots = [after(pick(cots, row ^ k), mem_p, tok_p) for k in range(4)]
    cot = jnp.concatenate([cots[0]] + [swap(cots[k], "row", k) for k in (1, 2, 3)], axis=1)
    cot_got = swap(cot, "dp", 1)
    o, logs = attention_forward(tok_p, mem_p, row_attr, col_attr)
    o_got = swap(o[HALF:], "row", 1)
    rec_q, rec_m = reconstruction(tok_p, mem_p, cot, own_x, own_y)
    mid, x2 = residual_mid(raw_tok, o, o_got, w_back, gain2, rec_m)

    x2_got = swap(x2, "dp", 1)
    out_keep, out_send, gx_keep, gx_send, *grads = feed_forward(
        x2, x2_got, cot, cot_got, (own, own_y, own_x), far_up, far_down
    )
    gx_got = swap(gx_send, "dp", 1)
    g_mid, g_attn, go_keep, go_send, gain2_sum = mid_back(
        gx_keep, gx_got, mid, cot, gain2, w_back
    )
    go_got = swap(go_send, "row", 1)

    own, own_y, own_x, far_up, far_down = grads
    far_up = after(swap(far_up, "col", half_col), go_got)
    far_down = after(swap(far_down, "dp", 2), go_got)
    sum_x = own_x.at[0].set(add_low(own_x[0], far_up))
    sum_y = own_y.at[1].set(add_low(own_y[1], far_down))
    got_x, got_y = swap(sum_x, "dp", 2), swap(sum_y, "col", half_col)

    def to_owners(blocks):
        return [blocks[0]] + [swap(blocks[k], "row", k) for k in (1, 2, 3)]

    def in_order(blocks):
        blocks = [jnp.where(low_first, blocks[k], blocks[k ^ 1]) for k in range(4)]
        blocks = [jnp.where(z_high == 0, blocks[k], blocks[k ^ 2]) for k in range(4)]
        return jnp.concatenate(blocks, axis=0)

    out_got = swap(out_send, "dp", 1)
    g_out = out_grad(o, o_got, g_attn)
    outs = out_sum(mid, out_keep, out_got, g_out[1])
    outs = to_owners([outs[0]] + [after(piece, go_got) for piece in outs[1:]])

    g_tok, g_mem = attention_backward(
        tok_p, mem_p, go_keep, go_got, o, logs, rec_q, rec_m, row_attr, col_attr,
        sum_x, sum_y, outs[0],
    )
    gx, gx_send, gain1_tok = tok_grad(g_tok, w_tok, raw_tok, *outs[1:])
    gx_got = swap(gx_send, "row", 1)
    distance = half_col
    if distance > 1:
        total = (own.astype(F32) + got_x.astype(F32) + got_y.astype(F32)).astype(BF)
        while distance > 1:
            distance //= 2
            n = total.shape[3] // 2
            total = add_low(total[..., :n], swap(total[..., n:], "col", distance))
        even, odd = total[:, :2], total[:, 2:]
    else:
        even, odd = merge([own, got_x, got_y], gx_send, axis=1)

    def halves(g):
        return g.reshape((n_col, part) + g.shape[1:])

    g_qkv = qkv_grad(g_tok, x_tok, g_mem, x_mem, odd)
    g_out, out_send = merge([g_out[0], swap(g_out[1], "dp", 1)], g_qkv[1])
    out_got = swap(out_send, "dp", 2)
    gain1_mem, conv_sum = mem_grad(g_mem, w_mem, raw_mem, gain1, conv, out_send)
    d_rows = input_grad(gx, gx_got, raw_tok, g_mid, gain1, gain1_mem)
    d_input = to_owners(d_rows)
    if heads_part % 2 == 0:
        g_out, out_send = merge([halves(g_out[0]), halves(out_got[0])], d_rows[0])
    g_qkv, qkv_send = merge([g_qkv[0], swap(g_qkv[1], "dp", 1)], out_send)
    qkv_got = swap(qkv_send, "dp", 2)
    even, even_send = merge([even, swap(odd, "row", 1)], qkv_send, axis=1)
    even_got = swap(even_send[:, 0], "row", 2)
    if heads_part % 2 == 0:
        def over_row(g, got, first, second):
            g, send = merge([g, got], first, lanes=True)
            g, last = merge([g, swap(send, "row", 2)], second, lanes=True)
            return g, swap(last, "row", 1), send

        g_qkv, qkv_send = merge(
            [halves(g_qkv[0]), halves(qkv_got[0])], even_send, *d_input[1:]
        )
        out_pair = over_row(g_out[0], swap(out_send[0], "col", 1), qkv_send, qkv_send)
        g_qkv, got, last = over_row(
            g_qkv[0], swap(qkv_send[0], "col", 1), out_pair[2], out_pair[2]
        )
        grad_qkv = by_low(jnp.stack([g_qkv, got])).astype(F32)
        grad_qkv = grad_qkv.reshape(heads_part, 3, span, QUARTER)
        g_out, got, _ = out_pair
        g_out, got = jnp.swapaxes(g_out, 0, 1), jnp.swapaxes(got, 0, 1)
        grad_out = by_low(g_out.astype(F32) + jnp.flip(got, axis=0).astype(F32))
        grad_out = grad_out.reshape(heads_part, span, QUARTER)
    else:
        g_out, g_qkv = add_low(g_out[0], out_got[0]), add_low(g_qkv[0], qkv_got[0])
        g_qkv = halve_col(g_qkv, 2)
        qkv_send = g_qkv
        grad_qkv, grad_out = reduce_heads(g_qkv, g_out, by_low, low_first)
        last = d_rows[0]
    vectors = jnp.concatenate([gain1_tok + gain1_mem, gain2_sum, conv_sum], axis=0)
    vectors = after(vectors, qkv_send)
    vectors = vectors.reshape(5, 4, QUARTER).transpose(1, 0, 2)
    for distance in (1, 2):
        vectors = vectors + swap(vectors, "dp", distance)
    distance = 1
    while distance < n_col:
        vectors = vectors + swap(vectors, "col", distance)
        distance *= 2
    vectors = after(vectors, g_qkv, even_got)
    vectors = vectors[:2] + swap(vectors[2:], "row", 2)
    vectors = vectors[0] + swap(vectors[1], "row", 1)
    grad_qkv = grad_qkv.transpose(3, 1, 0, 2)
    grads = even[:, 0].astype(F32) + even_got.astype(F32)
    d_input, out = in_order(d_input), in_order(outs)
    return (
        out, d_input, grad_qkv, grad_out, grads[0], grads[1].T, vectors[0], vectors[1], vectors[2:]
    )


def reduce_heads(g_qkv, g_out, by_low, low_first):
    span = DH // 4
    zeros = jnp.zeros_like(g_qkv)
    g_qkv = add_low(
        jnp.where(low_first, g_qkv, zeros), swap(jnp.where(low_first, zeros, g_qkv), "col", 1)
    )
    g_out = by_low(jnp.swapaxes(g_out, 0, 1))
    g_out = halve_col(add_low(g_out[0], swap(g_out[1], "col", 1)), 2)
    g_qkv = halve_row(jnp.moveaxis(g_qkv.reshape(3, span, 4, QUARTER), 2, 0))[None]
    g_out = halve_row(jnp.moveaxis(g_out.reshape(span, 4, QUARTER), 1, 0))[None]
    return g_qkv, g_out


def solution(mesh):
    tokens, features = ("dp", "col"), "row"
    placed = (
        P(tokens, features),
        P(tokens, features),
        P(tokens, features),
        P(("dp", "row")),
        P(("dp", "row")),
        P(("dp", "row")),
        P(("dp", "row")),
        P(tokens, features),
        P("row", None, "col", "dp"),
        P("col", "dp", "row"),
        P("row", tokens),
        P(tokens, "row"),
        P("row"),
        P("row"),
        P(None, "row"),
    )
    return jax.shard_map(
        per_device,
        mesh=mesh,
        in_specs=placed,
        out_specs=(
            P(tokens, features),
            P(tokens, features),
            P("row", None, "col", "dp"),
            P("col", "dp", "row"),
            P("row", tokens),
            P(tokens, "row"),
            P("row"),
            P("row"),
            P(None, "row"),
        ),
        check_vma=False,
    )
```
